32 devices in a mesh: dp: 8 (over z, x), tm: 4 (over y, core).
Axes of the slice: x: 2, y: 2, z: 4, core: 2. Of those that a mesh axis runs over, the one named last changes fastest.
Arguments:
- clips: bfloat16 [8, 32, 16, 16, 256], P('dp', 'tm'), may hold values from -6 to 6
- frame_counts: int32 [8], P('dp'), may hold values from 5 to 32, as said below
- weight: bfloat16 [6912, 256], P('dp'), may hold values from -0.078125 to 0.078125
- gain: float32 [256], replicated, may hold values from 0.1 to 1.9
- bias: float32 [256], replicated, may hold values from -3 to 3
- cotangent: bfloat16 [8, 16, 8, 8, 256], P('dp', 'tm'), may hold values from -6 to 6
Outputs:
- output: bfloat16 [8, 16, 8, 8, 256], P('dp', 'tm')
- input_grad: bfloat16 [8, 32, 16, 16, 256], P('dp', 'tm')
- weight_grad: float32 [6912, 256], P('dp')
The draws below stay inside these ranges and needn't reach their ends.
Inputs may be any that keep to these rules, and one draw needn't show every extreme that they name: frame_counts[c] frames of clip c are valid, the remaining slots are padding; in every draw some clip uses all 32 slots.
All inputs are finite; a program needn't handle non-finite values.
Results may differ from the reference program's by a relative error of at most 0.0048.
Values may be sent and summed in bfloat16 or wider, within the bound.
A program may use at most 64 MiB of HBM per device.

```python
import jax
import jax.numpy as jnp
from jax import lax

CHANNELS = 256
GROUPS = 32
ROWS = 16
COLS = 16
CLIPS = 8
FRAMES = 32


def draw_frame_counts(key, part):
    first_key = jax.random.fold_in(key, 11)
    second_key = jax.random.fold_in(key, 12)
    counts = jax.random.randint(first_key, (CLIPS,), FRAMES // 8 + 1, FRAMES + 1)
    position = jax.random.randint(second_key, (), 0, CLIPS)
    return jnp.where(jnp.arange(CLIPS) == position, FRAMES, counts).astype(jnp.int32)


def steps_of(rng, dims, shards, smallest, top_value):
    factor_of, own = 1.0, jax.random.fold_in(rng, 6)
    for axis_at, parts in shards:
        heights = jnp.exp(jax.random.uniform(jax.random.fold_in(own, axis_at), (parts,), jnp.float32, smallest / len(shards), top_value / len(shards)))
        factor_of = factor_of * jnp.repeat(heights, dims[axis_at] // parts).reshape([-1 if axis == axis_at else 1 for axis in range(len(dims))])
    return factor_of


def centred(rng, shape, spread, bound, cuts=(), dtype=jnp.bfloat16):
    array = jax.random.normal(rng, shape, jnp.float32) * spread
    if len(cuts) > 0:
        array = steps_of(rng, shape, cuts, -0.22, 0.18) * array
    return jnp.clip(array, min=-bound, max=bound).astype(dtype)


def setup_inputs(seed: int = 0) -> dict:
    seeds = jax.random.split(jax.random.key(seed), 7)
    clips = centred(seeds[0], (CLIPS, FRAMES, ROWS, COLS, CHANNELS), 1.0, 6.0, ((0, 8), (1, 4)))
    frame_counts = draw_frame_counts(jax.random.fold_in(seeds[6], 71), 0)
    weight = centred(seeds[2], (27 * CHANNELS, CHANNELS), (27 * CHANNELS) ** -0.5, 0.078125, ((0, 8),))
    gain = jnp.clip(1.0 + 0.18 * jax.random.normal(seeds[3], (CHANNELS,), jnp.float32), 0.1, 1.9)
    bias = centred(seeds[4], (CHANNELS,), 0.5, 3.0, (), jnp.float32)
    cotangent = centred(seeds[5], (CLIPS, FRAMES // 2, ROWS // 2, COLS // 2, CHANNELS), 1.0, 6.0, ((0, 8), (1, 4)))
    return dict(clips=clips, frame_counts=frame_counts, weight=weight, gain=gain, bias=bias, cotangent=cotangent)


EPS = 1e-06

def unfold(padded, frames_out, rows_out, cols_out):
    tap_list = []
    for step_t in range(3):
        for step_r in range(3):
            for step_c in range(3):
                tap_piece = padded[step_t:step_t + 2 * frames_out:2, step_r:step_r + 2 * rows_out:2, step_c:step_c + 2 * cols_out:2, :]
                tap_list.append(tap_piece.reshape(frames_out * rows_out * cols_out, -1))
    return jnp.concatenate(tap_list, axis=1)

def spread_taps(values, data_axis, tap_axis, length):
    moved = jnp.moveaxis(values, tap_axis, 0)
    count = moved.shape[data_axis + 1]
    width_list = [(0, 0)] * (moved.ndim - 1)
    after = list(width_list)
    after[data_axis] = (0, 1)
    before = list(width_list)
    before[data_axis] = (1, 0)
    even_part = jnp.pad(moved[0], after) + jnp.pad(moved[2], before)
    odd_part = jnp.pad(moved[1], after)
    joined = jnp.stack([even_part, odd_part], axis=data_axis + 1)
    shape_new = list(even_part.shape)
    shape_new[data_axis] = 2 * (count + 1)
    joined = joined.reshape(shape_new)
    return lax.slice_in_dim(joined, 0, length, axis=data_axis)

def fold_back(columns, padded_shape, frames_out, rows_out, cols_out):
    channels = padded_shape[3]
    blocks = columns.reshape(frames_out, rows_out, cols_out, 3, 3, 3, channels)
    blocks = spread_taps(blocks, 0, 3, padded_shape[0])
    blocks = spread_taps(blocks, 1, 3, padded_shape[1])
    blocks = spread_taps(blocks, 2, 3, padded_shape[2])
    return blocks

def silu_slope(preact):
    sig = jax.nn.sigmoid(preact)
    return sig * (1.0 + preact * (1.0 - sig))

def reference(clips, frame_counts, weight, gain, bias, cotangent):

    def clip_pass(running, scanned):
        clip_data, frames_valid, cot_block = scanned
        frame_count, row_count, col_count, channels = clip_data.shape
        width_g = channels // GROUPS
        frame_mask = (jnp.arange(frame_count) < frames_valid).astype(jnp.float32)[:, None, None, None]
        mask_group = frame_mask[..., None]
        entries = frames_valid.astype(jnp.float32) * (row_count * col_count * width_g)
        values = clip_data.astype(jnp.float32).reshape(frame_count, row_count, col_count, GROUPS, width_g)
        sum_first = lax.optimization_barrier(jnp.sum(values * mask_group, axis=(0, 1, 2, 4)))
        sum_second = lax.optimization_barrier(jnp.sum(values * values * mask_group, axis=(0, 1, 2, 4)))
        group_mean = sum_first / entries
        variance = sum_second / entries - group_mean * group_mean
        inv_std = lax.rsqrt(variance + EPS)
        normed_g = (values - group_mean[:, None]) * inv_std[:, None]
        normed = normed_g.reshape(frame_count, row_count, col_count, channels)
        preact = normed * gain + bias
        hidden = (jax.nn.silu(preact) * frame_mask).astype(jnp.bfloat16)
        padded = jnp.pad(hidden, ((2, 0), (1, 0), (1, 0), (0, 0)))
        frames_out, rows_out, cols_out = (frame_count // 2, row_count // 2, col_count // 2)
        patches = unfold(padded, frames_out, rows_out, cols_out)
        out_block = jnp.dot(patches, weight, preferred_element_type=jnp.float32).astype(jnp.bfloat16)
        out_block = out_block.reshape(frames_out, rows_out, cols_out, channels)
        cot_rows = cot_block.reshape(-1, channels)
        weight_grad = running + lax.dot_general(patches, cot_rows, (((0,), (0,)), ((), ())), preferred_element_type=jnp.float32)
        dcols = lax.dot_general(cot_rows, weight, (((1,), (1,)), ((), ())), preferred_element_type=jnp.float32)
        dpad = fold_back(dcols, padded.shape, frames_out, rows_out, cols_out)
        dhidden = dpad[2:, 1:, 1:, :]
        dnormed = dhidden * frame_mask * silu_slope(preact) * gain
        grad_norm = dnormed.reshape(frame_count, row_count, col_count, GROUPS, width_g)
        back_first = lax.optimization_barrier(jnp.sum(grad_norm, axis=(0, 1, 2, 4)))
        back_second = lax.optimization_barrier(jnp.sum(grad_norm * normed_g, axis=(0, 1, 2, 4)))
        input_grad = mask_group * inv_std[:, None] * (grad_norm - back_first[:, None] / entries - normed_g * back_second[:, None] / entries)
        input_grad = input_grad.reshape(frame_count, row_count, col_count, channels).astype(jnp.bfloat16)
        return (weight_grad, (out_block, input_grad))
    start_grad = jnp.zeros(weight.shape, jnp.float32)
    weight_grad, (output, input_grad) = lax.scan(clip_pass, start_grad, (clips, frame_counts, cotangent))
    return (output, input_grad, weight_grad)
```

```python
import functools

import jax
import jax.numpy as jnp
from jax import lax
from jax.experimental import pallas as pl
from jax.experimental.pallas import tpu as pltpu
from jax.sharding import PartitionSpec as P

GROUPS = 32
EPS = 1e-06
PARTS = 3
MESH = pl.DeviceIdType.MESH
VMEM = pl.BlockSpec(memory_space=pltpu.VMEM)
SMEM = pl.BlockSpec(memory_space=pltpu.SMEM)


def plan(dp_size, tm_size):
    dp_bits = [("dp", k) for k in range(dp_size.bit_length() - 1)]
    tm_bits = [("tm", k) for k in range(tm_size.bit_length() - 1)]
    cut = len(dp_bits) // 2
    ways = [tm_bits[1:], dp_bits[:cut], dp_bits[cut:]]
    orders = []
    for part in range(PARTS):
        turned = ways[part:] + ways[:part]
        orders.append(tm_bits[:1] + turned[0] + turned[1] + turned[2])
    return dp_bits[::-1] + tm_bits[::-1], orders


def lane_group_sum(value, width):
    channels = value.shape[-1]
    lane = lax.broadcasted_iota(jnp.int32, value.shape, value.ndim - 1)
    step = 1
    while step < width:
        above = pltpu.roll(value, channels - step, value.ndim - 1)
        below = pltpu.roll(value, step, value.ndim - 1)
        value = value + jnp.where((lane // step) % 2 == 0, above, below)
        step *= 2
    return value


def block_kernel(
    labels, orders, dp_size, tm_size, near, width_g,
    valid_ref, params_ref, clip_ref, cot_ref, weight_ref,
    out_ref, input_grad_ref, weight_grad_ref,
    earlier, next_cot, full_weight, patches, grads, held, wide, views, spread, shared, sums_in, back_in,
    *scratch,
):
    frames, half_rows, _, cols, channels = clip_ref.shape
    frames_out, half_cols, lanes = frames // 2, cols // 2, channels // 128
    area = half_rows * half_cols
    count = frames_out * area
    depth = len(labels)
    sends, receives, kept = (scratch[i * depth : (i + 1) * depth] for i in range(3))
    (send_sem, recv_sem, share_send, share_recv, ring_send, ring_recv, sum_send, sum_recv,
     far_send, far_recv, near_send, near_recv, mate_send, mate_recv, cross_send, cross_recv, own_sem) = scratch[3 * depth :]
    dp, tm = lax.axis_index("dp"), lax.axis_index("tm")
    place = {"dp": dp, "tm": tm}
    far_size = dp_size // near
    far_at, near_at = dp // near, dp % near
    core = tm % 2
    mate = {"tm": tm + 1 - 2 * core}

    def bit_of(label):
        return (place[label[0]] // 2 ** label[1]) % 2

    def partner(label):
        return {label[0]: place[label[0]] + (1 - 2 * bit_of(label)) * 2 ** label[1]}

    def send(source, target, sem_out, sem_in, device):
        copy = pltpu.make_async_remote_copy(
            src_ref=source, dst_ref=target, send_sem=sem_out, recv_sem=sem_in,
            device_id=device, device_id_type=MESH,
        )
        copy.start()
        return copy

    barrier = pltpu.get_barrier_semaphore()
    greeted = [{"tm": (tm + step) % tm_size} for step in range(1, tm_size)]
    greeted += [{"dp": dp_index} for dp_index in dp_peers(dp, dp_size, near)]
    for device in greeted:
        pl.semaphore_signal(barrier, inc=1, device_id=device, device_id_type=MESH)
    pl.semaphore_wait(barrier, len(greeted))

    ring = [
        send(clip_ref.at[frames - 2 : frames], earlier, ring_send.at[0], ring_recv.at[0], {"tm": (tm + 1) % tm_size}),
        send(cot_ref.at[0:area], next_cot, ring_send.at[1], ring_recv.at[1], {"tm": (tm + tm_size - 1) % tm_size}),
    ]

    rows_w = weight_ref.shape[0]
    half_lane = pl.ds(pl.multiple_of(core * 128, 128), 128)

    crossed = tm_size == 4 and rows_w % 48 == 0
    rows_x = rows_w // 3 if crossed else 0
    span_w = rows_w - rows_x
    across = (tm // 2) % 2 if crossed else 0
    cross_mate = {"tm": (tm + 2) % tm_size}
    span_at = across * rows_x

    def rows_of(index, start, size):
        return full_weight.at[pl.ds(pl.multiple_of(index * rows_w + start, 8), size), half_lane]

    def block_at(index):
        return rows_of(index, span_at, span_w)

    own_copy = pltpu.make_async_copy(
        weight_ref, full_weight.at[pl.ds(pl.multiple_of(dp * rows_w, 8), rows_w), :], own_sem
    )
    own_copy.start()
    own_half = weight_ref.at[pl.ds(pl.multiple_of(span_at, 8), span_w), half_lane]
    far_copies = [
        send(own_half, block_at(dp), far_send.at[step], far_recv.at[step],
             {"dp": ((far_at + step) % far_size) * near + near_at})
        for step in range(1, far_size)
    ]
    near_copies, mate_copies, cross_copies = {}, [], []

    def send_near(step, source, index):
        for hop in range(1, near):
            near_copies[step, hop] = send(
                source, block_at(index), near_send.at[step, hop], near_recv.at[step, hop],
                {"dp": far_at * near + (near_at + hop) % near},
            )

    def send_mate(step, hop, index):
        if crossed:
            cross = rows_of(index, across * (span_w), rows_x)
            copy = send(cross, cross, cross_send.at[step, hop], cross_recv.at[step, hop], cross_mate)
            cross_copies.append((copy, step, hop, index))
        mate_copies.append(
            send(block_at(index), block_at(index), mate_send.at[0, step, hop], mate_recv.at[0, step, hop], mate)
        )

    def weight_cross():
        for copy, step, hop, index in cross_copies:
            copy.wait_recv()
            rest = rows_of(index, (1 - across) * span_w, rows_x)
            mate_copies.append(
                send(rest, rest, mate_send.at[1, step, hop], mate_recv.at[1, step, hop], mate)
            )

    send_near(0, own_half, dp)

    def weight_far(step):
        far_copies[step - 1].wait_recv()
        index = ((far_at + far_size - step) % far_size) * near + near_at
        send_near(step, block_at(index), index)
        send_mate(step, 0, index)

    def weight_near(step):
        for hop in range(1, near):
            near_copies[step, hop].wait_recv()
            index = ((far_at + far_size - step) % far_size) * near + (near_at + near - hop) % near
            send_mate(step, hop, index)

    first = tm * frames
    valid = valid_ref[0]
    gain, bias = params_ref[0:1, :], params_ref[1:2, :]
    entries = jnp.full((1, channels), valid.astype(jnp.float32)) * float(2 * half_rows * cols * width_g)
    zero = jnp.zeros((8, channels), jnp.float32)

    def fold(value):
        return jnp.sum(value.reshape(-1, 8, channels), axis=0)

    def frame_mask(frame):
        slot = first + frame
        return jnp.where((slot >= 0) & (slot < valid), 1.0, 0.0).astype(jnp.float32)

    def moment_rows(index, sums):
        frame, row = index // half_rows, index % half_rows
        values = clip_ref[frame, row].astype(jnp.float32)
        masked = values * frame_mask(frame)
        return sums[0] + fold(masked), sums[1] + fold(masked * values)

    def exchange(sums, buffer, sems):
        pair = [jnp.sum(value, axis=0, keepdims=True) for value in sums]
        buffer[tm] = jnp.concatenate(pair + [jnp.zeros((6, channels), jnp.float32)], axis=0)
        copies = [
            send(buffer.at[tm], buffer.at[tm], sum_send.at[sems, step], sum_recv.at[sems, step],
                 {"tm": (tm + step) % tm_size})
            for step in range(1, tm_size)
        ]

        def finish():
            for copy in copies:
                copy.wait()
            total = buffer[0]
            for index in range(1, tm_size):
                total = total + buffer[index]
            return lane_group_sum(total, width_g)

        return finish

    finish = exchange(lax.fori_loop(0, frames * half_rows, moment_rows, (zero, zero), unroll=4), sums_in, 0)
    held[...] = jnp.zeros_like(held)
    total = finish()
    mean = total[0:1] / entries
    inv_std = lax.rsqrt(total[1:2] / entries - mean * mean + EPS)
    for copy in ring:
        copy.wait()

    ticks = [functools.partial(weight_far, step) for step in range(1, far_size)]
    for frame in range(frames + 1):
        source = earlier.at[frame] if frame < 2 else clip_ref.at[frame - 2]
        mask = frame_mask(frame - 2)

        def rows(index, _):
            values = source[index].astype(jnp.float32)
            preact = (values - mean) * inv_std * gain + bias
            hidden = preact / (1.0 + jnp.exp(-preact)) * mask
            for lane in range(lanes):
                part = hidden[:, :, lane * 128 : (lane + 1) * 128]
                held[lane, index, 1, 8 : 8 + cols, :] = part[0]
                held[lane, index + 1, 0, 8 : 8 + cols, :] = part[1]
            return 0

        lax.fori_loop(0, half_rows, rows, 0, unroll=4)
        for step_r in range(3):
            for step_c in range(3):
                pieces = [
                    held[
                        lane,
                        step_r // 2 : step_r // 2 + half_rows,
                        step_r % 2,
                        pl.ds(7 + step_c, half_cols, 2),
                        :,
                    ].reshape(area, 128)
                    for lane in range(lanes)
                ]
                piece = jnp.concatenate(pieces, axis=1).astype(jnp.bfloat16)
                for step_t in range(3):
                    if (frame - step_t) % 2 == 0 and 0 <= frame - step_t < frames:
                        at = (frame - step_t) // 2
                        tap = 9 * step_t + 3 * step_r + step_c
                        patches[at * area : (at + 1) * area, tap * channels : (tap + 1) * channels] = piece
        if frame % 3 == 2 and ticks:
            ticks.pop(0)()

    def tap_grad(tap, _):
        at = pl.multiple_of(tap * channels, channels)
        grads[pl.ds(at, channels), :] = lax.dot_general(
            patches[:, pl.ds(at, channels)],
            cot_ref[...],
            (((0,), (0,)), ((), ())),
            preferred_element_type=jnp.float32,
        )
        return 0

    for tick in ticks:
        tick()
    weight_near(0)
    lax.fori_loop(0, 27, tap_grad, 0)

    left = [list(labels) for _ in range(PARTS)]
    copies = [[None] * depth for _ in range(PARTS)]
    piece_rows = grads.shape[0] // (dp_size * tm_size * PARTS)

    def index_of(stride, number, bit):
        return (number // stride) * (2 * stride) + bit * stride + number % stride

    def read(stage, part, index):
        if stage == 0:
            at = (index * PARTS + part) * piece_rows
            if piece_rows % 8 == 0:
                return grads[pl.ds(pl.multiple_of(at, 8), piece_rows), :]
            window = (piece_rows + 14) // 8 * 8
            block = grads[pl.ds(pl.multiple_of(at // 8 * 8, 8), window), :]
            return pltpu.roll(block, (window - at % 8) % window, 0)[:piece_rows]
        return kept[stage - 1][part, index]

    def add(stage, part):
        label = orders[part][stage]
        stride = 2 ** (len(left[part]) - 1 - left[part].index(label))
        number = 2 ** (len(left[part]) - 1)
        copies[part][stage].wait_recv()

        def one(block, _):
            kept[stage][part, block] = read(
                stage, part, index_of(stride, block, bit_of(label))
            ) + receives[stage][part, block].astype(jnp.float32)
            return 0

        lax.fori_loop(0, number, one, 0)
        left[part].remove(label)

    def halve(stage):
        for part in range(PARTS):
            if stage > 0:
                add(stage - 1, part)
            label = orders[part][stage]
            stride = 2 ** (len(left[part]) - 1 - left[part].index(label))
            number = 2 ** (len(left[part]) - 1)

            def pack(block, _):
                sends[stage][part, block] = read(
                    stage, part, index_of(stride, block, 1 - bit_of(label))
                ).astype(jnp.bfloat16)
                return 0

            lax.fori_loop(0, number, pack, 0)
            copies[part][stage] = send(
                sends[stage].at[part], receives[stage].at[part],
                send_sem.at[part, stage], recv_sem.at[part, stage], partner(label),
            )

    halve(0)
    for step in range(1, far_size):
        weight_near(step)
    halve(1)
    weight_cross()
    for copy in mate_copies:
        copy.wait_recv()
    own_copy.wait()
    total = jnp.zeros((count, channels), jnp.float32)
    deep = 9 * channels
    for step in range(3):
        total += jnp.dot(
            patches[:, step * deep : (step + 1) * deep],
            full_weight[step * deep : (step + 1) * deep, :],
            preferred_element_type=jnp.float32,
        )
    out_ref[...] = total.astype(jnp.bfloat16)
    wide[...] = jnp.zeros_like(wide)
    last = jnp.where(tm < tm_size - 1, 1.0, 0.0).astype(jnp.float32)
    for frame in range(frames_out + 1):
        if frame < frames_out:
            piece = cot_ref[frame * area : (frame + 1) * area, :].astype(jnp.float32)
        else:
            piece = next_cot[...].astype(jnp.float32) * last
        wide[frame, 0:half_rows, 0:half_cols, :] = piece.reshape(half_rows, half_cols, channels)
    for dt in range(2):
        for dr in range(2):
            for dc in range(2):
                piece = wide[dt : dt + frames_out, dr : dr + half_rows, dc : dc + half_cols, :]
                views[4 * dt + 2 * dr + dc] = piece.reshape(count, channels).astype(jnp.bfloat16)
    times = (((2, 0), (0, 1)), ((1, 1),))
    spaces = (((1, 0),), ((2, 0), (0, 1)))
    stage = 2
    for part_t in range(2):
        for part_r in range(2):
            for part_c in range(2):
                total = jnp.zeros((count, channels), jnp.float32)
                for step_t, dt in times[part_t]:
                    for step_r, dr in spaces[part_r]:
                        for step_c, dc in spaces[part_c]:
                            tap = 9 * step_t + 3 * step_r + step_c
                            total += lax.dot_general(
                                views[4 * dt + 2 * dr + dc],
                                full_weight[tap * channels : (tap + 1) * channels, :],
                                (((1,), (1,)), ((), ())),
                                preferred_element_type=jnp.float32,
                            )
                total = total.reshape(frames_out, half_rows, half_cols, channels)
                for frame in range(frames_out):
                    for lane in range(lanes):
                        spread[
                            lane, 2 * frame + part_t, :, part_r, pl.ds(part_c, half_cols, 2), :
                        ] = total[frame, :, :, lane * 128 : (lane + 1) * 128]
    halve(stage)

    def back_rows(index, sums):
        frame, row = index // half_rows, index % half_rows
        normed = (clip_ref[frame, row].astype(jnp.float32) - mean) * inv_std
        preact = normed * gain + bias
        sig = 1.0 / (1.0 + jnp.exp(-preact))
        slope = sig * (1.0 + preact * (1.0 - sig))
        hidden_grad = jnp.concatenate([spread[lane, frame, row] for lane in range(lanes)], axis=-1)
        value = hidden_grad * frame_mask(frame) * slope * gain
        for lane in range(lanes):
            spread[lane, frame, row] = value[:, :, lane * 128 : (lane + 1) * 128]
        return sums[0] + fold(value), sums[1] + fold(value * normed)

    finish = exchange(lax.fori_loop(0, frames * half_rows, back_rows, (zero, zero), unroll=4), back_in, 1)
    for stage in range(3, depth):
        halve(stage)
    for part in range(PARTS):
        add(depth - 1, part)
        shared[tm, part] = kept[depth - 1][part, 0].astype(jnp.bfloat16)

    tm_bits = [label for label in labels if label[0] == "tm"]
    shares, serial = [], 0
    for label in tm_bits:
        span = 2 ** (label[1] + 1)
        stage_shares = []
        for high in range(tm_size // span):
            block = high * span + tm % span
            stage_shares.append(
                send(shared.at[block], shared.at[block],
                     share_send.at[serial], share_recv.at[serial], partner(label))
            )
            serial += 1
        if label == tm_bits[0]:
            total = finish()
            back_first, back_second = total[0:1] / entries, total[1:2] / entries

            def input_rows(index, _):
                frame, row = index // half_rows, index % half_rows
                normed = (clip_ref[frame, row].astype(jnp.float32) - mean) * inv_std
                value = jnp.concatenate([spread[lane, frame, row] for lane in range(lanes)], axis=-1)
                input_grad_ref[frame, row] = (
                    frame_mask(frame) * inv_std * (value - back_first - normed * back_second)
                ).astype(jnp.bfloat16)
                return 0

            lax.fori_loop(0, frames * half_rows, input_rows, 0, unroll=4)
        for share in stage_shares:
            share.wait_recv()
        shares += stage_shares
    for block in range(tm_size):
        weight_grad_ref[block] = shared[block].astype(jnp.float32)
    for copy in shares + far_copies + list(near_copies.values()) + mate_copies + [item[0] for item in cross_copies]:
        copy.wait_send()
    for part in range(PARTS):
        for copy in copies[part]:
            copy.wait_send()


def dp_peers(dp, dp_size, near):
    far_at, near_at, far_size = dp // near, dp % near, dp_size // near
    peers = [((far_at + step) % far_size) * near + near_at for step in range(1, far_size)]
    return peers + [far_at * near + (near_at + hop) % near for hop in range(1, near)]


def shards(dp_size, tm_size, clips, frame_counts, weight, gain, bias, cotangent):
    clip_data, cot_block = clips[0], cotangent[0]
    frame_count, row_count, col_count, channels = clip_data.shape
    frames_out, rows_out, cols_out = cot_block.shape[:3]
    area = rows_out * cols_out
    count = frames_out * area
    split = (frame_count, row_count // 2, 2, col_count, channels)
    labels, orders = plan(dp_size, tm_size)
    depth = len(labels)
    rows = dp_size * weight.shape[0]
    piece = rows // (dp_size * tm_size * PARTS)
    halves = [(PARTS, 2 ** (depth - 1 - stage), piece, channels) for stage in range(depth)]
    near = 2 ** ((dp_size.bit_length() - 1) // 2)
    far = dp_size // near
    lanes = channels // 128
    dma = pltpu.SemaphoreType.DMA
    f32, bf16 = jnp.float32, jnp.bfloat16
    output, input_grad, weight_grad = pl.pallas_call(
        functools.partial(block_kernel, labels, orders, dp_size, tm_size, near, channels // GROUPS),
        out_shape=(
            jax.ShapeDtypeStruct((count, channels), bf16),
            jax.ShapeDtypeStruct(split, bf16),
            jax.ShapeDtypeStruct((tm_size, PARTS, piece, channels), f32),
        ),
        in_specs=[SMEM] + [VMEM] * 4,
        out_specs=(VMEM, VMEM, VMEM),
        scratch_shapes=[
            pltpu.VMEM((2,) + split[1:], bf16),
            pltpu.VMEM((area, channels), bf16),
            pltpu.VMEM((rows, channels), bf16),
            pltpu.VMEM((count, rows), bf16),
            pltpu.VMEM((rows, channels), f32),
            pltpu.VMEM((lanes, rows_out + 1, 2, col_count + 8, 128), f32),
            pltpu.VMEM((frames_out + 1, rows_out + 1, 16, channels), f32),
            pltpu.VMEM((8, count, channels), bf16),
            pltpu.VMEM((lanes,) + split[:-1] + (128,), f32),
            pltpu.VMEM((tm_size, PARTS, piece, channels), bf16),
            pltpu.VMEM((tm_size, 8, channels), f32),
            pltpu.VMEM((tm_size, 8, channels), f32),
        ]
        + [pltpu.VMEM(shape, bf16) for shape in halves] * 2
        + [pltpu.VMEM(shape, f32) for shape in halves]
        + [dma((PARTS, depth))] * 2
        + [dma((tm_size,))] * 2
        + [dma((2,))] * 2
        + [dma((2, tm_size))] * 2
        + [dma((far,))] * 2
        + [dma((far, near))] * 2
        + [dma((2, far, near))] * 2
        + [dma((far, near))] * 2
        + [dma(())],
        compiler_params=pltpu.CompilerParams(
            collective_id=0, has_side_effects=True, vmem_limit_bytes=56 * 2**20
        ),
    )(frame_counts, jnp.stack([gain, bias]), clip_data.reshape(split), cot_block.reshape(count, channels), weight)
    return (
        output.reshape(cot_block.shape)[None],
        input_grad.reshape(clip_data.shape)[None],
        weight_grad.reshape(weight.shape),
    )


UP, DOWN = 0, 1
EDGE, MIDDLE = 0, 1
SIGN = (1, -1)


def ring_kernel(
    dp_size, tm_size, edge, width_g,
    valid_ref, params_ref, clip_ref, cot_ref, weight_ref,
    out_ref, input_grad_ref, weight_grad_ref,
    earlier, next_cot, full_weight, patches, turned, grads, mate_out, mate_in,
    fold_out, fold_in, edge_out, edge_in, middle_out, middle_in,
    last_edge, last_middle, share_out, share_in,
    held, wide, views, spread, sums_in, back_in,
    halo_send, halo_recv, sum_send, sum_recv, own_sem,
    gather_send, gather_recv, cross_send, cross_recv, copy_send, copy_recv,
    mate_send, mate_recv, fold_send, fold_recv, ring_send, ring_recv,
    last_send, last_recv, share_send, share_recv,
):
    frames, half_rows, _, cols, channels = clip_ref.shape
    frames_out, half_cols, lanes = frames // 2, cols // 2, channels // 128
    area = half_rows * half_cols
    count = frames_out * area
    rows_w = weight_ref.shape[0]
    middle = rows_w - 2 * edge
    dp, tm = lax.axis_index("dp"), lax.axis_index("tm")
    core, side = tm % 2, tm // 2
    mate = {"tm": tm + 1 - 2 * core}
    across = {"tm": (tm + 2) % tm_size}
    far_size, reach = dp_size // 2, dp_size // 2
    pos = dp // 2 + (dp % 2) * (2 * far_size - 1 - 2 * (dp // 2))

    def dp_at(place):
        place = (place + 2 * dp_size) % dp_size
        turn = place // far_size
        return 2 * (place + turn * (2 * far_size - 1 - 2 * place)) + turn

    onward = [{"dp": dp_at(pos + sign)} for sign in SIGN]
    pending = []

    def send(source, target, sem_out, sem_in, device):
        copy = pltpu.make_async_remote_copy(
            src_ref=source, dst_ref=target, send_sem=sem_out, recv_sem=sem_in,
            device_id=device, device_id_type=MESH,
        )
        copy.start()
        pending.append(copy)
        return copy

    barrier = pltpu.get_barrier_semaphore()
    greeted = [{"tm": (tm + step) % tm_size} for step in range(1, tm_size)] + onward
    for device in greeted:
        pl.semaphore_signal(barrier, inc=1, device_id=device, device_id_type=MESH)
    pl.semaphore_wait(barrier, len(greeted))

    edge_at, other_at = side * (edge + middle), (1 - side) * (edge + middle)
    spans = ((edge_at, edge), (edge, middle))
    half_lane = pl.ds(pl.multiple_of(core * 128, 128), 128)
    other_lane = pl.ds(pl.multiple_of((1 - core) * 128, 128), 128)

    def rows_at(block, start, size):
        return pl.ds(pl.multiple_of(block * rows_w + start, 16), size)

    gather_last = ((reach, reach - 1), (reach - 1, reach))
    gathers, crosses, mates = {}, {}, []

    def gather(way, kind, step):
        start, size = spans[kind]
        target = full_weight.at[core, rows_at(dp_at(pos - SIGN[way] * (step - 1)), start, size)]
        source = weight_ref.at[pl.ds(pl.multiple_of(start, 16), size), half_lane] if step == 1 else target
        gathers[way, kind, step] = send(
            source, target, gather_send.at[way, kind, step - 1], gather_recv.at[way, kind, step - 1], onward[way]
        )

    def gathered(way, kind, step):
        gathers[way, kind, step].wait_recv()
        if step < gather_last[way][kind]:
            gather(way, kind, step + 1)
        start, size = spans[kind]
        region = full_weight.at[core, rows_at(dp_at(pos - SIGN[way] * step), start, size)]
        if kind == EDGE:
            crosses[way, step] = send(
                region, region, cross_send.at[way, step - 1], cross_recv.at[way, step - 1], across
            )
        mates.append(
            send(region, region, copy_send.at[way, kind, step - 1], copy_recv.at[way, kind, step - 1], mate)
        )

    def crossed(way, step):
        crosses[way, step].wait_recv()
        region = full_weight.at[core, rows_at(dp_at(pos - SIGN[way] * step), other_at, edge)]
        mates.append(
            send(region, region, copy_send.at[way, 2, step - 1], copy_recv.at[way, 2, step - 1], mate)
        )

    for kind in (EDGE, MIDDLE):
        for way in (UP, DOWN):
            gather(way, kind, 1)
    own_copies = []
    for half in range(2):
        own_copies.append(
            pltpu.make_async_copy(
                weight_ref.at[:, half * 128 : (half + 1) * 128],
                full_weight.at[half, rows_at(dp, 0, rows_w)], own_sem.at[half],
            )
        )
        own_copies[half].start()

    first = tm * frames
    valid = valid_ref[0]
    gain, bias = params_ref[0:1, :], params_ref[1:2, :]
    entries = jnp.full((1, channels), valid.astype(jnp.float32)) * float(2 * half_rows * cols * width_g)
    zero = jnp.zeros((8, channels), jnp.float32)

    def fold(value):
        return jnp.sum(value.reshape(-1, 8, channels), axis=0)

    def frame_mask(frame):
        slot = first + frame
        return jnp.where((slot >= 0) & (slot < valid), 1.0, 0.0).astype(jnp.float32)

    def moment_rows(index, sums):
        frame, row = index // half_rows, index % half_rows
        values = clip_ref[frame, row].astype(jnp.float32)
        masked = values * frame_mask(frame)
        return sums[0] + fold(masked), sums[1] + fold(masked * values)

    def exchange(sums, buffer, sems):
        pair = [jnp.sum(value, axis=0, keepdims=True) for value in sums]
        buffer[tm] = jnp.concatenate(pair + [jnp.zeros((6, channels), jnp.float32)], axis=0)
        copies = [
            send(buffer.at[tm], buffer.at[tm], sum_send.at[sems, step], sum_recv.at[sems, step],
                 {"tm": (tm + step) % tm_size})
            for step in range(1, tm_size)
        ]

        def finish():
            for copy in copies:
                copy.wait_recv()
            total = buffer[0]
            for index in range(1, tm_size):
                total = total + buffer[index]
            return lane_group_sum(total, width_g)

        return finish

    finish = exchange(lax.fori_loop(0, frames * half_rows, moment_rows, (zero, zero), unroll=4), sums_in, 0)
    halos = [
        send(clip_ref.at[frames - 2 : frames], earlier, halo_send.at[0], halo_recv.at[0], {"tm": (tm + 1) % tm_size}),
        send(cot_ref.at[0:area], next_cot, halo_send.at[1], halo_recv.at[1], {"tm": (tm + tm_size - 1) % tm_size}),
    ]
    held[...] = jnp.zeros_like(held)
    turned[:, 0:128] = cot_ref[:, half_lane]
    turned[:, 128:256] = cot_ref[:, other_lane]
    gathered(UP, EDGE, 1)
    gathered(DOWN, EDGE, 1)
    total = finish()
    mean = total[0:1] / entries
    inv_std = lax.rsqrt(total[1:2] / entries - mean * mean + EPS)

    for turn, frame in enumerate([*range(2, frames + 1), 0, 1]):
        if frame == 0:
            for copy in halos:
                copy.wait_recv()
        source = earlier.at[frame] if frame < 2 else clip_ref.at[frame - 2]
        mask = frame_mask(frame - 2)

        def rows(index, _):
            values = source[index].astype(jnp.float32)
            preact = (values - mean) * inv_std * gain + bias
            hidden = preact / (1.0 + jnp.exp(-preact)) * mask
            for lane in range(lanes):
                part = hidden[:, :, lane * 128 : (lane + 1) * 128]
                held[lane, index, 1, 8 : 8 + cols, :] = part[0]
                held[lane, index + 1, 0, 8 : 8 + cols, :] = part[1]
            return 0

        lax.fori_loop(0, half_rows, rows, 0, unroll=4)
        for step_r in range(3):
            for step_c in range(3):
                pieces = [
                    held[
                        lane,
                        step_r // 2 : step_r // 2 + half_rows,
                        step_r % 2,
                        pl.ds(7 + step_c, half_cols, 2),
                        :,
                    ].reshape(area, 128)
                    for lane in range(lanes)
                ]
                piece = jnp.concatenate(pieces, axis=1).astype(jnp.bfloat16)
                for step_t in range(3):
                    if (frame - step_t) % 2 == 0 and 0 <= frame - step_t < frames:
                        at = (frame - step_t) // 2
                        tap = 9 * step_t + 3 * step_r + step_c
                        patches[at * area : (at + 1) * area, tap * channels : (tap + 1) * channels] = piece
        if turn == 5:
            gathered(UP, MIDDLE, 1)
            gathered(DOWN, MIDDLE, 1)

    def tap_grad(tap, _):
        at = pl.multiple_of(tap * channels, channels)
        value = lax.dot_general(
            patches[:, pl.ds(at, channels)],
            turned[...],
            (((0,), (0,)), ((), ())),
            preferred_element_type=jnp.float32,
        )
        grads[pl.ds(at, channels), :] = value[:, 0:128]
        mate_out[pl.ds(at, channels), :] = value[:, 128:256].astype(jnp.bfloat16)
        return 0

    ticks = {
        0: [(crossed, UP, 1), (crossed, DOWN, 1)],
        1: [(gathered, UP, EDGE, 2), (gathered, DOWN, EDGE, 2)],
        4: [(gathered, UP, MIDDLE, 2), (gathered, DOWN, MIDDLE, 2)],
        5: [(crossed, UP, 2), (crossed, DOWN, 2)],
        7: [(gathered, UP, EDGE, 3), (gathered, DOWN, EDGE, 3)],
    }
    swaps = []
    for group in range(9):
        lax.fori_loop(3 * group, 3 * group + 3, tap_grad, 0, unroll=3)
        span = pl.ds(3 * group * channels, 3 * channels)
        swaps.append(send(mate_out.at[span], mate_in.at[span], mate_send.at[group], mate_recv.at[group], mate))
        for call, *args in ticks.get(group, ()):
            call(*args)

    for copy in swaps:
        copy.wait_recv()

    def base(block, start, size):
        span = rows_at(block, start, size)
        return grads[span, :] + mate_in[span, :].astype(jnp.float32)

    rings, folds = {}, {}
    ring_last = ((reach - 1, reach), (reach, reach - 1))
    ring_out, ring_in = (edge_out, middle_out), (edge_in, middle_in)

    def fold_over(offset):
        index = offset % dp_size
        fold_out[index] = base(dp_at(pos + offset), other_at, edge).astype(jnp.bfloat16)
        folds[index] = send(fold_out.at[index], fold_in.at[index], fold_send.at[index], fold_recv.at[index], across)

    def gradient(way, kind, step):
        offset = SIGN[way] * step
        value = base(dp_at(pos + offset), *spans[kind])
        if kind == EDGE:
            folds[offset % dp_size].wait_recv()
            value = value + fold_in[offset % dp_size].astype(jnp.float32)
        if step < ring_last[way][kind]:
            rings[way, kind, step + 1].wait_recv()
            value = value + ring_in[kind][way, step].astype(jnp.float32)
        ring_out[kind][way, step - 1] = value.astype(jnp.bfloat16)
        rings[way, kind, step] = send(
            ring_out[kind].at[way, step - 1], ring_in[kind].at[way, step - 1],
            ring_send.at[way, kind, step - 1], ring_recv.at[way, kind, step - 1], onward[way],
        )

    lasts, shares = {}, []

    def summed(kind):
        value = base(dp, *spans[kind])
        if kind == EDGE:
            folds[0].wait_recv()
            value = value + fold_in[0].astype(jnp.float32)
        for way in (UP, DOWN):
            rings[way, kind, 1].wait_recv()
            value = value + ring_in[kind][way, 0].astype(jnp.float32)
        last = (last_edge, last_middle)[kind]
        last[0] = value.astype(jnp.bfloat16)
        lasts[kind] = send(last.at[0], last.at[1], last_send.at[kind], last_recv.at[kind], across)
        if kind == EDGE:
            share(edge_at, edge, last_edge[0].astype(jnp.float32))

    def share(start, size, value):
        span = pl.ds(pl.multiple_of(start, 16), size)
        share_out[span, :] = value
        at = len(shares)
        shares.append(send(share_out.at[span], share_in.at[span], share_send.at[at], share_recv.at[at], mate))

    def shared(kind):
        lasts[kind].wait_recv()
        if kind == EDGE:
            share(other_at, edge, last_edge[1].astype(jnp.float32))
        else:
            share(edge, middle, last_middle[0].astype(jnp.float32) + last_middle[1].astype(jnp.float32))

    gradient(UP, MIDDLE, reach)
    gradient(DOWN, MIDDLE, reach - 1)
    fold_over(reach)
    for step in range(reach - 1, 0, -1):
        fold_over(step)
        fold_over(-step)
    fold_over(0)
    gathered(UP, MIDDLE, 3)
    gathered(DOWN, MIDDLE, 3)
    crossed(UP, 3)
    crossed(DOWN, 3)
    gathered(UP, EDGE, 4)
    gathered(DOWN, MIDDLE, 4)
    gradient(DOWN, EDGE, 4)
    gradient(UP, EDGE, 3)
    gradient(UP, MIDDLE, 3)
    gradient(DOWN, MIDDLE, 2)

    wide[...] = jnp.zeros_like(wide)
    inner = jnp.where(tm < tm_size - 1, 1.0, 0.0).astype(jnp.float32)
    for frame in range(frames_out + 1):
        if frame < frames_out:
            piece = cot_ref[frame * area : (frame + 1) * area, :].astype(jnp.float32)
        else:
            piece = next_cot[...].astype(jnp.float32) * inner
        wide[frame, 0:half_rows, 0:half_cols, :] = piece.reshape(half_rows, half_cols, channels)
    for dt in range(2):
        for dr in range(2):
            for dc in range(2):
                piece = wide[dt : dt + frames_out, dr : dr + half_rows, dc : dc + half_cols, :]
                views[4 * dt + 2 * dr + dc] = piece.reshape(count, channels).astype(jnp.bfloat16)

    crossed(UP, 4)
    for copy in mates:
        copy.wait_recv()
    for copy in own_copies:
        copy.wait()
    gradient(DOWN, EDGE, 3)
    gradient(UP, EDGE, 2)

    def weight_rows(start, size):
        return jnp.concatenate([full_weight[half, start : start + size, :] for half in range(2)], axis=1)

    times = (((2, 0), (0, 1)), ((1, 1),))
    spaces = (((1, 0),), ((2, 0), (0, 1)))
    later = {
        0: [(gradient, UP, MIDDLE, 2), (gradient, DOWN, MIDDLE, 1)],
        4: [(gradient, DOWN, EDGE, 2), (gradient, UP, EDGE, 1)],
    }
    for part in range(8):
        part_t, part_r, part_c = part // 4, part // 2 % 2, part % 2
        total = jnp.zeros((count, channels), jnp.float32)
        for step_t, dt in times[part_t]:
            for step_r, dr in spaces[part_r]:
                for step_c, dc in spaces[part_c]:
                    tap = 9 * step_t + 3 * step_r + step_c
                    total += lax.dot_general(
                        views[4 * dt + 2 * dr + dc],
                        weight_rows(tap * channels, channels),
                        (((1,), (1,)), ((), ())),
                        preferred_element_type=jnp.float32,
                    )
        total = total.reshape(frames_out, half_rows, half_cols, channels)
        for frame in range(frames_out):
            for lane in range(lanes):
                spread[
                    lane, 2 * frame + part_t, :, part_r, pl.ds(part_c, half_cols, 2), :
                ] = total[frame, :, :, lane * 128 : (lane + 1) * 128]
        for call, *args in later.get(part, ()):
            call(*args)

    def back_rows(index, sums):
        frame, row = index // half_rows, index % half_rows
        normed = (clip_ref[frame, row].astype(jnp.float32) - mean) * inv_std
        preact = normed * gain + bias
        sig = 1.0 / (1.0 + jnp.exp(-preact))
        slope = sig * (1.0 + preact * (1.0 - sig))
        hidden_grad = jnp.concatenate([spread[lane, frame, row] for lane in range(lanes)], axis=-1)
        value = hidden_grad * frame_mask(frame) * slope * gain
        for lane in range(lanes):
            spread[lane, frame, row] = value[:, :, lane * 128 : (lane + 1) * 128]
        return sums[0] + fold(value), sums[1] + fold(value * normed)

    finish = exchange(lax.fori_loop(0, frames * half_rows, back_rows, (zero, zero), unroll=4), back_in, 1)
    gradient(UP, MIDDLE, 1)
    gradient(DOWN, EDGE, 1)

    total = jnp.zeros((count, channels), jnp.float32)
    deep = 9 * channels
    for step in range(3):
        total += jnp.dot(
            patches[:, step * deep : (step + 1) * deep],
            weight_rows(step * deep, deep),
            preferred_element_type=jnp.float32,
        )
    out_ref[...] = total.astype(jnp.bfloat16)

    total = finish()
    back_first, back_second = total[0:1] / entries, total[1:2] / entries

    def input_rows(index, _):
        frame, row = index // half_rows, index % half_rows
        normed = (clip_ref[frame, row].astype(jnp.float32) - mean) * inv_std
        value = jnp.concatenate([spread[lane, frame, row] for lane in range(lanes)], axis=-1)
        input_grad_ref[frame, row] = (
            frame_mask(frame) * inv_std * (value - back_first - normed * back_second)
        ).astype(jnp.bfloat16)
        return 0

    lax.fori_loop(0, frames * half_rows, input_rows, 0, unroll=4)
    summed(EDGE)
    summed(MIDDLE)
    shared(EDGE)
    shared(MIDDLE)
    for copy in shares:
        copy.wait_recv()
    weight_grad_ref[:, half_lane] = share_out[...]
    weight_grad_ref[:, other_lane] = share_in[...]
    for copy in pending:
        copy.wait_send()


def ring_shards(dp_size, tm_size, clips, frame_counts, weight, gain, bias, cotangent):
    clip_data, cot_block = clips[0], cotangent[0]
    frame_count, row_count, col_count, channels = clip_data.shape
    frames_out, rows_out, cols_out = cot_block.shape[:3]
    area = rows_out * cols_out
    count = frames_out * area
    split = (frame_count, row_count // 2, 2, col_count, channels)
    rows_w = weight.shape[0]
    rows = dp_size * rows_w
    lanes = channels // 128
    edge = rows_w * 13 // 50 // 16 * 16
    middle = rows_w - 2 * edge
    reach = dp_size // 2
    dma = pltpu.SemaphoreType.DMA
    f32, bf16 = jnp.float32, jnp.bfloat16
    sems = [(2,), (2, tm_size)]
    pairs = [
        (2, 2, reach), (2, reach), (2, 3, reach), (9,), (dp_size,), (2, 2, reach), (2,), (3,),
    ]
    output, input_grad, weight_grad = pl.pallas_call(
        functools.partial(ring_kernel, dp_size, tm_size, edge, channels // GROUPS),
        out_shape=(
            jax.ShapeDtypeStruct((count, channels), bf16),
            jax.ShapeDtypeStruct(split, bf16),
            jax.ShapeDtypeStruct((rows_w, channels), f32),
        ),
        in_specs=[SMEM] + [VMEM] * 4,
        out_specs=(VMEM, VMEM, VMEM),
        scratch_shapes=[
            pltpu.VMEM((2,) + split[1:], bf16),
            pltpu.VMEM((area, channels), bf16),
            pltpu.VMEM((2, rows, 128), bf16),
            pltpu.VMEM((count, rows), bf16),
            pltpu.VMEM((count, channels), bf16),
            pltpu.VMEM((rows, 128), f32),
            pltpu.VMEM((rows, 128), bf16),
            pltpu.VMEM((rows, 128), bf16),
            pltpu.VMEM((dp_size, edge, 128), bf16),
            pltpu.VMEM((dp_size, edge, 128), bf16),
            pltpu.VMEM((2, reach, edge, 128), bf16),
            pltpu.VMEM((2, reach, edge, 128), bf16),
            pltpu.VMEM((2, reach, middle, 128), bf16),
            pltpu.VMEM((2, reach, middle, 128), bf16),
            pltpu.VMEM((2, edge, 128), bf16),
            pltpu.VMEM((2, middle, 128), bf16),
            pltpu.VMEM((rows_w, 128), f32),
            pltpu.VMEM((rows_w, 128), f32),
            pltpu.VMEM((lanes, rows_out + 1, 2, col_count + 8, 128), f32),
            pltpu.VMEM((frames_out + 1, rows_out + 1, 16, channels), f32),
            pltpu.VMEM((8, count, channels), bf16),
            pltpu.VMEM((lanes,) + split[:-1] + (128,), f32),
            pltpu.VMEM((tm_size, 8, channels), f32),
            pltpu.VMEM((tm_size, 8, channels), f32),
        ]
        + [dma((2,))] * 2
        + [dma((2, tm_size))] * 2
        + [dma((2,))]
        + [dma(shape) for shape in pairs for _ in range(2)],
        compiler_params=pltpu.CompilerParams(
            collective_id=0, has_side_effects=True, vmem_limit_bytes=56 * 2**20
        ),
    )(frame_counts, jnp.stack([gain, bias]), clip_data.reshape(split), cot_block.reshape(count, channels), weight)
    return (
        output.reshape(cot_block.shape)[None],
        input_grad.reshape(clip_data.shape)[None],
        weight_grad,
    )


def by_ring(dp_size, tm_size, weight_rows):
    return dp_size == 8 and tm_size == 4 and weight_rows % 16 == 0


def device_part(dp_size, tm_size, *arrays):
    chosen = ring_shards if by_ring(dp_size, tm_size, arrays[2].shape[0]) else shards
    return chosen(dp_size, tm_size, *arrays)


def solution(mesh):
    placed = (
        P("dp", "tm", None, None, None),
        P("dp"),
        P("dp", None),
        P(),
        P(),
        P("dp", "tm", None, None, None),
    )
    return jax.shard_map(
        functools.partial(device_part, mesh.shape["dp"], mesh.shape["tm"]),
        mesh=mesh,
        in_specs=placed,
        out_specs=(P("dp", "tm", None, None, None), P("dp", "tm", None, None, None), P("dp", None)),
        check_vma=False,
    )
```

```python
import functools

import jax
import jax.numpy as jnp
from jax import lax
from jax.experimental import pallas as pl
from jax.experimental.pallas import tpu as pltpu
from jax.sharding import PartitionSpec as P

GROUPS = 32
EPS = 1e-06
PARTS = 3
MESH = pl.DeviceIdType.MESH
VMEM = pl.BlockSpec(memory_space=pltpu.VMEM)
SMEM = pl.BlockSpec(memory_space=pltpu.SMEM)


def plan(dp_size, tm_size):
    dp_bits = [("dp", k) for k in range(dp_size.bit_length() - 1)]
    tm_bits = [("tm", k) for k in range(tm_size.bit_length() - 1)]
    cut = len(dp_bits) // 2
    ways = [tm_bits[1:], dp_bits[:cut], dp_bits[cut:]]
    orders = []
    for part in range(PARTS):
        turned = ways[part:] + ways[:part]
        orders.append(tm_bits[:1] + turned[0] + turned[1] + turned[2])
    return dp_bits[::-1] + tm_bits[::-1], orders


def lane_group_sum(value, width):
    channels = value.shape[-1]
    lane = lax.broadcasted_iota(jnp.int32, value.shape, value.ndim - 1)
    step = 1
    while step < width:
        above = pltpu.roll(value, channels - step, value.ndim - 1)
        below = pltpu.roll(value, step, value.ndim - 1)
        value = value + jnp.where((lane // step) % 2 == 0, above, below)
        step *= 2
    return value


def block_kernel(
    labels, orders, dp_size, tm_size, near, width_g,
    valid_ref, params_ref, clip_ref, cot_ref, weight_ref,
    out_ref, input_grad_ref, weight_grad_ref,
    earlier, next_cot, full_weight, patches, grads, held, wide, views, spread, shared, sums_in, back_in,
    *scratch,
):
    frames, half_rows, _, cols, channels = clip_ref.shape
    frames_out, half_cols, lanes = frames // 2, cols // 2, channels // 128
    area = half_rows * half_cols
    count = frames_out * area
    depth = len(labels)
    sends, receives, kept = (scratch[i * depth : (i + 1) * depth] for i in range(3))
    (send_sem, recv_sem, share_send, share_recv, ring_send, ring_recv, sum_send, sum_recv,
     far_send, far_recv, near_send, near_recv, mate_send, mate_recv, cross_send, cross_recv, own_sem) = scratch[3 * depth :]
    dp, tm = lax.axis_index("dp"), lax.axis_index("tm")
    place = {"dp": dp, "tm": tm}
    far_size = dp_size // near
    far_at, near_at = dp // near, dp % near
    core = tm % 2
    mate = {"tm": tm + 1 - 2 * core}

    def bit_of(label):
        return (place[label[0]] // 2 ** label[1]) % 2

    def partner(label):
        return {label[0]: place[label[0]] + (1 - 2 * bit_of(label)) * 2 ** label[1]}

    def send(source, target, sem_out, sem_in, device):
        copy = pltpu.make_async_remote_copy(
            src_ref=source, dst_ref=target, send_sem=sem_out, recv_sem=sem_in,
            device_id=device, device_id_type=MESH,
        )
        copy.start()
        return copy

    barrier = pltpu.get_barrier_semaphore()
    greeted = [{"tm": (tm + step) % tm_size} for step in range(1, tm_size)]
    greeted += [{"dp": dp_index} for dp_index in dp_peers(dp, dp_size, near)]
    for device in greeted:
        pl.semaphore_signal(barrier, inc=1, device_id=device, device_id_type=MESH)
    pl.semaphore_wait(barrier, len(greeted))

    ring = [
        send(clip_ref.at[frames - 2 : frames], earlier, ring_send.at[0], ring_recv.at[0], {"tm": (tm + 1) % tm_size}),
        send(cot_ref.at[0:area], next_cot, ring_send.at[1], ring_recv.at[1], {"tm": (tm + tm_size - 1) % tm_size}),
    ]

    rows_w = weight_ref.shape[0]
    half_lane = pl.ds(pl.multiple_of(core * 128, 128), 128)

    crossed = tm_size == 4 and rows_w % 48 == 0
    rows_x = rows_w // 3 if crossed else 0
    span_w = rows_w - rows_x
    across = (tm // 2) % 2 if crossed else 0
    cross_mate = {"tm": (tm + 2) % tm_size}
    span_at = across * rows_x

    def rows_of(index, start, size):
        return full_weight.at[pl.ds(pl.multiple_of(index * rows_w + start, 8), size), half_lane]

    def block_at(index):
        return rows_of(index, span_at, span_w)

    own_copy = pltpu.make_async_copy(
        weight_ref, full_weight.at[pl.ds(pl.multiple_of(dp * rows_w, 8), rows_w), :], own_sem
    )
    own_copy.start()
    own_half = weight_ref.at[pl.ds(pl.multiple_of(span_at, 8), span_w), half_lane]
    far_copies = [
        send(own_half, block_at(dp), far_send.at[step], far_recv.at[step],
             {"dp": ((far_at + step) % far_size) * near + near_at})
        for step in range(1, far_size)
    ]
    near_copies, mate_copies, cross_copies = {}, [], []

    def send_near(step, source, index):
        for hop in range(1, near):
            near_copies[step, hop] = send(
                source, block_at(index), near_send.at[step, hop], near_recv.at[step, hop],
                {"dp": far_at * near + (near_at + hop) % near},
            )

    def send_mate(step, hop, index):
        if crossed:
            cross = rows_of(index, across * (span_w), rows_x)
            copy = send(cross, cross, cross_send.at[step, hop], cross_recv.at[step, hop], cross_mate)
            cross_copies.append((copy, step, hop, index))
        mate_copies.append(
            send(block_at(index), block_at(index), mate_send.at[0, step, hop], mate_recv.at[0, step, hop], mate)
        )

    def weight_cross():
        for copy, step, hop, index in cross_copies:
            copy.wait_recv()
            rest = rows_of(index, (1 - across) * span_w, rows_x)
            mate_copies.append(
                send(rest, rest, mate_send.at[1, step, hop], mate_recv.at[1, step, hop], mate)
            )

    send_near(0, own_half, dp)

    def weight_far(step):
        far_copies[step - 1].wait_recv()
        index = ((far_at + far_size - step) % far_size) * near + near_at
        send_near(step, block_at(index), index)
        send_mate(step, 0, index)

    def weight_near(step):
        for hop in range(1, near):
            near_copies[step, hop].wait_recv()
            index = ((far_at + far_size - step) % far_size) * near + (near_at + near - hop) % near
            send_mate(step, hop, index)

    first = tm * frames
    valid = valid_ref[0]
    gain, bias = params_ref[0:1, :], params_ref[1:2, :]
    entries = jnp.full((1, channels), valid.astype(jnp.float32)) * float(2 * half_rows * cols * width_g)
    zero = jnp.zeros((8, channels), jnp.float32)

    def fold(value):
        return jnp.sum(value.reshape(-1, 8, channels), axis=0)

    def frame_mask(frame):
        slot = first + frame
        return jnp.where((slot >= 0) & (slot < valid), 1.0, 0.0).astype(jnp.float32)

    def moment_rows(index, sums):
        frame, row = index // half_rows, index % half_rows
        values = clip_ref[frame, row].astype(jnp.float32)
        masked = values * frame_mask(frame)
        return sums[0] + fold(masked), sums[1] + fold(masked * values)

    def exchange(sums, buffer, sems):
        pair = [jnp.sum(value, axis=0, keepdims=True) for value in sums]
        buffer[tm] = jnp.concatenate(pair + [jnp.zeros((6, channels), jnp.float32)], axis=0)
        copies = [
            send(buffer.at[tm], buffer.at[tm], sum_send.at[sems, step], sum_recv.at[sems, step],
                 {"tm": (tm + step) % tm_size})
            for step in range(1, tm_size)
        ]

        def finish():
            for copy in copies:
                copy.wait()
            total = buffer[0]
            for index in range(1, tm_size):
                total = total + buffer[index]
            return lane_group_sum(total, width_g)

        return finish

    finish = exchange(lax.fori_loop(0, frames * half_rows, moment_rows, (zero, zero), unroll=4), sums_in, 0)
    held[...] = jnp.zeros_like(held)
    total = finish()
    mean = total[0:1] / entries
    inv_std = lax.rsqrt(total[1:2] / entries - mean * mean + EPS)
    for copy in ring:
        copy.wait()

    ticks = [functools.partial(weight_far, step) for step in range(1, far_size)]
    for frame in range(frames + 1):
        source = earlier.at[frame] if frame < 2 else clip_ref.at[frame - 2]
        mask = frame_mask(frame - 2)

        def rows(index, _):
            values = source[index].astype(jnp.float32)
            preact = (values - mean) * inv_std * gain + bias
            hidden = preact / (1.0 + jnp.exp(-preact)) * mask
            for lane in range(lanes):
                part = hidden[:, :, lane * 128 : (lane + 1) * 128]
                held[lane, index, 1, 8 : 8 + cols, :] = part[0]
                held[lane, index + 1, 0, 8 : 8 + cols, :] = part[1]
            return 0

        lax.fori_loop(0, half_rows, rows, 0, unroll=4)
        for step_r in range(3):
            for step_c in range(3):
                pieces = [
                    held[
                        lane,
                        step_r // 2 : step_r // 2 + half_rows,
                        step_r % 2,
                        pl.ds(7 + step_c, half_cols, 2),
                        :,
                    ].reshape(area, 128)
                    for lane in range(lanes)
                ]
                piece = jnp.concatenate(pieces, axis=1).astype(jnp.bfloat16)
                for step_t in range(3):
                    if (frame - step_t) % 2 == 0 and 0 <= frame - step_t < frames:
                        at = (frame - step_t) // 2
                        tap = 9 * step_t + 3 * step_r + step_c
                        patches[at * area : (at + 1) * area, tap * channels : (tap + 1) * channels] = piece
        if frame % 3 == 2 and ticks:
            ticks.pop(0)()

    def tap_grad(tap, _):
        at = pl.multiple_of(tap * channels, channels)
        grads[pl.ds(at, channels), :] = lax.dot_general(
            patches[:, pl.ds(at, channels)],
            cot_ref[...],
            (((0,), (0,)), ((), ())),
            preferred_element_type=jnp.float32,
        )
        return 0

    for tick in ticks:
        tick()
    weight_near(0)
    lax.fori_loop(0, 27, tap_grad, 0)

    left = [list(labels) for _ in range(PARTS)]
    copies = [[None] * depth for _ in range(PARTS)]
    piece_rows = grads.shape[0] // (dp_size * tm_size * PARTS)

    def index_of(stride, number, bit):
        return (number // stride) * (2 * stride) + bit * stride + number % stride

    def read(stage, part, index):
        if stage == 0:
            at = (index * PARTS + part) * piece_rows
            if piece_rows % 8 == 0:
                return grads[pl.ds(pl.multiple_of(at, 8), piece_rows), :]
            window = (piece_rows + 14) // 8 * 8
            block = grads[pl.ds(pl.multiple_of(at // 8 * 8, 8), window), :]
            return pltpu.roll(block, (window - at % 8) % window, 0)[:piece_rows]
        return kept[stage - 1][part, index]

    def add(stage, part):
        label = orders[part][stage]
        stride = 2 ** (len(left[part]) - 1 - left[part].index(label))
        number = 2 ** (len(left[part]) - 1)
        copies[part][stage].wait_recv()

        def one(block, _):
            kept[stage][part, block] = read(
                stage, part, index_of(stride, block, bit_of(label))
            ) + receives[stage][part, block].astype(jnp.float32)
            return 0

        lax.fori_loop(0, number, one, 0)
        left[part].remove(label)

    def halve(stage):
        for part in range(PARTS):
            if stage > 0:
                add(stage - 1, part)
            label = orders[part][stage]
            stride = 2 ** (len(left[part]) - 1 - left[part].index(label))
            number = 2 ** (len(left[part]) - 1)

            def pack(block, _):
                sends[stage][part, block] = read(
                    stage, part, index_of(stride, block, 1 - bit_of(label))
                ).astype(jnp.bfloat16)
                return 0

            lax.fori_loop(0, number, pack, 0)
            copies[part][stage] = send(
                sends[stage].at[part], receives[stage].at[part],
                send_sem.at[part, stage], recv_sem.at[part, stage], partner(label),
            )

    halve(0)
    for step in range(1, far_size):
        weight_near(step)
    halve(1)
    weight_cross()
    for copy in mate_copies:
        copy.wait_recv()
    own_copy.wait()
    total = jnp.zeros((count, channels), jnp.float32)
    deep = 9 * channels
    for step in range(3):
        total += jnp.dot(
            patches[:, step * deep : (step + 1) * deep],
            full_weight[step * deep : (step + 1) * deep, :],
            preferred_element_type=jnp.float32,
        )
    out_ref[...] = total.astype(jnp.bfloat16)
    wide[...] = jnp.zeros_like(wide)
    last = jnp.where(tm < tm_size - 1, 1.0, 0.0).astype(jnp.float32)
    for frame in range(frames_out + 1):
        if frame < frames_out:
            piece = cot_ref[frame * area : (frame + 1) * area, :].astype(jnp.float32)
        else:
            piece = next_cot[...].astype(jnp.float32) * last
        wide[frame, 0:half_rows, 0:half_cols, :] = piece.reshape(half_rows, half_cols, channels)
    for dt in range(2):
        for dr in range(2):
            for dc in range(2):
                piece = wide[dt : dt + frames_out, dr : dr + half_rows, dc : dc + half_cols, :]
                views[4 * dt + 2 * dr + dc] = piece.reshape(count, channels).astype(jnp.bfloat16)
    times = (((2, 0), (0, 1)), ((1, 1),))
    spaces = (((1, 0),), ((2, 0), (0, 1)))
    stage = 2
    for part_t in range(2):
        for part_r in range(2):
            for part_c in range(2):
                total = jnp.zeros((count, channels), jnp.float32)
                for step_t, dt in times[part_t]:
                    for step_r, dr in spaces[part_r]:
                        for step_c, dc in spaces[part_c]:
                            tap = 9 * step_t + 3 * step_r + step_c
                            total += lax.dot_general(
                                views[4 * dt + 2 * dr + dc],
                                full_weight[tap * channels : (tap + 1) * channels, :],
                                (((1,), (1,)), ((), ())),
                                preferred_element_type=jnp.float32,
                            )
                total = total.reshape(frames_out, half_rows, half_cols, channels)
                for frame in range(frames_out):
                    for lane in range(lanes):
                        spread[
                            lane, 2 * frame + part_t, :, part_r, pl.ds(part_c, half_cols, 2), :
                        ] = total[frame, :, :, lane * 128 : (lane + 1) * 128]
    halve(stage)

    def back_rows(index, sums):
        frame, row = index // half_rows, index % half_rows
        normed = (clip_ref[frame, row].astype(jnp.float32) - mean) * inv_std
        preact = normed * gain + bias
        sig = 1.0 / (1.0 + jnp.exp(-preact))
        slope = sig * (1.0 + preact * (1.0 - sig))
        hidden_grad = jnp.concatenate([spread[lane, frame, row] for lane in range(lanes)], axis=-1)
        value = hidden_grad * frame_mask(frame) * slope * gain
        for lane in range(lanes):
            spread[lane, frame, row] = value[:, :, lane * 128 : (lane + 1) * 128]
        return sums[0] + fold(value), sums[1] + fold(value * normed)

    finish = exchange(lax.fori_loop(0, frames * half_rows, back_rows, (zero, zero), unroll=4), back_in, 1)
    for stage in range(3, depth):
        halve(stage)
    for part in range(PARTS):
        add(depth - 1, part)
        shared[tm, part] = kept[depth - 1][part, 0].astype(jnp.bfloat16)

    tm_bits = [label for label in labels if label[0] == "tm"]
    shares, serial = [], 0
    for label in tm_bits:
        span = 2 ** (label[1] + 1)
        stage_shares = []
        for high in range(tm_size // span):
            block = high * span + tm % span
            stage_shares.append(
                send(shared.at[block], shared.at[block],
                     share_send.at[serial], share_recv.at[serial], partner(label))
            )
            serial += 1
        if label == tm_bits[0]:
            total = finish()
            back_first, back_second = total[0:1] / entries, total[1:2] / entries

            def input_rows(index, _):
                frame, row = index // half_rows, index % half_rows
                normed = (clip_ref[frame, row].astype(jnp.float32) - mean) * inv_std
                value = jnp.concatenate([spread[lane, frame, row] for lane in range(lanes)], axis=-1)
                input_grad_ref[frame, row] = (
                    frame_mask(frame) * inv_std * (value - back_first - normed * back_second)
                ).astype(jnp.bfloat16)
                return 0

            lax.fori_loop(0, frames * half_rows, input_rows, 0, unroll=4)
        for share in stage_shares:
            share.wait_recv()
        shares += stage_shares
    for block in range(tm_size):
        weight_grad_ref[block] = shared[block].astype(jnp.float32)
    for copy in shares + far_copies + list(near_copies.values()) + mate_copies + [item[0] for item in cross_copies]:
        copy.wait_send()
    for part in range(PARTS):
        for copy in copies[part]:
            copy.wait_send()


def dp_peers(dp, dp_size, near):
    far_at, near_at, far_size = dp // near, dp % near, dp_size // near
    peers = [((far_at + step) % far_size) * near + near_at for step in range(1, far_size)]
    return peers + [far_at * near + (near_at + hop) % near for hop in range(1, near)]


def shards(dp_size, tm_size, clips, frame_counts, weight, gain, bias, cotangent):
    clip_data, cot_block = clips[0], cotangent[0]
    frame_count, row_count, col_count, channels = clip_data.shape
    frames_out, rows_out, cols_out = cot_block.shape[:3]
    area = rows_out * cols_out
    count = frames_out * area
    split = (frame_count, row_count // 2, 2, col_count, channels)
    labels, orders = plan(dp_size, tm_size)
    depth = len(labels)
    rows = dp_size * weight.shape[0]
    piece = rows // (dp_size * tm_size * PARTS)
    halves = [(PARTS, 2 ** (depth - 1 - stage), piece, channels) for stage in range(depth)]
    near = 2 ** ((dp_size.bit_length() - 1) // 2)
    far = dp_size // near
    lanes = channels // 128
    dma = pltpu.SemaphoreType.DMA
    f32, bf16 = jnp.float32, jnp.bfloat16
    output, input_grad, weight_grad = pl.pallas_call(
        functools.partial(block_kernel, labels, orders, dp_size, tm_size, near, channels // GROUPS),
        out_shape=(
            jax.ShapeDtypeStruct((count, channels), bf16),
            jax.ShapeDtypeStruct(split, bf16),
            jax.ShapeDtypeStruct((tm_size, PARTS, piece, channels), f32),
        ),
        in_specs=[SMEM] + [VMEM] * 4,
        out_specs=(VMEM, VMEM, VMEM),
        scratch_shapes=[
            pltpu.VMEM((2,) + split[1:], bf16),
            pltpu.VMEM((area, channels), bf16),
            pltpu.VMEM((rows, channels), bf16),
            pltpu.VMEM((count, rows), bf16),
            pltpu.VMEM((rows, channels), f32),
            pltpu.VMEM((lanes, rows_out + 1, 2, col_count + 8, 128), f32),
            pltpu.VMEM((frames_out + 1, rows_out + 1, 16, channels), f32),
            pltpu.VMEM((8, count, channels), bf16),
            pltpu.VMEM((lanes,) + split[:-1] + (128,), f32),
            pltpu.VMEM((tm_size, PARTS, piece, channels), bf16),
            pltpu.VMEM((tm_size, 8, channels), f32),
            pltpu.VMEM((tm_size, 8, channels), f32),
        ]
        + [pltpu.VMEM(shape, bf16) for shape in halves] * 2
        + [pltpu.VMEM(shape, f32) for shape in halves]
        + [dma((PARTS, depth))] * 2
        + [dma((tm_size,))] * 2
        + [dma((2,))] * 2
        + [dma((2, tm_size))] * 2
        + [dma((far,))] * 2
        + [dma((far, near))] * 2
        + [dma((2, far, near))] * 2
        + [dma((far, near))] * 2
        + [dma(())],
        compiler_params=pltpu.CompilerParams(
            collective_id=0, has_side_effects=True, vmem_limit_bytes=56 * 2**20
        ),
    )(frame_counts, jnp.stack([gain, bias]), clip_data.reshape(split), cot_block.reshape(count, channels), weight)
    return (
        output.reshape(cot_block.shape)[None],
        input_grad.reshape(clip_data.shape)[None],
        weight_grad.reshape(weight.shape),
    )


HBM = pl.BlockSpec(memory_space=pl.ANY)
UP, DOWN = 0, 1
EDGE, MIDDLE = 0, 1
SIGN = (1, -1)
COPY_PARTS = 2
RING_VMEM = 54 * 2**20
COPY_VMEM = 16 * 2**20
ORDER = (
    ("m",), ("s",), ("p", 1), ("p", 3), ("p", 5), ("p", 2), ("g", 1, 0, 1, 0), ("g", 0, 0, 1, 0), ("p", 6),
    ("p", 0), ("g", 0, 0, 1, 1), ("p", 4), ("g", 1, 1, 1, 0), ("g", 0, 1, 1, 0), ("g", 0, 1, 1, 1),
    ("g", 1, 1, 1, 1), ("g", 1, 0, 1, 1), ("p", 7), ("p", 8), ("t", 0), ("t", 1), ("g", 1, 0, 2, 0), ("t", 2),
    ("g", 0, 0, 2, 0), ("t", 3), ("t", 4), ("g", 0, 0, 2, 1), ("g", 0, 1, 2, 0), ("g", 1, 1, 2, 0), ("t", 5),
    ("t", 6), ("t", 7), ("g", 1, 0, 2, 1), ("g", 0, 1, 2, 1), ("x", 0, 1, 0), ("g", 1, 1, 2, 1), ("r", 0, 1, 4, 0),
    ("g", 1, 0, 3, 0), ("f", 4, 0), ("r", 1, 1, 3, 0), ("g", 1, 1, 3, 0), ("g", 0, 0, 3, 0), ("f", 5, 0),
    ("g", 0, 1, 3, 0), ("f", 3, 0), ("x", 1, 3, 0), ("f", 6, 0), ("f", 2, 0), ("g", 1, 1, 3, 1), ("g", 0, 0, 3, 1),
    ("r", 0, 1, 3, 0), ("r", 1, 0, 4, 0), ("g", 1, 1, 4, 0), ("g", 1, 0, 3, 1), ("g", 0, 0, 4, 0), ("x", 1, 1, 0),
    ("x", 1, 1, 1), ("r", 0, 0, 3, 0), ("r", 1, 1, 2, 0), ("g", 0, 0, 4, 1), ("x", 1, 2, 0), ("r", 1, 0, 3, 0),
    ("x", 1, 2, 1), ("x", 0, 1, 1), ("g", 0, 1, 3, 1), ("f", 7, 0), ("f", 0, 0), ("r", 0, 1, 2, 0), ("f", 1, 0),
    ("r", 0, 0, 2, 0), ("g", 1, 1, 4, 1), ("x", 0, 3, 0), ("x", 0, 2, 0), ("x", 0, 4, 0), ("r", 1, 0, 2, 0),
    ("x", 0, 2, 1), ("x", 0, 3, 1), ("v",), ("x", 0, 4, 1), ("r", 1, 1, 1, 0), ("x", 1, 3, 1), ("r", 0, 1, 1, 0),
    ("r", 0, 0, 1, 0), ("r", 1, 0, 1, 0), ("w",), ("d", 7), ("d", 1), ("d", 4), ("d", 3), ("d", 6), ("d", 5),
    ("d", 0), ("d", 2), ("b", 3), ("b", 2), ("b", 0), ("u", 1, 0), ("b", 1), ("o", 2), ("u", 0, 0), ("e",),
    ("o", 1), ("o", 0), ("h", 1, 0), ("h", 0, 0), ("z",), ("i", 3), ("i", 2), ("i", 1), ("i", 0), ("y",),
)
PLAN = (256, 2, 192, 1, ORDER)


def ring_kernel(
    dp_size, tm_size, plan, width_g,
    valid_ref, gain_ref, bias_ref, clip_hbm, cot_hbm, weight_hbm,
    out_ref, input_grad_ref, weight_grad_ref,
    clip_ref, cot_ref, earlier, next_cot, full_weight, patches, turned, grads, mate_out, mate_in,
    fold_out, fold_in, edge_out, edge_in, middle_out, middle_in,
    last_edge, last_middle, share_out, share_in,
    held, wide, views, spread, sums_in, back_in,
    halo_send, halo_recv, sum_send, sum_recv, own_sem, load_sem,
    gather_send, gather_recv, cross_send, cross_recv, copy_send, copy_recv,
    mate_send, mate_recv, fold_send, fold_recv, ring_send, ring_recv,
    last_send, last_recv, share_send, share_recv,
):
    frames, half_rows, _, cols, channels = clip_ref.shape
    frames_out, half_cols, lanes = frames // 2, cols // 2, channels // 128
    area = half_rows * half_cols
    count = frames_out * area
    window, rows_all = grads.shape[1], full_weight.shape[1]
    rows_w = weight_hbm.shape[0]
    gather_edge, gather_cuts, edge, cuts, order = plan
    gather_middle, middle = rows_w - 2 * gather_edge, rows_w - 2 * edge
    dp, tm = lax.axis_index("dp"), lax.axis_index("tm")
    core, side = tm % 2, tm // 2
    mate = {"tm": tm + 1 - 2 * core}
    across = {"tm": (tm + 2) % tm_size}
    far_size, reach = dp_size // 2, dp_size // 2
    pos = dp // 2 + (dp % 2) * (2 * far_size - 1 - 2 * (dp // 2))

    def dp_at(place):
        place = (place + 2 * dp_size) % dp_size
        turn = place // far_size
        return 2 * (place + turn * (2 * far_size - 1 - 2 * place)) + turn

    onward = [{"dp": dp_at(pos + sign)} for sign in SIGN]
    pending = []

    def send(source, target, sem_out, sem_in, device):
        copy = pltpu.make_async_remote_copy(
            src_ref=source, dst_ref=target, send_sem=sem_out, recv_sem=sem_in,
            device_id=device, device_id_type=MESH,
        )
        copy.start()
        pending.append(copy)
        return copy

    barrier = pltpu.get_barrier_semaphore()
    greeted = [{"tm": (tm + step) % tm_size} for step in range(1, tm_size)] + onward
    for device in greeted:
        pl.semaphore_signal(barrier, inc=1, device_id=device, device_id_type=MESH)

    half_lane = pl.ds(pl.multiple_of(core * 128, 128), 128)
    other_lane = pl.ds(pl.multiple_of((1 - core) * 128, 128), 128)

    def planes(edge, middle):
        return side * (edge + middle), (1 - side) * (edge + middle)

    gather_at, gather_other = planes(gather_edge, gather_middle)
    gather_spans = ((gather_at, gather_edge), (gather_edge, gather_middle))

    def piece_of(start, size, cuts, cut):
        return start + cut * (size // cuts), size // cuts

    def rows_at(block, start, size):
        return pl.ds(pl.multiple_of(block * rows_w + start, 16), size)

    def region(block, start, size):
        return full_weight.at[core, rows_at(block, start, size)]

    gather_last = ((reach, reach - 1), (reach - 1, reach))
    gathers, crosses, mates = {}, {}, []

    def gather(way, kind, step, cut):
        start, size = piece_of(*gather_spans[kind], gather_cuts, cut)
        target = region(dp_at(pos - SIGN[way] * (step - 1)), start, size)
        at = (way, kind, step - 1, cut)
        gathers[way, kind, step, cut] = send(target, target, gather_send.at[at], gather_recv.at[at], onward[way])

    def to_mate(way, third, step, start, size):
        block = region(dp_at(pos - SIGN[way] * step), start, size)
        at = (way, third, step - 1)
        mates.append(send(block, block, copy_send.at[at], copy_recv.at[at], mate))

    def gathered(way, kind, step, cut):
        gathers[way, kind, step, cut].wait_recv()
        if step < gather_last[way][kind]:
            gather(way, kind, step + 1, cut)
        if kind == EDGE:
            start, size = piece_of(*gather_spans[kind], gather_cuts, cut)
            block = region(dp_at(pos - SIGN[way] * step), start, size)
            at = (way, step - 1, cut)
            crosses[way, step, cut] = send(block, block, cross_send.at[at], cross_recv.at[at], across)
        if cut == gather_cuts - 1:
            to_mate(way, kind, step, *gather_spans[kind])

    def crossed(way, step, cut):
        crosses[way, step, cut].wait_recv()
        if cut == gather_cuts - 1:
            to_mate(way, 2, step, gather_other, gather_edge)

    first = tm * frames
    valid = valid_ref[0]
    gain, bias = gain_ref[...], bias_ref[...]
    entries = jnp.full((1, channels), valid.astype(jnp.float32)) * float(2 * half_rows * cols * width_g)
    zero = jnp.zeros((8, channels), jnp.float32)

    def fold(value):
        return jnp.sum(value.reshape(-1, 8, channels), axis=0)

    def frame_mask(frame):
        slot = first + frame
        return jnp.where((slot >= 0) & (slot < valid), 1.0, 0.0).astype(jnp.float32)

    def moment_rows(index, sums):
        frame, row = index // half_rows, index % half_rows
        values = clip_ref[frame, row].astype(jnp.float32)
        masked = values * frame_mask(frame)
        return sums[0] + fold(masked), sums[1] + fold(masked * values)

    def exchange(sums, buffer, sems):
        pair = [jnp.sum(value, axis=0, keepdims=True) for value in sums]
        buffer[tm] = jnp.concatenate(pair + [jnp.zeros((6, channels), jnp.float32)], axis=0)
        copies = [
            send(buffer.at[tm], buffer.at[tm], sum_send.at[sems, step], sum_recv.at[sems, step],
                 {"tm": (tm + step) % tm_size})
            for step in range(1, tm_size)
        ]

        def finish():
            for copy in copies:
                copy.wait_recv()
            total = buffer[0]
            for index in range(1, tm_size):
                total = total + buffer[index]
            return lane_group_sum(total, width_g)

        return finish

    state = {}
    own_loads = [
        pltpu.make_async_copy(
            weight_hbm.at[:, half * 128 : (half + 1) * 128], full_weight.at[half, rows_at(dp, 0, rows_w)],
            own_sem.at[half],
        )
        for half in range(2)
    ]
    clip_loads = [
        pltpu.make_async_copy(clip_hbm.at[frame], clip_ref.at[frame], load_sem.at[frame]) for frame in range(frames)
    ]
    cot_load = pltpu.make_async_copy(cot_hbm, cot_ref, load_sem.at[frames])
    for copy in clip_loads + own_loads + [cot_load]:
        copy.start()

    def begin():
        for kind in (EDGE, MIDDLE):
            for cut in range(gather_cuts):
                for way in (UP, DOWN):
                    gather(way, kind, 1, cut)

    def moments():
        sums = (zero, zero)
        for frame in range(frames):
            clip_loads[frame].wait()
            sums = lax.fori_loop(
                0, half_rows, lambda step, sums: moment_rows(frame * half_rows + step, sums), sums, unroll=4
            )
        pl.semaphore_wait(barrier, len(greeted))
        state["finish"] = exchange(sums, sums_in, 0)
        for copy in own_loads:
            copy.wait()
        begin()
        cot_load.wait()
        state["halos"] = [
            send(clip_ref.at[frames - 2 : frames], earlier, halo_send.at[0], halo_recv.at[0],
                 {"tm": (tm + 1) % tm_size}),
            send(cot_ref.at[0:area], next_cot, halo_send.at[1], halo_recv.at[1],
                 {"tm": (tm + tm_size - 1) % tm_size}),
        ]
        held[...] = jnp.zeros_like(held)
        turned[:, 0:128] = cot_ref[:, half_lane]
        turned[:, 128:256] = cot_ref[:, other_lane]
        patches[:, rows_all:] = jnp.zeros((count, patches.shape[1] - rows_all), jnp.bfloat16)

    def statistics():
        total = state["finish"]()
        mean = total[0:1] / entries
        inv_std = lax.rsqrt(total[1:2] / entries - mean * mean + EPS)
        state["norm"] = mean, inv_std

    def halo_once(index):
        if index not in state:
            state[index] = True
            state["halos"][index].wait_recv()

    def patch(turn):
        frame = (turn + 2) % (frames + 1)
        if frame < 2:
            halo_once(0)
        mean, inv_std = state["norm"]
        source = earlier.at[frame] if frame < 2 else clip_ref.at[frame - 2]
        mask = frame_mask(frame - 2)

        def rows(index, _):
            values = source[index].astype(jnp.float32)
            preact = (values - mean) * inv_std * gain + bias
            hidden = preact / (1.0 + jnp.exp(-preact)) * mask
            for lane in range(lanes):
                part = hidden[:, :, lane * 128 : (lane + 1) * 128]
                held[lane, index, 1, 8 : 8 + cols, :] = part[0]
                held[lane, index + 1, 0, 8 : 8 + cols, :] = part[1]
            return 0

        lax.fori_loop(0, half_rows, rows, 0, unroll=4)
        for step_r in range(3):
            for step_c in range(3):
                pieces = [
                    held[
                        lane,
                        step_r // 2 : step_r // 2 + half_rows,
                        step_r % 2,
                        pl.ds(7 + step_c, half_cols, 2),
                        :,
                    ].reshape(area, 128)
                    for lane in range(lanes)
                ]
                piece = jnp.concatenate(pieces, axis=1).astype(jnp.bfloat16)
                for step_t in range(3):
                    if (frame - step_t) % 2 == 0 and 0 <= frame - step_t < frames:
                        at = (frame - step_t) // 2
                        tap = 9 * step_t + 3 * step_r + step_c
                        patches[at * area : (at + 1) * area, tap * channels : (tap + 1) * channels] = piece

    offsets = [reach]
    for step in range(reach - 1, 0, -1):
        offsets += [-step, step]
    offsets.append(0)
    slot_of = {offset % dp_size: slot for slot, offset in enumerate(offsets)}
    swaps = {}

    def skew_of(offset):
        return dp_at(pos + offset) * rows_w % 128

    def taps(slot):
        skew = skew_of(offsets[slot])
        start = pl.multiple_of(dp_at(pos + offsets[slot]) * rows_w - skew, 128)
        value = lax.dot_general(
            patches[:, pl.ds(start, window)],
            turned[...],
            (((0,), (0,)), ((), ())),
            preferred_element_type=jnp.float32,
        )
        grads[slot] = value[:, 0:128]
        mate_out[slot] = value[:, 128:256].astype(jnp.bfloat16)
        span = pl.ds(pl.multiple_of(skew, 32), rows_w)
        swaps[slot] = send(
            mate_out.at[slot, span], mate_in.at[slot, span], mate_send.at[slot], mate_recv.at[slot], mate
        )

    edge_at, other_at = planes(edge, middle)
    spans = ((edge_at, edge), (edge, middle))

    def base(offset, start, size):
        slot = slot_of[offset % dp_size]
        if ("swap", slot) not in state:
            state["swap", slot] = True
            swaps[slot].wait_recv()
        span = pl.ds(pl.multiple_of(skew_of(offset) + start, 16), size)
        return grads[slot, span, :] + mate_in[slot, span, :].astype(jnp.float32)

    rings, folds = {}, {}
    ring_last = ((reach - 1, reach), (reach, reach - 1))
    ring_out, ring_in = (edge_out, middle_out), (edge_in, middle_in)

    def fold_over(index, cut):
        at = (index, cut)
        fold_out[at] = base(index, *piece_of(other_at, edge, cuts, cut)).astype(jnp.bfloat16)
        folds[at] = send(fold_out.at[at], fold_in.at[at], fold_send.at[at], fold_recv.at[at], across)

    def gathered_sum(offset, kind, cut):
        value = base(offset, *piece_of(*spans[kind], cuts, cut))
        if kind == EDGE:
            at = (offset % dp_size, cut)
            folds[at].wait_recv()
            value = value + fold_in[at].astype(jnp.float32)
        return value

    def gradient(way, kind, step, cut):
        value = gathered_sum(SIGN[way] * step, kind, cut)
        if step < ring_last[way][kind]:
            rings[way, kind, step + 1, cut].wait_recv()
            value = value + ring_in[kind][way, step, cut].astype(jnp.float32)
        at, sem = (way, step - 1, cut), (way, kind, step - 1, cut)
        ring_out[kind][at] = value.astype(jnp.bfloat16)
        rings[way, kind, step, cut] = send(
            ring_out[kind].at[at], ring_in[kind].at[at], ring_send.at[sem], ring_recv.at[sem], onward[way]
        )

    lasts, shares = {}, []
    last_of = (last_edge, last_middle)

    def share(third, start, size, cut, value):
        start, size = piece_of(start, size, cuts, cut)
        span = pl.ds(pl.multiple_of(start, 16), size)
        share_out[span, :] = value
        at = (third, cut)
        shares.append(send(share_out.at[span], share_in.at[span], share_send.at[at], share_recv.at[at], mate))

    def summed(kind, cut):
        value = gathered_sum(0, kind, cut)
        for way in (UP, DOWN):
            rings[way, kind, 1, cut].wait_recv()
            value = value + ring_in[kind][way, 0, cut].astype(jnp.float32)
        last = last_of[kind]
        last[0, cut] = value.astype(jnp.bfloat16)
        at = (kind, cut)
        lasts[at] = send(last.at[0, cut], last.at[1, cut], last_send.at[at], last_recv.at[at], across)
        if kind == EDGE:
            share(0, edge_at, edge, cut, last[0, cut].astype(jnp.float32))

    def shared(kind, cut):
        lasts[kind, cut].wait_recv()
        value = last_of[kind][1, cut].astype(jnp.float32)
        if kind == EDGE:
            share(1, other_at, edge, cut, value)
        else:
            share(2, edge, middle, cut, last_of[kind][0, cut].astype(jnp.float32) + value)

    def cotangent_views():
        halo_once(1)
        wide[...] = jnp.zeros_like(wide)
        inner = jnp.where(tm < tm_size - 1, 1.0, 0.0).astype(jnp.float32)
        for frame in range(frames_out + 1):
            if frame < frames_out:
                piece = cot_ref[frame * area : (frame + 1) * area, :].astype(jnp.float32)
            else:
                piece = next_cot[...].astype(jnp.float32) * inner
            wide[frame, 0:half_rows, 0:half_cols, :] = piece.reshape(half_rows, half_cols, channels)
        for dt in range(2):
            for dr in range(2):
                for dc in range(2):
                    piece = wide[dt : dt + frames_out, dr : dr + half_rows, dc : dc + half_cols, :]
                    views[4 * dt + 2 * dr + dc] = piece.reshape(count, channels).astype(jnp.bfloat16)

    def weights():
        for copy in mates:
            copy.wait_recv()

    def weight_rows(start, size):
        return jnp.concatenate([full_weight[half, start : start + size, :] for half in range(2)], axis=1)

    times = (((2, 0), (0, 1)), ((1, 1),))
    spaces = (((1, 0),), ((2, 0), (0, 1)))

    def hidden_part(part):
        part_t, part_r, part_c = part // 4, part // 2 % 2, part % 2
        total = jnp.zeros((count, channels), jnp.float32)
        for step_t, dt in times[part_t]:
            for step_r, dr in spaces[part_r]:
                for step_c, dc in spaces[part_c]:
                    tap = 9 * step_t + 3 * step_r + step_c
                    total += lax.dot_general(
                        views[4 * dt + 2 * dr + dc],
                        weight_rows(tap * channels, channels),
                        (((1,), (1,)), ((), ())),
                        preferred_element_type=jnp.float32,
                    )
        total = total.reshape(frames_out, half_rows, half_cols, channels)
        for frame in range(frames_out):
            for lane in range(lanes):
                spread[
                    lane, 2 * frame + part_t, :, part_r, pl.ds(part_c, half_cols, 2), :
                ] = total[frame, :, :, lane * 128 : (lane + 1) * 128]

    quarter = frames * half_rows // 4

    def back(part):
        mean, inv_std = state["norm"]

        def back_rows(index, sums):
            frame, row = index // half_rows, index % half_rows
            normed = (clip_ref[frame, row].astype(jnp.float32) - mean) * inv_std
            preact = normed * gain + bias
            sig = 1.0 / (1.0 + jnp.exp(-preact))
            slope = sig * (1.0 + preact * (1.0 - sig))
            hidden_grad = jnp.concatenate([spread[lane, frame, row] for lane in range(lanes)], axis=-1)
            value = hidden_grad * frame_mask(frame) * slope * gain
            for lane in range(lanes):
                spread[lane, frame, row] = value[:, :, lane * 128 : (lane + 1) * 128]
            return sums[0] + fold(value), sums[1] + fold(value * normed)

        sums = state.get("sums", (zero, zero))
        state["sums"] = lax.fori_loop(
            0, quarter, lambda step, sums: back_rows(part * quarter + step, sums), sums, unroll=4
        )

    def back_exchange():
        state["finish"] = exchange(state["sums"], back_in, 1)

    deep = 9 * channels

    def output_part(step):
        total = state.get("total", jnp.zeros((count, channels), jnp.float32))
        total += jnp.dot(
            patches[:, step * deep : (step + 1) * deep],
            weight_rows(step * deep, deep),
            preferred_element_type=jnp.float32,
        )
        state["total"] = total
        state["outs"] = state.get("outs", 0) + 1
        if state["outs"] == 3:
            out_ref[...] = total.astype(jnp.bfloat16)

    def back_finish():
        total = state["finish"]()
        state["back"] = total[0:1] / entries, total[1:2] / entries

    def input_part(part):
        mean, inv_std = state["norm"]
        back_first, back_second = state["back"]

        def input_rows(index, _):
            frame, row = index // half_rows, index % half_rows
            normed = (clip_ref[frame, row].astype(jnp.float32) - mean) * inv_std
            value = jnp.concatenate([spread[lane, frame, row] for lane in range(lanes)], axis=-1)
            input_grad_ref[frame, row] = (
                frame_mask(frame) * inv_std * (value - back_first - normed * back_second)
            ).astype(jnp.bfloat16)
            return 0

        lax.fori_loop(0, quarter, lambda step, _: input_rows(part * quarter + step, 0), 0, unroll=4)

    def result():
        for copy in shares:
            copy.wait_recv()
        weight_grad_ref[:, half_lane] = share_out[...]
        weight_grad_ref[:, other_lane] = share_in[...]

    steps = {
        "m": moments, "s": statistics, "p": patch, "t": taps, "g": gathered, "x": crossed, "f": fold_over,
        "r": gradient, "u": summed, "h": shared, "v": cotangent_views, "w": weights, "d": hidden_part,
        "b": back, "e": back_exchange, "o": output_part, "z": back_finish, "i": input_part, "y": result,
    }
    for name, *where in order:
        steps[name](*where)
    for copy in pending:
        copy.wait_send()


def ring_shards(dp_size, tm_size, clips, frame_counts, weight, gain, bias, cotangent):
    clip_data, cot_block = clips[0], cotangent[0]
    frame_count, row_count, col_count, channels = clip_data.shape
    frames_out, rows_out, cols_out = cot_block.shape[:3]
    area = rows_out * cols_out
    count = frames_out * area
    split = (frame_count, row_count // 2, 2, col_count, channels)
    rows_w = weight.shape[0]
    rows = dp_size * rows_w
    lanes = channels // 128
    gather_edge, gather_cuts, edge, cuts, _ = PLAN
    middle = rows_w - 2 * edge
    reach = dp_size // 2
    window = (rows_w + 96 + 127) // 128 * 128
    dma = pltpu.SemaphoreType.DMA
    f32, bf16 = jnp.float32, jnp.bfloat16
    pairs = [
        (2, 2, reach, gather_cuts), (2, reach, gather_cuts), (2, 3, reach), (dp_size,), (dp_size, cuts),
        (2, 2, reach, cuts), (2, cuts), (3, cuts),
    ]
    output, input_grad, weight_grad = pl.pallas_call(
        functools.partial(ring_kernel, dp_size, tm_size, PLAN, channels // GROUPS),
        out_shape=(
            pltpu.VMEM((count, channels), bf16),
            pltpu.VMEM(split, bf16),
            pltpu.VMEM((rows_w, channels), f32),
        ),
        in_specs=[SMEM] + [VMEM] * 2 + [HBM] * 3,
        out_specs=(VMEM, VMEM, VMEM),
        scratch_shapes=[
            pltpu.VMEM(split, bf16),
            pltpu.VMEM((count, channels), bf16),
            pltpu.VMEM((2,) + split[1:], bf16),
            pltpu.VMEM((area, channels), bf16),
            pltpu.VMEM((2, rows, 128), bf16),
            pltpu.VMEM((count, rows + 128), bf16),
            pltpu.VMEM((count, channels), bf16),
            pltpu.VMEM((dp_size, window, 128), f32),
            pltpu.VMEM((dp_size, window, 128), bf16),
            pltpu.VMEM((dp_size, window, 128), bf16),
            pltpu.VMEM((dp_size, cuts, edge // cuts, 128), bf16),
            pltpu.VMEM((dp_size, cuts, edge // cuts, 128), bf16),
            pltpu.VMEM((2, reach, cuts, edge // cuts, 128), bf16),
            pltpu.VMEM((2, reach, cuts, edge // cuts, 128), bf16),
            pltpu.VMEM((2, reach, cuts, middle // cuts, 128), bf16),
            pltpu.VMEM((2, reach, cuts, middle // cuts, 128), bf16),
            pltpu.VMEM((2, cuts, edge // cuts, 128), bf16),
            pltpu.VMEM((2, cuts, middle // cuts, 128), bf16),
            pltpu.VMEM((rows_w, 128), f32),
            pltpu.VMEM((rows_w, 128), f32),
            pltpu.VMEM((lanes, rows_out + 1, 2, col_count + 8, 128), f32),
            pltpu.VMEM((frames_out + 1, rows_out + 1, 16, channels), f32),
            pltpu.VMEM((8, count, channels), bf16),
            pltpu.VMEM((lanes,) + split[:-1] + (128,), f32),
            pltpu.VMEM((tm_size, 8, channels), f32),
            pltpu.VMEM((tm_size, 8, channels), f32),
        ]
        + [dma((2,))] * 2
        + [dma((2, tm_size))] * 2
        + [dma((2,)), dma((frame_count + 1,))]
        + [dma(shape) for shape in pairs for _ in range(2)],
        compiler_params=pltpu.CompilerParams(
            collective_id=0, has_side_effects=True, vmem_limit_bytes=RING_VMEM
        ),
    )(frame_counts, gain[None], bias[None], clip_data.reshape(split), cot_block.reshape(count, channels), weight)
    output, input_grad, weight_grad = settled(output, input_grad, weight_grad)
    return (
        output.reshape(cot_block.shape)[None],
        input_grad.reshape(clip_data.shape)[None],
        weight_grad,
    )


def copy_kernel(*refs):
    count = len(refs) // 2
    sems = refs[-1]
    copies = []
    for index in range(count):
        size = refs[index].shape[0] // COPY_PARTS
        for part in range(COPY_PARTS):
            span = pl.ds(part * size, size)
            copies.append(
                pltpu.make_async_copy(refs[index].at[span], refs[count + index].at[span], sems.at[len(copies)])
            )
            copies[-1].start()
    for copy in copies:
        copy.wait()


def settled(*arrays):
    sems = pltpu.SemaphoreType.DMA((COPY_PARTS * len(arrays),))
    return pl.pallas_call(
        copy_kernel,
        out_shape=tuple(jax.ShapeDtypeStruct(array.shape, array.dtype) for array in arrays),
        in_specs=[VMEM] * len(arrays),
        out_specs=(HBM,) * len(arrays),
        scratch_shapes=[sems],
        compiler_params=pltpu.CompilerParams(vmem_limit_bytes=COPY_VMEM),
    )(*arrays)


def by_ring(dp_size, tm_size, weight_rows):
    return dp_size == 8 and tm_size == 4 and weight_rows == 864


def device_part(dp_size, tm_size, *arrays):
    chosen = ring_shards if by_ring(dp_size, tm_size, arrays[2].shape[0]) else shards
    return chosen(dp_size, tm_size, *arrays)


def solution(mesh):
    placed = (
        P("dp", "tm", None, None, None),
        P("dp"),
        P("dp", None),
        P(),
        P(),
        P("dp", "tm", None, None, None),
    )
    return jax.shard_map(
        functools.partial(device_part, mesh.shape["dp"], mesh.shape["tm"]),
        mesh=mesh,
        in_specs=placed,
        out_specs=(P("dp", "tm", None, None, None), P("dp", "tm", None, None, None), P("dp", None)),
        check_vma=False,
    )
```

```python
import functools

import jax
import jax.numpy as jnp
from jax import lax
from jax.experimental import pallas as pl
from jax.experimental.pallas import tpu as pltpu
from jax.sharding import PartitionSpec as P

GROUPS = 32
EPS = 1e-06
PARTS = 3
MESH = pl.DeviceIdType.MESH
VMEM = pl.BlockSpec(memory_space=pltpu.VMEM)
SMEM = pl.BlockSpec(memory_space=pltpu.SMEM)


def plan(dp_size, tm_size):
    dp_bits = [("dp", k) for k in range(dp_size.bit_length() - 1)]
    tm_bits = [("tm", k) for k in range(tm_size.bit_length() - 1)]
    cut = len(dp_bits) // 2
    ways = [tm_bits[1:], dp_bits[:cut], dp_bits[cut:]]
    orders = []
    for part in range(PARTS):
        turned = ways[part:] + ways[:part]
        orders.append(tm_bits[:1] + turned[0] + turned[1] + turned[2])
    return dp_bits[::-1] + tm_bits[::-1], orders


def lane_group_sum(value, width):
    channels = value.shape[-1]
    lane = lax.broadcasted_iota(jnp.int32, value.shape, value.ndim - 1)
    step = 1
    while step < width:
        above = pltpu.roll(value, channels - step, value.ndim - 1)
        below = pltpu.roll(value, step, value.ndim - 1)
        value = value + jnp.where((lane // step) % 2 == 0, above, below)
        step *= 2
    return value


def block_kernel(
    labels, orders, dp_size, tm_size, near, width_g,
    valid_ref, params_ref, clip_ref, cot_ref, weight_ref,
    out_ref, input_grad_ref, weight_grad_ref,
    earlier, next_cot, full_weight, patches, grads, held, wide, views, spread, shared, sums_in, back_in,
    *scratch,
):
    frames, half_rows, _, cols, channels = clip_ref.shape
    frames_out, half_cols, lanes = frames // 2, cols // 2, channels // 128
    area = half_rows * half_cols
    count = frames_out * area
    depth = len(labels)
    sends, receives, kept = (scratch[i * depth : (i + 1) * depth] for i in range(3))
    (send_sem, recv_sem, share_send, share_recv, ring_send, ring_recv, sum_send, sum_recv,
     far_send, far_recv, near_send, near_recv, mate_send, mate_recv, cross_send, cross_recv, own_sem) = scratch[3 * depth :]
    dp, tm = lax.axis_index("dp"), lax.axis_index("tm")
    place = {"dp": dp, "tm": tm}
    far_size = dp_size // near
    far_at, near_at = dp // near, dp % near
    core = tm % 2
    mate = {"tm": tm + 1 - 2 * core}

    def bit_of(label):
        return (place[label[0]] // 2 ** label[1]) % 2

    def partner(label):
        return {label[0]: place[label[0]] + (1 - 2 * bit_of(label)) * 2 ** label[1]}

    def send(source, target, sem_out, sem_in, device):
        copy = pltpu.make_async_remote_copy(
            src_ref=source, dst_ref=target, send_sem=sem_out, recv_sem=sem_in,
            device_id=device, device_id_type=MESH,
        )
        copy.start()
        return copy

    barrier = pltpu.get_barrier_semaphore()
    greeted = [{"tm": (tm + step) % tm_size} for step in range(1, tm_size)]
    greeted += [{"dp": dp_index} for dp_index in dp_peers(dp, dp_size, near)]
    for device in greeted:
        pl.semaphore_signal(barrier, inc=1, device_id=device, device_id_type=MESH)
    pl.semaphore_wait(barrier, len(greeted))

    ring = [
        send(clip_ref.at[frames - 2 : frames], earlier, ring_send.at[0], ring_recv.at[0], {"tm": (tm + 1) % tm_size}),
        send(cot_ref.at[0:area], next_cot, ring_send.at[1], ring_recv.at[1], {"tm": (tm + tm_size - 1) % tm_size}),
    ]

    rows_w = weight_ref.shape[0]
    half_lane = pl.ds(pl.multiple_of(core * 128, 128), 128)

    crossed = tm_size == 4 and rows_w % 48 == 0
    rows_x = rows_w // 3 if crossed else 0
    span_w = rows_w - rows_x
    across = (tm // 2) % 2 if crossed else 0
    cross_mate = {"tm": (tm + 2) % tm_size}
    span_at = across * rows_x

    def rows_of(index, start, size):
        return full_weight.at[pl.ds(pl.multiple_of(index * rows_w + start, 8), size), half_lane]

    def block_at(index):
        return rows_of(index, span_at, span_w)

    own_copy = pltpu.make_async_copy(
        weight_ref, full_weight.at[pl.ds(pl.multiple_of(dp * rows_w, 8), rows_w), :], own_sem
    )
    own_copy.start()
    own_half = weight_ref.at[pl.ds(pl.multiple_of(span_at, 8), span_w), half_lane]
    far_copies = [
        send(own_half, block_at(dp), far_send.at[step], far_recv.at[step],
             {"dp": ((far_at + step) % far_size) * near + near_at})
        for step in range(1, far_size)
    ]
    near_copies, mate_copies, cross_copies = {}, [], []

    def send_near(step, source, index):
        for hop in range(1, near):
            near_copies[step, hop] = send(
                source, block_at(index), near_send.at[step, hop], near_recv.at[step, hop],
                {"dp": far_at * near + (near_at + hop) % near},
            )

    def send_mate(step, hop, index):
        if crossed:
            cross = rows_of(index, across * (span_w), rows_x)
            copy = send(cross, cross, cross_send.at[step, hop], cross_recv.at[step, hop], cross_mate)
            cross_copies.append((copy, step, hop, index))
        mate_copies.append(
            send(block_at(index), block_at(index), mate_send.at[0, step, hop], mate_recv.at[0, step, hop], mate)
        )

    def weight_cross():
        for copy, step, hop, index in cross_copies:
            copy.wait_recv()
            rest = rows_of(index, (1 - across) * span_w, rows_x)
            mate_copies.append(
                send(rest, rest, mate_send.at[1, step, hop], mate_recv.at[1, step, hop], mate)
            )

    send_near(0, own_half, dp)

    def weight_far(step):
        far_copies[step - 1].wait_recv()
        index = ((far_at + far_size - step) % far_size) * near + near_at
        send_near(step, block_at(index), index)
        send_mate(step, 0, index)

    def weight_near(step):
        for hop in range(1, near):
            near_copies[step, hop].wait_recv()
            index = ((far_at + far_size - step) % far_size) * near + (near_at + near - hop) % near
            send_mate(step, hop, index)

    first = tm * frames
    valid = valid_ref[0]
    gain, bias = params_ref[0:1, :], params_ref[1:2, :]
    entries = jnp.full((1, channels), valid.astype(jnp.float32)) * float(2 * half_rows * cols * width_g)
    zero = jnp.zeros((8, channels), jnp.float32)

    def fold(value):
        return jnp.sum(value.reshape(-1, 8, channels), axis=0)

    def frame_mask(frame):
        slot = first + frame
        return jnp.where((slot >= 0) & (slot < valid), 1.0, 0.0).astype(jnp.float32)

    def moment_rows(index, sums):
        frame, row = index // half_rows, index % half_rows
        values = clip_ref[frame, row].astype(jnp.float32)
        masked = values * frame_mask(frame)
        return sums[0] + fold(masked), sums[1] + fold(masked * values)

    def exchange(sums, buffer, sems):
        pair = [jnp.sum(value, axis=0, keepdims=True) for value in sums]
        buffer[tm] = jnp.concatenate(pair + [jnp.zeros((6, channels), jnp.float32)], axis=0)
        copies = [
            send(buffer.at[tm], buffer.at[tm], sum_send.at[sems, step], sum_recv.at[sems, step],
                 {"tm": (tm + step) % tm_size})
            for step in range(1, tm_size)
        ]

        def finish():
            for copy in copies:
                copy.wait()
            total = buffer[0]
            for index in range(1, tm_size):
                total = total + buffer[index]
            return lane_group_sum(total, width_g)

        return finish

    finish = exchange(lax.fori_loop(0, frames * half_rows, moment_rows, (zero, zero), unroll=4), sums_in, 0)
    held[...] = jnp.zeros_like(held)
    total = finish()
    mean = total[0:1] / entries
    inv_std = lax.rsqrt(total[1:2] / entries - mean * mean + EPS)
    for copy in ring:
        copy.wait()

    ticks = [functools.partial(weight_far, step) for step in range(1, far_size)]
    for frame in range(frames + 1):
        source = earlier.at[frame] if frame < 2 else clip_ref.at[frame - 2]
        mask = frame_mask(frame - 2)

        def rows(index, _):
            values = source[index].astype(jnp.float32)
            preact = (values - mean) * inv_std * gain + bias
            hidden = preact / (1.0 + jnp.exp(-preact)) * mask
            for lane in range(lanes):
                part = hidden[:, :, lane * 128 : (lane + 1) * 128]
                held[lane, index, 1, 8 : 8 + cols, :] = part[0]
                held[lane, index + 1, 0, 8 : 8 + cols, :] = part[1]
            return 0

        lax.fori_loop(0, half_rows, rows, 0, unroll=4)
        for step_r in range(3):
            for step_c in range(3):
                pieces = [
                    held[
                        lane,
                        step_r // 2 : step_r // 2 + half_rows,
                        step_r % 2,
                        pl.ds(7 + step_c, half_cols, 2),
                        :,
                    ].reshape(area, 128)
                    for lane in range(lanes)
                ]
                piece = jnp.concatenate(pieces, axis=1).astype(jnp.bfloat16)
                for step_t in range(3):
                    if (frame - step_t) % 2 == 0 and 0 <= frame - step_t < frames:
                        at = (frame - step_t) // 2
                        tap = 9 * step_t + 3 * step_r + step_c
                        patches[at * area : (at + 1) * area, tap * channels : (tap + 1) * channels] = piece
        if frame % 3 == 2 and ticks:
            ticks.pop(0)()

    def tap_grad(tap, _):
        at = pl.multiple_of(tap * channels, channels)
        grads[pl.ds(at, channels), :] = lax.dot_general(
            patches[:, pl.ds(at, channels)],
            cot_ref[...],
            (((0,), (0,)), ((), ())),
            preferred_element_type=jnp.float32,
        )
        return 0

    for tick in ticks:
        tick()
    weight_near(0)
    lax.fori_loop(0, 27, tap_grad, 0)

    left = [list(labels) for _ in range(PARTS)]
    copies = [[None] * depth for _ in range(PARTS)]
    piece_rows = grads.shape[0] // (dp_size * tm_size * PARTS)

    def index_of(stride, number, bit):
        return (number // stride) * (2 * stride) + bit * stride + number % stride

    def read(stage, part, index):
        if stage == 0:
            at = (index * PARTS + part) * piece_rows
            if piece_rows % 8 == 0:
                return grads[pl.ds(pl.multiple_of(at, 8), piece_rows), :]
            window = (piece_rows + 14) // 8 * 8
            block = grads[pl.ds(pl.multiple_of(at // 8 * 8, 8), window), :]
            return pltpu.roll(block, (window - at % 8) % window, 0)[:piece_rows]
        return kept[stage - 1][part, index]

    def add(stage, part):
        label = orders[part][stage]
        stride = 2 ** (len(left[part]) - 1 - left[part].index(label))
        number = 2 ** (len(left[part]) - 1)
        copies[part][stage].wait_recv()

        def one(block, _):
            kept[stage][part, block] = read(
                stage, part, index_of(stride, block, bit_of(label))
            ) + receives[stage][part, block].astype(jnp.float32)
            return 0

        lax.fori_loop(0, number, one, 0)
        left[part].remove(label)

    def halve(stage):
        for part in range(PARTS):
            if stage > 0:
                add(stage - 1, part)
            label = orders[part][stage]
            stride = 2 ** (len(left[part]) - 1 - left[part].index(label))
            number = 2 ** (len(left[part]) - 1)

            def pack(block, _):
                sends[stage][part, block] = read(
                    stage, part, index_of(stride, block, 1 - bit_of(label))
                ).astype(jnp.bfloat16)
                return 0

            lax.fori_loop(0, number, pack, 0)
            copies[part][stage] = send(
                sends[stage].at[part], receives[stage].at[part],
                send_sem.at[part, stage], recv_sem.at[part, stage], partner(label),
            )

    halve(0)
    for step in range(1, far_size):
        weight_near(step)
    halve(1)
    weight_cross()
    for copy in mate_copies:
        copy.wait_recv()
    own_copy.wait()
    total = jnp.zeros((count, channels), jnp.float32)
    deep = 9 * channels
    for step in range(3):
        total += jnp.dot(
            patches[:, step * deep : (step + 1) * deep],
            full_weight[step * deep : (step + 1) * deep, :],
            preferred_element_type=jnp.float32,
        )
    out_ref[...] = total.astype(jnp.bfloat16)
    wide[...] = jnp.zeros_like(wide)
    last = jnp.where(tm < tm_size - 1, 1.0, 0.0).astype(jnp.float32)
    for frame in range(frames_out + 1):
        if frame < frames_out:
            piece = cot_ref[frame * area : (frame + 1) * area, :].astype(jnp.float32)
        else:
            piece = next_cot[...].astype(jnp.float32) * last
        wide[frame, 0:half_rows, 0:half_cols, :] = piece.reshape(half_rows, half_cols, channels)
    for dt in range(2):
        for dr in range(2):
            for dc in range(2):
                piece = wide[dt : dt + frames_out, dr : dr + half_rows, dc : dc + half_cols, :]
                views[4 * dt + 2 * dr + dc] = piece.reshape(count, channels).astype(jnp.bfloat16)
    times = (((2, 0), (0, 1)), ((1, 1),))
    spaces = (((1, 0),), ((2, 0), (0, 1)))
    stage = 2
    for part_t in range(2):
        for part_r in range(2):
            for part_c in range(2):
                total = jnp.zeros((count, channels), jnp.float32)
                for step_t, dt in times[part_t]:
                    for step_r, dr in spaces[part_r]:
                        for step_c, dc in spaces[part_c]:
                            tap = 9 * step_t + 3 * step_r + step_c
                            total += lax.dot_general(
                                views[4 * dt + 2 * dr + dc],
                                full_weight[tap * channels : (tap + 1) * channels, :],
                                (((1,), (1,)), ((), ())),
                                preferred_element_type=jnp.float32,
                            )
                total = total.reshape(frames_out, half_rows, half_cols, channels)
                for frame in range(frames_out):
                    for lane in range(lanes):
                        spread[
                            lane, 2 * frame + part_t, :, part_r, pl.ds(part_c, half_cols, 2), :
                        ] = total[frame, :, :, lane * 128 : (lane + 1) * 128]
    halve(stage)

    def back_rows(index, sums):
        frame, row = index // half_rows, index % half_rows
        normed = (clip_ref[frame, row].astype(jnp.float32) - mean) * inv_std
        preact = normed * gain + bias
        sig = 1.0 / (1.0 + jnp.exp(-preact))
        slope = sig * (1.0 + preact * (1.0 - sig))
        hidden_grad = jnp.concatenate([spread[lane, frame, row] for lane in range(lanes)], axis=-1)
        value = hidden_grad * frame_mask(frame) * slope * gain
        for lane in range(lanes):
            spread[lane, frame, row] = value[:, :, lane * 128 : (lane + 1) * 128]
        return sums[0] + fold(value), sums[1] + fold(value * normed)

    finish = exchange(lax.fori_loop(0, frames * half_rows, back_rows, (zero, zero), unroll=4), back_in, 1)
    for stage in range(3, depth):
        halve(stage)
    for part in range(PARTS):
        add(depth - 1, part)
        shared[tm, part] = kept[depth - 1][part, 0].astype(jnp.bfloat16)

    tm_bits = [label for label in labels if label[0] == "tm"]
    shares, serial = [], 0
    for label in tm_bits:
        span = 2 ** (label[1] + 1)
        stage_shares = []
        for high in range(tm_size // span):
            block = high * span + tm % span
            stage_shares.append(
                send(shared.at[block], shared.at[block],
                     share_send.at[serial], share_recv.at[serial], partner(label))
            )
            serial += 1
        if label == tm_bits[0]:
            total = finish()
            back_first, back_second = total[0:1] / entries, total[1:2] / entries

            def input_rows(index, _):
                frame, row = index // half_rows, index % half_rows
                normed = (clip_ref[frame, row].astype(jnp.float32) - mean) * inv_std
                value = jnp.concatenate([spread[lane, frame, row] for lane in range(lanes)], axis=-1)
                input_grad_ref[frame, row] = (
                    frame_mask(frame) * inv_std * (value - back_first - normed * back_second)
                ).astype(jnp.bfloat16)
                return 0

            lax.fori_loop(0, frames * half_rows, input_rows, 0, unroll=4)
        for share in stage_shares:
            share.wait_recv()
        shares += stage_shares
    for block in range(tm_size):
        weight_grad_ref[block] = shared[block].astype(jnp.float32)
    for copy in shares + far_copies + list(near_copies.values()) + mate_copies + [item[0] for item in cross_copies]:
        copy.wait_send()
    for part in range(PARTS):
        for copy in copies[part]:
            copy.wait_send()


def dp_peers(dp, dp_size, near):
    far_at, near_at, far_size = dp // near, dp % near, dp_size // near
    peers = [((far_at + step) % far_size) * near + near_at for step in range(1, far_size)]
    return peers + [far_at * near + (near_at + hop) % near for hop in range(1, near)]


def shards(dp_size, tm_size, clips, frame_counts, weight, gain, bias, cotangent):
    clip_data, cot_block = clips[0], cotangent[0]
    frame_count, row_count, col_count, channels = clip_data.shape
    frames_out, rows_out, cols_out = cot_block.shape[:3]
    area = rows_out * cols_out
    count = frames_out * area
    split = (frame_count, row_count // 2, 2, col_count, channels)
    labels, orders = plan(dp_size, tm_size)
    depth = len(labels)
    rows = dp_size * weight.shape[0]
    piece = rows // (dp_size * tm_size * PARTS)
    halves = [(PARTS, 2 ** (depth - 1 - stage), piece, channels) for stage in range(depth)]
    near = 2 ** ((dp_size.bit_length() - 1) // 2)
    far = dp_size // near
    lanes = channels // 128
    dma = pltpu.SemaphoreType.DMA
    f32, bf16 = jnp.float32, jnp.bfloat16
    output, input_grad, weight_grad = pl.pallas_call(
        functools.partial(block_kernel, labels, orders, dp_size, tm_size, near, channels // GROUPS),
        out_shape=(
            jax.ShapeDtypeStruct((count, channels), bf16),
            jax.ShapeDtypeStruct(split, bf16),
            jax.ShapeDtypeStruct((tm_size, PARTS, piece, channels), f32),
        ),
        in_specs=[SMEM] + [VMEM] * 4,
        out_specs=(VMEM, VMEM, VMEM),
        scratch_shapes=[
            pltpu.VMEM((2,) + split[1:], bf16),
            pltpu.VMEM((area, channels), bf16),
            pltpu.VMEM((rows, channels), bf16),
            pltpu.VMEM((count, rows), bf16),
            pltpu.VMEM((rows, channels), f32),
            pltpu.VMEM((lanes, rows_out + 1, 2, col_count + 8, 128), f32),
            pltpu.VMEM((frames_out + 1, rows_out + 1, 16, channels), f32),
            pltpu.VMEM((8, count, channels), bf16),
            pltpu.VMEM((lanes,) + split[:-1] + (128,), f32),
            pltpu.VMEM((tm_size, PARTS, piece, channels), bf16),
            pltpu.VMEM((tm_size, 8, channels), f32),
            pltpu.VMEM((tm_size, 8, channels), f32),
        ]
        + [pltpu.VMEM(shape, bf16) for shape in halves] * 2
        + [pltpu.VMEM(shape, f32) for shape in halves]
        + [dma((PARTS, depth))] * 2
        + [dma((tm_size,))] * 2
        + [dma((2,))] * 2
        + [dma((2, tm_size))] * 2
        + [dma((far,))] * 2
        + [dma((far, near))] * 2
        + [dma((2, far, near))] * 2
        + [dma((far, near))] * 2
        + [dma(())],
        compiler_params=pltpu.CompilerParams(
            collective_id=0, has_side_effects=True, vmem_limit_bytes=56 * 2**20
        ),
    )(frame_counts, jnp.stack([gain, bias]), clip_data.reshape(split), cot_block.reshape(count, channels), weight)
    return (
        output.reshape(cot_block.shape)[None],
        input_grad.reshape(clip_data.shape)[None],
        weight_grad.reshape(weight.shape),
    )


HBM = pl.BlockSpec(memory_space=pl.ANY)
UP, DOWN = 0, 1
EDGE, MIDDLE = 0, 1
SIGN = (1, -1)
COPY_PARTS = 2
RING_VMEM = 54 * 2**20
COPY_VMEM = 16 * 2**20
ORDER = (
    ("m",), ("s",), ("p", 0), ("p", 2), ("p", 4), ("p", 5), ("g", 1, 0, 1, 0), ("g", 0, 0, 1, 0), ("v",),
    ("g", 1, 0, 1, 1), ("p", 1), ("g", 0, 1, 1, 0), ("g", 1, 1, 1, 0), ("p", 6), ("g", 0, 1, 1, 1),
    ("g", 1, 1, 1, 1), ("g", 0, 0, 1, 1), ("p", 3), ("p", 7), ("p", 8), ("t", 0), ("t", 1), ("t", 2),
    ("g", 0, 0, 2, 0), ("g", 1, 0, 2, 0), ("t", 3), ("g", 0, 1, 2, 0), ("t", 4), ("g", 1, 0, 2, 1), ("t", 5),
    ("g", 1, 1, 2, 0), ("g", 0, 1, 2, 1), ("t", 6), ("t", 7), ("g", 1, 1, 2, 1), ("g", 0, 0, 2, 1),
    ("g", 1, 0, 3, 0), ("r", 0, 1, 4, 0), ("f", 4, 0), ("r", 1, 1, 3, 0), ("g", 0, 0, 3, 0), ("g", 0, 0, 3, 1),
    ("x", 0, 2, 0), ("f", 3, 0), ("x", 0, 1, 0), ("x", 1, 1, 0), ("f", 5, 0), ("g", 1, 0, 3, 1), ("g", 0, 1, 3, 0),
    ("g", 1, 1, 3, 0), ("x", 1, 2, 0), ("g", 0, 1, 3, 1), ("r", 1, 0, 4, 0), ("f", 2, 0), ("r", 0, 1, 3, 0),
    ("x", 0, 3, 0), ("g", 0, 0, 4, 0), ("g", 1, 1, 3, 1), ("x", 0, 1, 1), ("g", 0, 0, 4, 1), ("r", 0, 0, 3, 0),
    ("f", 6, 0), ("x", 1, 3, 0), ("g", 1, 1, 4, 0), ("r", 1, 0, 3, 0), ("x", 1, 2, 1), ("r", 1, 1, 2, 0),
    ("x", 0, 3, 1), ("r", 0, 1, 2, 0), ("x", 0, 2, 1), ("g", 1, 1, 4, 1), ("f", 1, 0), ("x", 0, 4, 0),
    ("x", 1, 3, 1), ("r", 0, 0, 2, 0), ("f", 7, 0), ("f", 0, 0), ("x", 1, 1, 1), ("x", 0, 4, 1), ("r", 1, 0, 2, 0),
    ("r", 1, 1, 1, 0), ("w",), ("r", 0, 1, 1, 0), ("d", 3), ("d", 2), ("d", 0), ("d", 4), ("d", 6),
    ("r", 0, 0, 1, 0), ("d", 7), ("r", 1, 0, 1, 0), ("d", 1), ("d", 5), ("b", 2), ("b", 1), ("b", 3), ("u", 1, 0),
    ("o", 2), ("b", 0), ("e",), ("u", 0, 0), ("o", 0), ("o", 1), ("h", 1, 0), ("z",), ("i", 1), ("h", 0, 0),
    ("i", 0), ("i", 3), ("i", 2), ("y",),
)
PLAN = (224, 2, 208, 1, ORDER)


def ring_kernel(
    dp_size, tm_size, plan, width_g,
    valid_ref, gain_ref, bias_ref, clip_hbm, cot_hbm, weight_hbm,
    out_ref, input_grad_ref, weight_grad_ref,
    clip_ref, cot_ref, out_sum, earlier, next_cot, full_weight, patches, turned, grads, mate_out, mate_in,
    fold_out, fold_in, edge_out, edge_in, middle_out, middle_in,
    last_edge, last_middle, share_out, share_in,
    held, wide, views, spread, sums_in, back_in,
    halo_send, halo_recv, sum_send, sum_recv, own_sem, load_sem,
    gather_send, gather_recv, cross_send, cross_recv, copy_send, copy_recv,
    mate_send, mate_recv, fold_send, fold_recv, ring_send, ring_recv,
    last_send, last_recv, share_send, share_recv,
):
    frames, half_rows, _, cols, channels = clip_ref.shape
    frames_out, half_cols, lanes = frames // 2, cols // 2, channels // 128
    area = half_rows * half_cols
    count = frames_out * area
    window, rows_all = grads.shape[1], full_weight.shape[1]
    rows_w = weight_hbm.shape[0]
    gather_edge, gather_cuts, edge, cuts, order = plan
    gather_middle, middle = rows_w - 2 * gather_edge, rows_w - 2 * edge
    dp, tm = lax.axis_index("dp"), lax.axis_index("tm")
    core, side = tm % 2, tm // 2
    mate = {"tm": tm + 1 - 2 * core}
    across = {"tm": (tm + 2) % tm_size}
    far_size, reach = dp_size // 2, dp_size // 2
    pos = dp // 2 + (dp % 2) * (2 * far_size - 1 - 2 * (dp // 2))

    def dp_at(place):
        place = (place + 2 * dp_size) % dp_size
        turn = place // far_size
        return 2 * (place + turn * (2 * far_size - 1 - 2 * place)) + turn

    onward = [{"dp": dp_at(pos + sign)} for sign in SIGN]
    pending = []

    def send(source, target, sem_out, sem_in, device):
        copy = pltpu.make_async_remote_copy(
            src_ref=source, dst_ref=target, send_sem=sem_out, recv_sem=sem_in,
            device_id=device, device_id_type=MESH,
        )
        copy.start()
        pending.append(copy)
        return copy

    barrier = pltpu.get_barrier_semaphore()
    greeted = [{"tm": (tm + step) % tm_size} for step in range(1, tm_size)] + onward
    for device in greeted:
        pl.semaphore_signal(barrier, inc=1, device_id=device, device_id_type=MESH)

    half_lane = pl.ds(pl.multiple_of(core * 128, 128), 128)
    other_lane = pl.ds(pl.multiple_of((1 - core) * 128, 128), 128)

    def planes(edge, middle):
        return side * (edge + middle), (1 - side) * (edge + middle)

    gather_at, gather_other = planes(gather_edge, gather_middle)
    gather_spans = ((gather_at, gather_edge), (gather_edge, gather_middle))

    def piece_of(start, size, cuts, cut):
        return start + cut * (size // cuts), size // cuts

    def rows_at(block, start, size):
        return pl.ds(pl.multiple_of(block * rows_w + start, 16), size)

    def region(block, start, size):
        return full_weight.at[core, rows_at(block, start, size)]

    gather_last = ((reach, reach - 1), (reach - 1, reach))
    gathers, crosses, mates = {}, {}, []

    def gather(way, kind, step, cut):
        start, size = piece_of(*gather_spans[kind], gather_cuts, cut)
        target = region(dp_at(pos - SIGN[way] * (step - 1)), start, size)
        at = (way, kind, step - 1, cut)
        gathers[way, kind, step, cut] = send(target, target, gather_send.at[at], gather_recv.at[at], onward[way])

    def to_mate(way, third, step, start, size):
        block = region(dp_at(pos - SIGN[way] * step), start, size)
        at = (way, third, step - 1)
        mates.append(send(block, block, copy_send.at[at], copy_recv.at[at], mate))

    def gathered(way, kind, step, cut):
        gathers[way, kind, step, cut].wait_recv()
        if step < gather_last[way][kind]:
            gather(way, kind, step + 1, cut)
        if kind == EDGE:
            start, size = piece_of(*gather_spans[kind], gather_cuts, cut)
            block = region(dp_at(pos - SIGN[way] * step), start, size)
            at = (way, step - 1, cut)
            crosses[way, step, cut] = send(block, block, cross_send.at[at], cross_recv.at[at], across)
        if cut == gather_cuts - 1:
            to_mate(way, kind, step, *gather_spans[kind])

    def crossed(way, step, cut):
        crosses[way, step, cut].wait_recv()
        if cut == gather_cuts - 1:
            to_mate(way, 2, step, gather_other, gather_edge)

    first = tm * frames
    valid = valid_ref[0]
    gain, bias = gain_ref[...], bias_ref[...]
    entries = jnp.full((1, channels), valid.astype(jnp.float32)) * float(2 * half_rows * cols * width_g)
    zero = jnp.zeros((8, channels), jnp.float32)

    def fold(value):
        return jnp.sum(value.reshape(-1, 8, channels), axis=0)

    def frame_mask(frame):
        slot = first + frame
        return jnp.where((slot >= 0) & (slot < valid), 1.0, 0.0).astype(jnp.float32)

    def moment_rows(index, sums):
        frame, row = index // half_rows, index % half_rows
        values = clip_ref[frame, row].astype(jnp.float32)
        masked = values * frame_mask(frame)
        return sums[0] + fold(masked), sums[1] + fold(masked * values)

    def exchange(sums, buffer, sems):
        pair = [jnp.sum(value, axis=0, keepdims=True) for value in sums]
        buffer[tm] = jnp.concatenate(pair + [jnp.zeros((6, channels), jnp.float32)], axis=0)
        copies = [
            send(buffer.at[tm], buffer.at[tm], sum_send.at[sems, step], sum_recv.at[sems, step],
                 {"tm": (tm + step) % tm_size})
            for step in range(1, tm_size)
        ]

        def finish():
            for copy in copies:
                copy.wait_recv()
            total = buffer[0]
            for index in range(1, tm_size):
                total = total + buffer[index]
            return lane_group_sum(total, width_g)

        return finish

    state = {}
    own_loads = [
        pltpu.make_async_copy(
            weight_hbm.at[:, half * 128 : (half + 1) * 128], full_weight.at[half, rows_at(dp, 0, rows_w)],
            own_sem.at[half],
        )
        for half in range(2)
    ]
    clip_loads = [
        pltpu.make_async_copy(clip_hbm.at[frame], clip_ref.at[frame], load_sem.at[frame]) for frame in range(frames)
    ]
    cot_load = pltpu.make_async_copy(cot_hbm, cot_ref, load_sem.at[frames])
    for copy in clip_loads + own_loads + [cot_load]:
        copy.start()

    def begin():
        for kind in (EDGE, MIDDLE):
            for cut in range(gather_cuts):
                for way in (UP, DOWN):
                    gather(way, kind, 1, cut)

    def moments():
        sums = (zero, zero)
        for frame in range(frames):
            clip_loads[frame].wait()
            sums = lax.fori_loop(
                0, half_rows, lambda step, sums: moment_rows(frame * half_rows + step, sums), sums, unroll=4
            )
        pl.semaphore_wait(barrier, len(greeted))
        state["finish"] = exchange(sums, sums_in, 0)
        for copy in own_loads:
            copy.wait()
        begin()
        cot_load.wait()
        state["halos"] = [
            send(clip_ref.at[frames - 2 : frames], earlier, halo_send.at[0], halo_recv.at[0],
                 {"tm": (tm + 1) % tm_size}),
            send(cot_ref.at[0:area], next_cot, halo_send.at[1], halo_recv.at[1],
                 {"tm": (tm + tm_size - 1) % tm_size}),
        ]
        held[...] = jnp.zeros_like(held)
        turned[:, 0:128] = cot_ref[:, half_lane]
        turned[:, 128:256] = cot_ref[:, other_lane]
        patches[:, rows_all:] = jnp.zeros((count, patches.shape[1] - rows_all), jnp.bfloat16)

    def statistics():
        total = state["finish"]()
        mean = total[0:1] / entries
        inv_std = lax.rsqrt(total[1:2] / entries - mean * mean + EPS)
        state["norm"] = mean, inv_std

    def halo_once(index):
        if index not in state:
            state[index] = True
            state["halos"][index].wait_recv()

    def patch(turn):
        frame = (turn + 2) % (frames + 1)
        if frame < 2:
            halo_once(0)
        mean, inv_std = state["norm"]
        source = earlier.at[frame] if frame < 2 else clip_ref.at[frame - 2]
        mask = frame_mask(frame - 2)

        def rows(index, _):
            values = source[index].astype(jnp.float32)
            preact = (values - mean) * inv_std * gain + bias
            hidden = preact / (1.0 + jnp.exp(-preact)) * mask
            for lane in range(lanes):
                part = hidden[:, :, lane * 128 : (lane + 1) * 128]
                held[lane, index, 1, 8 : 8 + cols, :] = part[0]
                held[lane, index + 1, 0, 8 : 8 + cols, :] = part[1]
            return 0

        lax.fori_loop(0, half_rows, rows, 0, unroll=4)
        for step_r in range(3):
            for step_c in range(3):
                pieces = [
                    held[
                        lane,
                        step_r // 2 : step_r // 2 + half_rows,
                        step_r % 2,
                        pl.ds(7 + step_c, half_cols, 2),
                        :,
                    ].reshape(area, 128)
                    for lane in range(lanes)
                ]
                piece = jnp.concatenate(pieces, axis=1).astype(jnp.bfloat16)
                for step_t in range(3):
                    if (frame - step_t) % 2 == 0 and 0 <= frame - step_t < frames:
                        at = (frame - step_t) // 2
                        tap = 9 * step_t + 3 * step_r + step_c
                        patches[at * area : (at + 1) * area, tap * channels : (tap + 1) * channels] = piece

    offsets = [reach]
    for step in range(reach - 1, 0, -1):
        offsets += [-step, step]
    offsets.append(0)
    slot_of = {offset % dp_size: slot for slot, offset in enumerate(offsets)}
    swaps = {}

    def skew_of(offset):
        return dp_at(pos + offset) * rows_w % 128

    def taps(slot):
        skew = skew_of(offsets[slot])
        start = pl.multiple_of(dp_at(pos + offsets[slot]) * rows_w - skew, 128)
        value = lax.dot_general(
            patches[:, pl.ds(start, window)],
            turned[...],
            (((0,), (0,)), ((), ())),
            preferred_element_type=jnp.float32,
        )
        grads[slot] = value[:, 0:128]
        mate_out[slot] = value[:, 128:256].astype(jnp.bfloat16)
        span = pl.ds(pl.multiple_of(skew, 32), rows_w)
        swaps[slot] = send(
            mate_out.at[slot, span], mate_in.at[slot, span], mate_send.at[slot], mate_recv.at[slot], mate
        )

    edge_at, other_at = planes(edge, middle)
    spans = ((edge_at, edge), (edge, middle))

    def base(offset, start, size):
        slot = slot_of[offset % dp_size]
        if ("swap", slot) not in state:
            state["swap", slot] = True
            swaps[slot].wait_recv()
        span = pl.ds(pl.multiple_of(skew_of(offset) + start, 16), size)
        return grads[slot, span, :] + mate_in[slot, span, :].astype(jnp.float32)

    rings, folds = {}, {}
    ring_last = ((reach - 1, reach), (reach, reach - 1))
    ring_out, ring_in = (edge_out, middle_out), (edge_in, middle_in)

    def fold_over(index, cut):
        at = (index, cut)
        fold_out[at] = base(index, *piece_of(other_at, edge, cuts, cut)).astype(jnp.bfloat16)
        folds[at] = send(fold_out.at[at], fold_in.at[at], fold_send.at[at], fold_recv.at[at], across)

    def gathered_sum(offset, kind, cut):
        value = base(offset, *piece_of(*spans[kind], cuts, cut))
        if kind == EDGE:
            at = (offset % dp_size, cut)
            folds[at].wait_recv()
            value = value + fold_in[at].astype(jnp.float32)
        return value

    def gradient(way, kind, step, cut):
        value = gathered_sum(SIGN[way] * step, kind, cut)
        if step < ring_last[way][kind]:
            rings[way, kind, step + 1, cut].wait_recv()
            value = value + ring_in[kind][way, step, cut].astype(jnp.float32)
        at, sem = (way, step - 1, cut), (way, kind, step - 1, cut)
        ring_out[kind][at] = value.astype(jnp.bfloat16)
        rings[way, kind, step, cut] = send(
            ring_out[kind].at[at], ring_in[kind].at[at], ring_send.at[sem], ring_recv.at[sem], onward[way]
        )

    lasts, shares = {}, []
    last_of = (last_edge, last_middle)

    def share(third, start, size, cut, value):
        start, size = piece_of(start, size, cuts, cut)
        span = pl.ds(pl.multiple_of(start, 16), size)
        share_out[span, :] = value
        at = (third, cut)
        shares.append(send(share_out.at[span], share_in.at[span], share_send.at[at], share_recv.at[at], mate))

    def summed(kind, cut):
        value = gathered_sum(0, kind, cut)
        for way in (UP, DOWN):
            rings[way, kind, 1, cut].wait_recv()
            value = value + ring_in[kind][way, 0, cut].astype(jnp.float32)
        last = last_of[kind]
        last[0, cut] = value.astype(jnp.bfloat16)
        at = (kind, cut)
        lasts[at] = send(last.at[0, cut], last.at[1, cut], last_send.at[at], last_recv.at[at], across)
        if kind == EDGE:
            share(0, edge_at, edge, cut, last[0, cut].astype(jnp.float32))

    def shared(kind, cut):
        lasts[kind, cut].wait_recv()
        value = last_of[kind][1, cut].astype(jnp.float32)
        if kind == EDGE:
            share(1, other_at, edge, cut, value)
        else:
            share(2, edge, middle, cut, last_of[kind][0, cut].astype(jnp.float32) + value)

    def cotangent_views():
        halo_once(1)
        wide[...] = jnp.zeros_like(wide)
        inner = jnp.where(tm < tm_size - 1, 1.0, 0.0).astype(jnp.float32)
        for frame in range(frames_out + 1):
            if frame < frames_out:
                piece = cot_ref[frame * area : (frame + 1) * area, :].astype(jnp.float32)
            else:
                piece = next_cot[...].astype(jnp.float32) * inner
            wide[frame, 0:half_rows, 0:half_cols, :] = piece.reshape(half_rows, half_cols, channels)
        for dt in range(2):
            for dr in range(2):
                for dc in range(2):
                    piece = wide[dt : dt + frames_out, dr : dr + half_rows, dc : dc + half_cols, :]
                    views[4 * dt + 2 * dr + dc] = piece.reshape(count, channels).astype(jnp.bfloat16)

    def weights():
        for copy in mates:
            copy.wait_recv()

    def weight_rows(start, size):
        return jnp.concatenate([full_weight[half, start : start + size, :] for half in range(2)], axis=1)

    times = (((2, 0), (0, 1)), ((1, 1),))
    spaces = (((1, 0),), ((2, 0), (0, 1)))

    def hidden_part(part):
        part_t, part_r, part_c = part // 4, part // 2 % 2, part % 2
        total = jnp.zeros((count, channels), jnp.float32)
        for step_t, dt in times[part_t]:
            for step_r, dr in spaces[part_r]:
                for step_c, dc in spaces[part_c]:
                    tap = 9 * step_t + 3 * step_r + step_c
                    total += lax.dot_general(
                        views[4 * dt + 2 * dr + dc],
                        weight_rows(tap * channels, channels),
                        (((1,), (1,)), ((), ())),
                        preferred_element_type=jnp.float32,
                    )
        total = total.reshape(frames_out, half_rows, half_cols, channels)
        for frame in range(frames_out):
            for lane in range(lanes):
                spread[
                    lane, 2 * frame + part_t, :, part_r, pl.ds(part_c, half_cols, 2), :
                ] = total[frame, :, :, lane * 128 : (lane + 1) * 128]

    quarter = frames * half_rows // 4

    def back(part):
        mean, inv_std = state["norm"]

        def back_rows(index, sums):
            frame, row = index // half_rows, index % half_rows
            normed = (clip_ref[frame, row].astype(jnp.float32) - mean) * inv_std
            preact = normed * gain + bias
            sig = 1.0 / (1.0 + jnp.exp(-preact))
            slope = sig * (1.0 + preact * (1.0 - sig))
            hidden_grad = jnp.concatenate([spread[lane, frame, row] for lane in range(lanes)], axis=-1)
            value = hidden_grad * frame_mask(frame) * slope * gain
            for lane in range(lanes):
                spread[lane, frame, row] = value[:, :, lane * 128 : (lane + 1) * 128]
            return sums[0] + fold(value), sums[1] + fold(value * normed)

        sums = state.get("sums", (zero, zero))
        state["sums"] = lax.fori_loop(
            0, quarter, lambda step, sums: back_rows(part * quarter + step, sums), sums, unroll=4
        )

    def back_exchange():
        state["finish"] = exchange(state["sums"], back_in, 1)

    deep = 9 * channels

    def output_part(step):
        total = jnp.dot(
            patches[:, step * deep : (step + 1) * deep],
            weight_rows(step * deep, deep),
            preferred_element_type=jnp.float32,
        )
        done = state.get("outs", 0)
        if done > 0:
            total += out_sum[...]
        if done == 2:
            out_ref[...] = total.astype(jnp.bfloat16)
        else:
            out_sum[...] = total
        state["outs"] = done + 1

    def back_finish():
        total = state["finish"]()
        state["back"] = total[0:1] / entries, total[1:2] / entries

    def input_part(part):
        mean, inv_std = state["norm"]
        back_first, back_second = state["back"]

        def input_rows(index, _):
            frame, row = index // half_rows, index % half_rows
            normed = (clip_ref[frame, row].astype(jnp.float32) - mean) * inv_std
            value = jnp.concatenate([spread[lane, frame, row] for lane in range(lanes)], axis=-1)
            input_grad_ref[frame, row] = (
                frame_mask(frame) * inv_std * (value - back_first - normed * back_second)
            ).astype(jnp.bfloat16)
            return 0

        lax.fori_loop(0, quarter, lambda step, _: input_rows(part * quarter + step, 0), 0, unroll=4)

    def result():
        for copy in shares:
            copy.wait_recv()
        weight_grad_ref[:, half_lane] = share_out[...]
        weight_grad_ref[:, other_lane] = share_in[...]

    steps = {
        "m": moments, "s": statistics, "p": patch, "t": taps, "g": gathered, "x": crossed, "f": fold_over,
        "r": gradient, "u": summed, "h": shared, "v": cotangent_views, "w": weights, "d": hidden_part,
        "b": back, "e": back_exchange, "o": output_part, "z": back_finish, "i": input_part, "y": result,
    }
    for name, *where in order:
        steps[name](*where)
    for copy in pending:
        copy.wait_send()


def ring_shards(dp_size, tm_size, clips, frame_counts, weight, gain, bias, cotangent):
    clip_data, cot_block = clips[0], cotangent[0]
    frame_count, row_count, col_count, channels = clip_data.shape
    frames_out, rows_out, cols_out = cot_block.shape[:3]
    area = rows_out * cols_out
    count = frames_out * area
    split = (frame_count, row_count // 2, 2, col_count, channels)
    rows_w = weight.shape[0]
    rows = dp_size * rows_w
    lanes = channels // 128
    gather_edge, gather_cuts, edge, cuts, _ = PLAN
    middle = rows_w - 2 * edge
    reach = dp_size // 2
    window = (rows_w + 96 + 127) // 128 * 128
    dma = pltpu.SemaphoreType.DMA
    f32, bf16 = jnp.float32, jnp.bfloat16
    pairs = [
        (2, 2, reach, gather_cuts), (2, reach, gather_cuts), (2, 3, reach), (dp_size,), (dp_size, cuts),
        (2, 2, reach, cuts), (2, cuts), (3, cuts),
    ]
    output, input_grad, weight_grad = pl.pallas_call(
        functools.partial(ring_kernel, dp_size, tm_size, PLAN, channels // GROUPS),
        out_shape=(
            pltpu.VMEM((count, channels), bf16),
            pltpu.VMEM(split, bf16),
            pltpu.VMEM((rows_w, channels), f32),
        ),
        in_specs=[SMEM] + [VMEM] * 2 + [HBM] * 3,
        out_specs=(VMEM, VMEM, VMEM),
        scratch_shapes=[
            pltpu.VMEM(split, bf16),
            pltpu.VMEM((count, channels), bf16),
            pltpu.VMEM((count, channels), f32),
            pltpu.VMEM((2,) + split[1:], bf16),
            pltpu.VMEM((area, channels), bf16),
            pltpu.VMEM((2, rows, 128), bf16),
            pltpu.VMEM((count, rows + 128), bf16),
            pltpu.VMEM((count, channels), bf16),
            pltpu.VMEM((dp_size, window, 128), f32),
            pltpu.VMEM((dp_size, window, 128), bf16),
            pltpu.VMEM((dp_size, window, 128), bf16),
            pltpu.VMEM((dp_size, cuts, edge // cuts, 128), bf16),
            pltpu.VMEM((dp_size, cuts, edge // cuts, 128), bf16),
            pltpu.VMEM((2, reach, cuts, edge // cuts, 128), bf16),
            pltpu.VMEM((2, reach, cuts, edge // cuts, 128), bf16),
            pltpu.VMEM((2, reach, cuts, middle // cuts, 128), bf16),
            pltpu.VMEM((2, reach, cuts, middle // cuts, 128), bf16),
            pltpu.VMEM((2, cuts, edge // cuts, 128), bf16),
            pltpu.VMEM((2, cuts, middle // cuts, 128), bf16),
            pltpu.VMEM((rows_w, 128), f32),
            pltpu.VMEM((rows_w, 128), f32),
            pltpu.VMEM((lanes, rows_out + 1, 2, col_count + 8, 128), f32),
            pltpu.VMEM((frames_out + 1, rows_out + 1, 16, channels), f32),
            pltpu.VMEM((8, count, channels), bf16),
            pltpu.VMEM((lanes,) + split[:-1] + (128,), f32),
            pltpu.VMEM((tm_size, 8, channels), f32),
            pltpu.VMEM((tm_size, 8, channels), f32),
        ]
        + [dma((2,))] * 2
        + [dma((2, tm_size))] * 2
        + [dma((2,)), dma((frame_count + 1,))]
        + [dma(shape) for shape in pairs for _ in range(2)],
        compiler_params=pltpu.CompilerParams(
            collective_id=0, has_side_effects=True, vmem_limit_bytes=RING_VMEM
        ),
    )(frame_counts, gain[None], bias[None], clip_data.reshape(split), cot_block.reshape(count, channels), weight)
    output, input_grad, weight_grad = settled(output, input_grad, weight_grad)
    return (
        output.reshape(cot_block.shape)[None],
        input_grad.reshape(clip_data.shape)[None],
        weight_grad,
    )


def copy_kernel(*refs):
    count = len(refs) // 2
    sems = refs[-1]
    copies = []
    for index in range(count):
        size = refs[index].shape[0] // COPY_PARTS
        for part in range(COPY_PARTS):
            span = pl.ds(part * size, size)
            copies.append(
                pltpu.make_async_copy(refs[index].at[span], refs[count + index].at[span], sems.at[len(copies)])
            )
            copies[-1].start()
    for copy in copies:
        copy.wait()


def settled(*arrays):
    sems = pltpu.SemaphoreType.DMA((COPY_PARTS * len(arrays),))
    return pl.pallas_call(
        copy_kernel,
        out_shape=tuple(jax.ShapeDtypeStruct(array.shape, array.dtype) for array in arrays),
        in_specs=[VMEM] * len(arrays),
        out_specs=(HBM,) * len(arrays),
        scratch_shapes=[sems],
        compiler_params=pltpu.CompilerParams(vmem_limit_bytes=COPY_VMEM),
    )(*arrays)


def by_ring(dp_size, tm_size, weight_rows):
    return dp_size == 8 and tm_size == 4 and weight_rows == 864


def device_part(dp_size, tm_size, *arrays):
    chosen = ring_shards if by_ring(dp_size, tm_size, arrays[2].shape[0]) else shards
    return chosen(dp_size, tm_size, *arrays)


def solution(mesh):
    placed = (
        P("dp", "tm", None, None, None),
        P("dp"),
        P("dp", None),
        P(),
        P(),
        P("dp", "tm", None, None, None),
    )
    return jax.shard_map(
        functools.partial(device_part, mesh.shape["dp"], mesh.shape["tm"]),
        mesh=mesh,
        in_specs=placed,
        out_specs=(P("dp", "tm", None, None, None), P("dp", "tm", None, None, None), P("dp", None)),
        check_vma=False,
    )
```

```python
import functools

import jax
import jax.numpy as jnp
from jax import lax
from jax.experimental import pallas as pl
from jax.experimental.pallas import tpu as pltpu
from jax.sharding import PartitionSpec as P

GROUPS = 32
EPS = 1e-06
PARTS = 3
MESH = pl.DeviceIdType.MESH
VMEM = pl.BlockSpec(memory_space=pltpu.VMEM)
SMEM = pl.BlockSpec(memory_space=pltpu.SMEM)


def plan(dp_size, tm_size):
    dp_bits = [("dp", k) for k in range(dp_size.bit_length() - 1)]
    tm_bits = [("tm", k) for k in range(tm_size.bit_length() - 1)]
    cut = len(dp_bits) // 2
    ways = [tm_bits[1:], dp_bits[:cut], dp_bits[cut:]]
    orders = []
    for part in range(PARTS):
        turned = ways[part:] + ways[:part]
        orders.append(tm_bits[:1] + turned[0] + turned[1] + turned[2])
    return dp_bits[::-1] + tm_bits[::-1], orders


def lane_group_sum(value, width):
    channels = value.shape[-1]
    lane = lax.broadcasted_iota(jnp.int32, value.shape, value.ndim - 1)
    step = 1
    while step < width:
        above = pltpu.roll(value, channels - step, value.ndim - 1)
        below = pltpu.roll(value, step, value.ndim - 1)
        value = value + jnp.where((lane // step) % 2 == 0, above, below)
        step *= 2
    return value


def block_kernel(
    labels, orders, dp_size, tm_size, near, width_g,
    valid_ref, params_ref, clip_ref, cot_ref, weight_ref,
    out_ref, input_grad_ref, weight_grad_ref,
    earlier, next_cot, full_weight, patches, grads, held, wide, views, spread, shared, sums_in, back_in,
    *scratch,
):
    frames, half_rows, _, cols, channels = clip_ref.shape
    frames_out, half_cols, lanes = frames // 2, cols // 2, channels // 128
    area = half_rows * half_cols
    count = frames_out * area
    depth = len(labels)
    sends, receives, kept = (scratch[i * depth : (i + 1) * depth] for i in range(3))
    (send_sem, recv_sem, share_send, share_recv, ring_send, ring_recv, sum_send, sum_recv,
     far_send, far_recv, near_send, near_recv, mate_send, mate_recv, cross_send, cross_recv, own_sem) = scratch[3 * depth :]
    dp, tm = lax.axis_index("dp"), lax.axis_index("tm")
    place = {"dp": dp, "tm": tm}
    far_size = dp_size // near
    far_at, near_at = dp // near, dp % near
    core = tm % 2
    mate = {"tm": tm + 1 - 2 * core}

    def bit_of(label):
        return (place[label[0]] // 2 ** label[1]) % 2

    def partner(label):
        return {label[0]: place[label[0]] + (1 - 2 * bit_of(label)) * 2 ** label[1]}

    def send(source, target, sem_out, sem_in, device):
        copy = pltpu.make_async_remote_copy(
            src_ref=source, dst_ref=target, send_sem=sem_out, recv_sem=sem_in,
            device_id=device, device_id_type=MESH,
        )
        copy.start()
        return copy

    barrier = pltpu.get_barrier_semaphore()
    greeted = [{"tm": (tm + step) % tm_size} for step in range(1, tm_size)]
    greeted += [{"dp": dp_index} for dp_index in dp_peers(dp, dp_size, near)]
    for device in greeted:
        pl.semaphore_signal(barrier, inc=1, device_id=device, device_id_type=MESH)
    pl.semaphore_wait(barrier, len(greeted))

    ring = [
        send(clip_ref.at[frames - 2 : frames], earlier, ring_send.at[0], ring_recv.at[0], {"tm": (tm + 1) % tm_size}),
        send(cot_ref.at[0:area], next_cot, ring_send.at[1], ring_recv.at[1], {"tm": (tm + tm_size - 1) % tm_size}),
    ]

    rows_w = weight_ref.shape[0]
    half_lane = pl.ds(pl.multiple_of(core * 128, 128), 128)

    crossed = tm_size == 4 and rows_w % 48 == 0
    rows_x = rows_w // 3 if crossed else 0
    span_w = rows_w - rows_x
    across = (tm // 2) % 2 if crossed else 0
    cross_mate = {"tm": (tm + 2) % tm_size}
    span_at = across * rows_x

    def rows_of(index, start, size):
        return full_weight.at[pl.ds(pl.multiple_of(index * rows_w + start, 8), size), half_lane]

    def block_at(index):
        return rows_of(index, span_at, span_w)

    own_copy = pltpu.make_async_copy(
        weight_ref, full_weight.at[pl.ds(pl.multiple_of(dp * rows_w, 8), rows_w), :], own_sem
    )
    own_copy.start()
    own_half = weight_ref.at[pl.ds(pl.multiple_of(span_at, 8), span_w), half_lane]
    far_copies = [
        send(own_half, block_at(dp), far_send.at[step], far_recv.at[step],
             {"dp": ((far_at + step) % far_size) * near + near_at})
        for step in range(1, far_size)
    ]
    near_copies, mate_copies, cross_copies = {}, [], []

    def send_near(step, source, index):
        for hop in range(1, near):
            near_copies[step, hop] = send(
                source, block_at(index), near_send.at[step, hop], near_recv.at[step, hop],
                {"dp": far_at * near + (near_at + hop) % near},
            )

    def send_mate(step, hop, index):
        if crossed:
            cross = rows_of(index, across * (span_w), rows_x)
            copy = send(cross, cross, cross_send.at[step, hop], cross_recv.at[step, hop], cross_mate)
            cross_copies.append((copy, step, hop, index))
        mate_copies.append(
            send(block_at(index), block_at(index), mate_send.at[0, step, hop], mate_recv.at[0, step, hop], mate)
        )

    def weight_cross():
        for copy, step, hop, index in cross_copies:
            copy.wait_recv()
            rest = rows_of(index, (1 - across) * span_w, rows_x)
            mate_copies.append(
                send(rest, rest, mate_send.at[1, step, hop], mate_recv.at[1, step, hop], mate)
            )

    send_near(0, own_half, dp)

    def weight_far(step):
        far_copies[step - 1].wait_recv()
        index = ((far_at + far_size - step) % far_size) * near + near_at
        send_near(step, block_at(index), index)
        send_mate(step, 0, index)

    def weight_near(step):
        for hop in range(1, near):
            near_copies[step, hop].wait_recv()
            index = ((far_at + far_size - step) % far_size) * near + (near_at + near - hop) % near
            send_mate(step, hop, index)

    first = tm * frames
    valid = valid_ref[0]
    gain, bias = params_ref[0:1, :], params_ref[1:2, :]
    entries = jnp.full((1, channels), valid.astype(jnp.float32)) * float(2 * half_rows * cols * width_g)
    zero = jnp.zeros((8, channels), jnp.float32)

    def fold(value):
        return jnp.sum(value.reshape(-1, 8, channels), axis=0)

    def frame_mask(frame):
        slot = first + frame
        return jnp.where((slot >= 0) & (slot < valid), 1.0, 0.0).astype(jnp.float32)

    def moment_rows(index, sums):
        frame, row = index // half_rows, index % half_rows
        values = clip_ref[frame, row].astype(jnp.float32)
        masked = values * frame_mask(frame)
        return sums[0] + fold(masked), sums[1] + fold(masked * values)

    def exchange(sums, buffer, sems):
        pair = [jnp.sum(value, axis=0, keepdims=True) for value in sums]
        buffer[tm] = jnp.concatenate(pair + [jnp.zeros((6, channels), jnp.float32)], axis=0)
        copies = [
            send(buffer.at[tm], buffer.at[tm], sum_send.at[sems, step], sum_recv.at[sems, step],
                 {"tm": (tm + step) % tm_size})
            for step in range(1, tm_size)
        ]

        def finish():
            for copy in copies:
                copy.wait()
            total = buffer[0]
            for index in range(1, tm_size):
                total = total + buffer[index]
            return lane_group_sum(total, width_g)

        return finish

    finish = exchange(lax.fori_loop(0, frames * half_rows, moment_rows, (zero, zero), unroll=4), sums_in, 0)
    held[...] = jnp.zeros_like(held)
    total = finish()
    mean = total[0:1] / entries
    inv_std = lax.rsqrt(total[1:2] / entries - mean * mean + EPS)
    for copy in ring:
        copy.wait()

    ticks = [functools.partial(weight_far, step) for step in range(1, far_size)]
    for frame in range(frames + 1):
        source = earlier.at[frame] if frame < 2 else clip_ref.at[frame - 2]
        mask = frame_mask(frame - 2)

        def rows(index, _):
            values = source[index].astype(jnp.float32)
            preact = (values - mean) * inv_std * gain + bias
            hidden = preact / (1.0 + jnp.exp(-preact)) * mask
            for lane in range(lanes):
                part = hidden[:, :, lane * 128 : (lane + 1) * 128]
                held[lane, index, 1, 8 : 8 + cols, :] = part[0]
                held[lane, index + 1, 0, 8 : 8 + cols, :] = part[1]
            return 0

        lax.fori_loop(0, half_rows, rows, 0, unroll=4)
        for step_r in range(3):
            for step_c in range(3):
                pieces = [
                    held[
                        lane,
                        step_r // 2 : step_r // 2 + half_rows,
                        step_r % 2,
                        pl.ds(7 + step_c, half_cols, 2),
                        :,
                    ].reshape(area, 128)
                    for lane in range(lanes)
                ]
                piece = jnp.concatenate(pieces, axis=1).astype(jnp.bfloat16)
                for step_t in range(3):
                    if (frame - step_t) % 2 == 0 and 0 <= frame - step_t < frames:
                        at = (frame - step_t) // 2
                        tap = 9 * step_t + 3 * step_r + step_c
                        patches[at * area : (at + 1) * area, tap * channels : (tap + 1) * channels] = piece
        if frame % 3 == 2 and ticks:
            ticks.pop(0)()

    def tap_grad(tap, _):
        at = pl.multiple_of(tap * channels, channels)
        grads[pl.ds(at, channels), :] = lax.dot_general(
            patches[:, pl.ds(at, channels)],
            cot_ref[...],
            (((0,), (0,)), ((), ())),
            preferred_element_type=jnp.float32,
        )
        return 0

    for tick in ticks:
        tick()
    weight_near(0)
    lax.fori_loop(0, 27, tap_grad, 0)

    left = [list(labels) for _ in range(PARTS)]
    copies = [[None] * depth for _ in range(PARTS)]
    piece_rows = grads.shape[0] // (dp_size * tm_size * PARTS)

    def index_of(stride, number, bit):
        return (number // stride) * (2 * stride) + bit * stride + number % stride

    def read(stage, part, index):
        if stage == 0:
            at = (index * PARTS + part) * piece_rows
            if piece_rows % 8 == 0:
                return grads[pl.ds(pl.multiple_of(at, 8), piece_rows), :]
            window = (piece_rows + 14) // 8 * 8
            block = grads[pl.ds(pl.multiple_of(at // 8 * 8, 8), window), :]
            return pltpu.roll(block, (window - at % 8) % window, 0)[:piece_rows]
        return kept[stage - 1][part, index]

    def add(stage, part):
        label = orders[part][stage]
        stride = 2 ** (len(left[part]) - 1 - left[part].index(label))
        number = 2 ** (len(left[part]) - 1)
        copies[part][stage].wait_recv()

        def one(block, _):
            kept[stage][part, block] = read(
                stage, part, index_of(stride, block, bit_of(label))
            ) + receives[stage][part, block].astype(jnp.float32)
            return 0

        lax.fori_loop(0, number, one, 0)
        left[part].remove(label)

    def halve(stage):
        for part in range(PARTS):
            if stage > 0:
                add(stage - 1, part)
            label = orders[part][stage]
            stride = 2 ** (len(left[part]) - 1 - left[part].index(label))
            number = 2 ** (len(left[part]) - 1)

            def pack(block, _):
                sends[stage][part, block] = read(
                    stage, part, index_of(stride, block, 1 - bit_of(label))
                ).astype(jnp.bfloat16)
                return 0

            lax.fori_loop(0, number, pack, 0)
            copies[part][stage] = send(
                sends[stage].at[part], receives[stage].at[part],
                send_sem.at[part, stage], recv_sem.at[part, stage], partner(label),
            )

    halve(0)
    for step in range(1, far_size):
        weight_near(step)
    halve(1)
    weight_cross()
    for copy in mate_copies:
        copy.wait_recv()
    own_copy.wait()
    total = jnp.zeros((count, channels), jnp.float32)
    deep = 9 * channels
    for step in range(3):
        total += jnp.dot(
            patches[:, step * deep : (step + 1) * deep],
            full_weight[step * deep : (step + 1) * deep, :],
            preferred_element_type=jnp.float32,
        )
    out_ref[...] = total.astype(jnp.bfloat16)
    wide[...] = jnp.zeros_like(wide)
    last = jnp.where(tm < tm_size - 1, 1.0, 0.0).astype(jnp.float32)
    for frame in range(frames_out + 1):
        if frame < frames_out:
            piece = cot_ref[frame * area : (frame + 1) * area, :].astype(jnp.float32)
        else:
            piece = next_cot[...].astype(jnp.float32) * last
        wide[frame, 0:half_rows, 0:half_cols, :] = piece.reshape(half_rows, half_cols, channels)
    for dt in range(2):
        for dr in range(2):
            for dc in range(2):
                piece = wide[dt : dt + frames_out, dr : dr + half_rows, dc : dc + half_cols, :]
                views[4 * dt + 2 * dr + dc] = piece.reshape(count, channels).astype(jnp.bfloat16)
    times = (((2, 0), (0, 1)), ((1, 1),))
    spaces = (((1, 0),), ((2, 0), (0, 1)))
    stage = 2
    for part_t in range(2):
        for part_r in range(2):
            for part_c in range(2):
                total = jnp.zeros((count, channels), jnp.float32)
                for step_t, dt in times[part_t]:
                    for step_r, dr in spaces[part_r]:
                        for step_c, dc in spaces[part_c]:
                            tap = 9 * step_t + 3 * step_r + step_c
                            total += lax.dot_general(
                                views[4 * dt + 2 * dr + dc],
                                full_weight[tap * channels : (tap + 1) * channels, :],
                                (((1,), (1,)), ((), ())),
                                preferred_element_type=jnp.float32,
                            )
                total = total.reshape(frames_out, half_rows, half_cols, channels)
                for frame in range(frames_out):
                    for lane in range(lanes):
                        spread[
                            lane, 2 * frame + part_t, :, part_r, pl.ds(part_c, half_cols, 2), :
                        ] = total[frame, :, :, lane * 128 : (lane + 1) * 128]
    halve(stage)

    def back_rows(index, sums):
        frame, row = index // half_rows, index % half_rows
        normed = (clip_ref[frame, row].astype(jnp.float32) - mean) * inv_std
        preact = normed * gain + bias
        sig = 1.0 / (1.0 + jnp.exp(-preact))
        slope = sig * (1.0 + preact * (1.0 - sig))
        hidden_grad = jnp.concatenate([spread[lane, frame, row] for lane in range(lanes)], axis=-1)
        value = hidden_grad * frame_mask(frame) * slope * gain
        for lane in range(lanes):
            spread[lane, frame, row] = value[:, :, lane * 128 : (lane + 1) * 128]
        return sums[0] + fold(value), sums[1] + fold(value * normed)

    finish = exchange(lax.fori_loop(0, frames * half_rows, back_rows, (zero, zero), unroll=4), back_in, 1)
    for stage in range(3, depth):
        halve(stage)
    for part in range(PARTS):
        add(depth - 1, part)
        shared[tm, part] = kept[depth - 1][part, 0].astype(jnp.bfloat16)

    tm_bits = [label for label in labels if label[0] == "tm"]
    shares, serial = [], 0
    for label in tm_bits:
        span = 2 ** (label[1] + 1)
        stage_shares = []
        for high in range(tm_size // span):
            block = high * span + tm % span
            stage_shares.append(
                send(shared.at[block], shared.at[block],
                     share_send.at[serial], share_recv.at[serial], partner(label))
            )
            serial += 1
        if label == tm_bits[0]:
            total = finish()
            back_first, back_second = total[0:1] / entries, total[1:2] / entries

            def input_rows(index, _):
                frame, row = index // half_rows, index % half_rows
                normed = (clip_ref[frame, row].astype(jnp.float32) - mean) * inv_std
                value = jnp.concatenate([spread[lane, frame, row] for lane in range(lanes)], axis=-1)
                input_grad_ref[frame, row] = (
                    frame_mask(frame) * inv_std * (value - back_first - normed * back_second)
                ).astype(jnp.bfloat16)
                return 0

            lax.fori_loop(0, frames * half_rows, input_rows, 0, unroll=4)
        for share in stage_shares:
            share.wait_recv()
        shares += stage_shares
    for block in range(tm_size):
        weight_grad_ref[block] = shared[block].astype(jnp.float32)
    for copy in shares + far_copies + list(near_copies.values()) + mate_copies + [item[0] for item in cross_copies]:
        copy.wait_send()
    for part in range(PARTS):
        for copy in copies[part]:
            copy.wait_send()


def dp_peers(dp, dp_size, near):
    far_at, near_at, far_size = dp // near, dp % near, dp_size // near
    peers = [((far_at + step) % far_size) * near + near_at for step in range(1, far_size)]
    return peers + [far_at * near + (near_at + hop) % near for hop in range(1, near)]


def shards(dp_size, tm_size, clips, frame_counts, weight, gain, bias, cotangent):
    clip_data, cot_block = clips[0], cotangent[0]
    frame_count, row_count, col_count, channels = clip_data.shape
    frames_out, rows_out, cols_out = cot_block.shape[:3]
    area = rows_out * cols_out
    count = frames_out * area
    split = (frame_count, row_count // 2, 2, col_count, channels)
    labels, orders = plan(dp_size, tm_size)
    depth = len(labels)
    rows = dp_size * weight.shape[0]
    piece = rows // (dp_size * tm_size * PARTS)
    halves = [(PARTS, 2 ** (depth - 1 - stage), piece, channels) for stage in range(depth)]
    near = 2 ** ((dp_size.bit_length() - 1) // 2)
    far = dp_size // near
    lanes = channels // 128
    dma = pltpu.SemaphoreType.DMA
    f32, bf16 = jnp.float32, jnp.bfloat16
    output, input_grad, weight_grad = pl.pallas_call(
        functools.partial(block_kernel, labels, orders, dp_size, tm_size, near, channels // GROUPS),
        out_shape=(
            jax.ShapeDtypeStruct((count, channels), bf16),
            jax.ShapeDtypeStruct(split, bf16),
            jax.ShapeDtypeStruct((tm_size, PARTS, piece, channels), f32),
        ),
        in_specs=[SMEM] + [VMEM] * 4,
        out_specs=(VMEM, VMEM, VMEM),
        scratch_shapes=[
            pltpu.VMEM((2,) + split[1:], bf16),
            pltpu.VMEM((area, channels), bf16),
            pltpu.VMEM((rows, channels), bf16),
            pltpu.VMEM((count, rows), bf16),
            pltpu.VMEM((rows, channels), f32),
            pltpu.VMEM((lanes, rows_out + 1, 2, col_count + 8, 128), f32),
            pltpu.VMEM((frames_out + 1, rows_out + 1, 16, channels), f32),
            pltpu.VMEM((8, count, channels), bf16),
            pltpu.VMEM((lanes,) + split[:-1] + (128,), f32),
            pltpu.VMEM((tm_size, PARTS, piece, channels), bf16),
            pltpu.VMEM((tm_size, 8, channels), f32),
            pltpu.VMEM((tm_size, 8, channels), f32),
        ]
        + [pltpu.VMEM(shape, bf16) for shape in halves] * 2
        + [pltpu.VMEM(shape, f32) for shape in halves]
        + [dma((PARTS, depth))] * 2
        + [dma((tm_size,))] * 2
        + [dma((2,))] * 2
        + [dma((2, tm_size))] * 2
        + [dma((far,))] * 2
        + [dma((far, near))] * 2
        + [dma((2, far, near))] * 2
        + [dma((far, near))] * 2
        + [dma(())],
        compiler_params=pltpu.CompilerParams(
            collective_id=0, has_side_effects=True, vmem_limit_bytes=56 * 2**20
        ),
    )(frame_counts, jnp.stack([gain, bias]), clip_data.reshape(split), cot_block.reshape(count, channels), weight)
    return (
        output.reshape(cot_block.shape)[None],
        input_grad.reshape(clip_data.shape)[None],
        weight_grad.reshape(weight.shape),
    )


HBM = pl.BlockSpec(memory_space=pl.ANY)
UP, DOWN = 0, 1
EDGE, MIDDLE = 0, 1
SIGN = (1, -1)
COPY_PARTS = 2
RING_VMEM = 54 * 2**20
COPY_VMEM = 16 * 2**20
ORDER = (
    ("m",), ("s",), ("p", 0), ("p", 2), ("p", 4), ("p", 5), ("g", 1, 0, 1, 0), ("g", 0, 0, 1, 0), ("v",),
    ("g", 1, 0, 1, 1), ("p", 1), ("g", 0, 1, 1, 0), ("g", 1, 1, 1, 0), ("p", 6), ("g", 0, 1, 1, 1),
    ("g", 1, 1, 1, 1), ("g", 0, 0, 1, 1), ("p", 3), ("p", 7), ("p", 8), ("t", 0), ("t", 1), ("t", 2),
    ("g", 0, 0, 2, 0), ("g", 1, 0, 2, 0), ("t", 3), ("g", 0, 1, 2, 0), ("t", 4), ("g", 1, 0, 2, 1), ("t", 5),
    ("g", 1, 1, 2, 0), ("g", 0, 1, 2, 1), ("t", 6), ("t", 7), ("g", 1, 1, 2, 1), ("g", 0, 0, 2, 1),
    ("g", 1, 0, 3, 0), ("r", 0, 1, 4, 0), ("f", 4, 0), ("r", 1, 1, 3, 0), ("f", 3, 0), ("g", 0, 0, 3, 0),
    ("g", 0, 0, 3, 1), ("f", 5, 0), ("x", 0, 2, 0), ("x", 0, 1, 0), ("x", 1, 1, 0), ("g", 1, 0, 3, 1),
    ("g", 0, 1, 3, 0), ("g", 1, 1, 3, 0), ("x", 1, 2, 0), ("g", 0, 1, 3, 1), ("r", 1, 0, 4, 0), ("f", 2, 0),
    ("r", 0, 1, 3, 0), ("x", 0, 3, 0), ("g", 0, 0, 4, 0), ("g", 1, 1, 3, 1), ("x", 0, 1, 1), ("g", 0, 0, 4, 1),
    ("r", 0, 0, 3, 0), ("f", 6, 0), ("x", 1, 3, 0), ("g", 1, 1, 4, 0), ("r", 1, 0, 3, 0), ("x", 1, 2, 1),
    ("r", 1, 1, 2, 0), ("x", 0, 3, 1), ("r", 0, 1, 2, 0), ("f", 1, 0), ("x", 0, 2, 1), ("g", 1, 1, 4, 1),
    ("x", 0, 4, 0), ("x", 1, 3, 1), ("r", 0, 0, 2, 0), ("f", 7, 0), ("f", 0, 0), ("x", 1, 1, 1), ("x", 0, 4, 1),
    ("r", 1, 0, 2, 0), ("r", 1, 1, 1, 0), ("w",), ("r", 0, 1, 1, 0), ("d", 3), ("d", 2), ("d", 0), ("d", 4),
    ("d", 6), ("r", 0, 0, 1, 0), ("d", 7), ("r", 1, 0, 1, 0), ("d", 1), ("d", 5), ("b", 2), ("b", 1), ("b", 3),
    ("u", 1, 0), ("o", 2), ("b", 0), ("e",), ("u", 0, 0), ("o", 0), ("o", 1), ("h", 1, 0), ("z",), ("i", 1),
    ("h", 0, 0), ("i", 0), ("i", 3), ("i", 2), ("y",),
)
PLAN = (224, 2, 208, 1, ORDER)


def ring_kernel(
    dp_size, tm_size, plan, width_g,
    valid_ref, gain_ref, bias_ref, clip_hbm, cot_hbm, weight_hbm,
    out_ref, input_grad_ref, weight_grad_ref,
    clip_ref, cot_ref, out_sum, earlier, next_cot, full_weight, patches, turned, grads, mate_out, mate_in,
    fold_out, fold_in, edge_out, edge_in, middle_out, middle_in,
    last_edge, last_middle, share_out, share_in,
    held, wide, views, spread, sums_in, back_in,
    halo_send, halo_recv, sum_send, sum_recv, own_sem, load_sem,
    gather_send, gather_recv, cross_send, cross_recv, copy_send, copy_recv,
    mate_send, mate_recv, fold_send, fold_recv, ring_send, ring_recv,
    last_send, last_recv, share_send, share_recv,
):
    frames, half_rows, _, cols, channels = clip_ref.shape
    frames_out, half_cols, lanes = frames // 2, cols // 2, channels // 128
    area = half_rows * half_cols
    count = frames_out * area
    window, rows_all = grads.shape[1], full_weight.shape[1]
    rows_w = weight_hbm.shape[0]
    gather_edge, gather_cuts, edge, cuts, order = plan
    gather_middle, middle = rows_w - 2 * gather_edge, rows_w - 2 * edge
    dp, tm = lax.axis_index("dp"), lax.axis_index("tm")
    core, side = tm % 2, tm // 2
    mate = {"tm": tm + 1 - 2 * core}
    across = {"tm": (tm + 2) % tm_size}
    far_size, reach = dp_size // 2, dp_size // 2
    pos = dp // 2 + (dp % 2) * (2 * far_size - 1 - 2 * (dp // 2))

    def dp_at(place):
        place = (place + 2 * dp_size) % dp_size
        turn = place // far_size
        return 2 * (place + turn * (2 * far_size - 1 - 2 * place)) + turn

    onward = [{"dp": dp_at(pos + sign)} for sign in SIGN]
    pending = []

    def send(source, target, sem_out, sem_in, device):
        copy = pltpu.make_async_remote_copy(
            src_ref=source, dst_ref=target, send_sem=sem_out, recv_sem=sem_in,
            device_id=device, device_id_type=MESH,
        )
        copy.start()
        pending.append(copy)
        return copy

    barrier = pltpu.get_barrier_semaphore()
    greeted = [{"tm": (tm + step) % tm_size} for step in range(1, tm_size)] + onward
    for device in greeted:
        pl.semaphore_signal(barrier, inc=1, device_id=device, device_id_type=MESH)

    half_lane = pl.ds(pl.multiple_of(core * 128, 128), 128)
    other_lane = pl.ds(pl.multiple_of((1 - core) * 128, 128), 128)

    def planes(edge, middle):
        return side * (edge + middle), (1 - side) * (edge + middle)

    gather_at, gather_other = planes(gather_edge, gather_middle)
    gather_spans = ((gather_at, gather_edge), (gather_edge, gather_middle))

    def piece_of(start, size, cuts, cut):
        return start + cut * (size // cuts), size // cuts

    def rows_at(block, start, size):
        return pl.ds(pl.multiple_of(block * rows_w + start, 16), size)

    def region(block, start, size):
        return full_weight.at[core, rows_at(block, start, size)]

    gather_last = ((reach, reach - 1), (reach - 1, reach))
    gathers, crosses, mates = {}, {}, []

    def gather(way, kind, step, cut):
        start, size = piece_of(*gather_spans[kind], gather_cuts, cut)
        target = region(dp_at(pos - SIGN[way] * (step - 1)), start, size)
        at = (way, kind, step - 1, cut)
        gathers[way, kind, step, cut] = send(target, target, gather_send.at[at], gather_recv.at[at], onward[way])

    def to_mate(way, third, step, start, size):
        block = region(dp_at(pos - SIGN[way] * step), start, size)
        at = (way, third, step - 1)
        mates.append(send(block, block, copy_send.at[at], copy_recv.at[at], mate))

    def gathered(way, kind, step, cut):
        gathers[way, kind, step, cut].wait_recv()
        if step < gather_last[way][kind]:
            gather(way, kind, step + 1, cut)
        if kind == EDGE:
            start, size = piece_of(*gather_spans[kind], gather_cuts, cut)
            block = region(dp_at(pos - SIGN[way] * step), start, size)
            at = (way, step - 1, cut)
            crosses[way, step, cut] = send(block, block, cross_send.at[at], cross_recv.at[at], across)
        if cut == gather_cuts - 1:
            to_mate(way, kind, step, *gather_spans[kind])

    def crossed(way, step, cut):
        crosses[way, step, cut].wait_recv()
        if cut == gather_cuts - 1:
            to_mate(way, 2, step, gather_other, gather_edge)

    first = tm * frames
    valid = valid_ref[0]
    gain, bias = gain_ref[...], bias_ref[...]
    entries = jnp.full((1, channels), valid.astype(jnp.float32)) * float(2 * half_rows * cols * width_g)
    zero = jnp.zeros((8, channels), jnp.float32)

    def fold(value):
        return jnp.sum(value.reshape(-1, 8, channels), axis=0)

    def frame_mask(frame):
        slot = first + frame
        return jnp.where((slot >= 0) & (slot < valid), 1.0, 0.0).astype(jnp.float32)

    def moment_rows(index, sums):
        frame, row = index // half_rows, index % half_rows
        values = clip_ref[frame, row].astype(jnp.float32)
        masked = values * frame_mask(frame)
        return sums[0] + fold(masked), sums[1] + fold(masked * values)

    def exchange(sums, buffer, sems):
        pair = [jnp.sum(value, axis=0, keepdims=True) for value in sums]
        buffer[tm] = jnp.concatenate(pair + [jnp.zeros((6, channels), jnp.float32)], axis=0)
        copies = [
            send(buffer.at[tm], buffer.at[tm], sum_send.at[sems, step], sum_recv.at[sems, step],
                 {"tm": (tm + step) % tm_size})
            for step in range(1, tm_size)
        ]

        def finish():
            for copy in copies:
                copy.wait_recv()
            total = buffer[0]
            for index in range(1, tm_size):
                total = total + buffer[index]
            return lane_group_sum(total, width_g)

        return finish

    state = {}
    own_loads = [
        pltpu.make_async_copy(
            weight_hbm.at[:, half * 128 : (half + 1) * 128], full_weight.at[half, rows_at(dp, 0, rows_w)],
            own_sem.at[half],
        )
        for half in range(2)
    ]
    clip_loads = [
        pltpu.make_async_copy(clip_hbm.at[frame], clip_ref.at[frame], load_sem.at[frame]) for frame in range(frames)
    ]
    cot_load = pltpu.make_async_copy(cot_hbm, cot_ref, load_sem.at[frames])
    for copy in clip_loads + own_loads + [cot_load]:
        copy.start()

    def begin():
        for kind in (EDGE, MIDDLE):
            for cut in range(gather_cuts):
                for way in (UP, DOWN):
                    gather(way, kind, 1, cut)

    def moments():
        sums = (zero, zero)
        for frame in range(frames):
            clip_loads[frame].wait()
            sums = lax.fori_loop(
                0, half_rows, lambda step, sums: moment_rows(frame * half_rows + step, sums), sums, unroll=4
            )
        pl.semaphore_wait(barrier, len(greeted))
        state["finish"] = exchange(sums, sums_in, 0)
        for copy in own_loads:
            copy.wait()
        begin()
        cot_load.wait()
        state["halos"] = [
            send(clip_ref.at[frames - 2 : frames], earlier, halo_send.at[0], halo_recv.at[0],
                 {"tm": (tm + 1) % tm_size}),
            send(cot_ref.at[0:area], next_cot, halo_send.at[1], halo_recv.at[1],
                 {"tm": (tm + tm_size - 1) % tm_size}),
        ]
        held[...] = jnp.zeros_like(held)
        turned[:, 0:128] = cot_ref[:, half_lane]
        turned[:, 128:256] = cot_ref[:, other_lane]
        patches[:, rows_all:] = jnp.zeros((count, patches.shape[1] - rows_all), jnp.bfloat16)

    def statistics():
        total = state["finish"]()
        mean = total[0:1] / entries
        inv_std = lax.rsqrt(total[1:2] / entries - mean * mean + EPS)
        state["norm"] = mean, inv_std

    def halo_once(index):
        if index not in state:
            state[index] = True
            state["halos"][index].wait_recv()

    def patch(turn):
        frame = (turn + 2) % (frames + 1)
        if frame < 2:
            halo_once(0)
        mean, inv_std = state["norm"]
        source = earlier.at[frame] if frame < 2 else clip_ref.at[frame - 2]
        mask = frame_mask(frame - 2)

        def rows(index, _):
            values = source[index].astype(jnp.float32)
            preact = (values - mean) * inv_std * gain + bias
            hidden = preact / (1.0 + jnp.exp(-preact)) * mask
            for lane in range(lanes):
                part = hidden[:, :, lane * 128 : (lane + 1) * 128]
                held[lane, index, 1, 8 : 8 + cols, :] = part[0]
                held[lane, index + 1, 0, 8 : 8 + cols, :] = part[1]
            return 0

        lax.fori_loop(0, half_rows, rows, 0, unroll=4)
        for step_r in range(3):
            for step_c in range(3):
                pieces = [
                    held[
                        lane,
                        step_r // 2 : step_r // 2 + half_rows,
                        step_r % 2,
                        pl.ds(7 + step_c, half_cols, 2),
                        :,
                    ].reshape(area, 128)
                    for lane in range(lanes)
                ]
                piece = jnp.concatenate(pieces, axis=1).astype(jnp.bfloat16)
                for step_t in range(3):
                    if (frame - step_t) % 2 == 0 and 0 <= frame - step_t < frames:
                        at = (frame - step_t) // 2
                        tap = 9 * step_t + 3 * step_r + step_c
                        patches[at * area : (at + 1) * area, tap * channels : (tap + 1) * channels] = piece

    offsets = [reach]
    for step in range(reach - 1, 0, -1):
        offsets += [-step, step]
    offsets.append(0)
    slot_of = {offset % dp_size: slot for slot, offset in enumerate(offsets)}
    swaps = {}

    def skew_of(offset):
        return dp_at(pos + offset) * rows_w % 128

    def taps(slot):
        skew = skew_of(offsets[slot])
        start = pl.multiple_of(dp_at(pos + offsets[slot]) * rows_w - skew, 128)
        value = lax.dot_general(
            patches[:, pl.ds(start, window)],
            turned[...],
            (((0,), (0,)), ((), ())),
            preferred_element_type=jnp.float32,
        )
        grads[slot] = value[:, 0:128]
        mate_out[slot] = value[:, 128:256].astype(jnp.bfloat16)
        span = pl.ds(pl.multiple_of(skew, 32), rows_w)
        swaps[slot] = send(
            mate_out.at[slot, span], mate_in.at[slot, span], mate_send.at[slot], mate_recv.at[slot], mate
        )

    edge_at, other_at = planes(edge, middle)
    spans = ((edge_at, edge), (edge, middle))

    def base(offset, start, size):
        slot = slot_of[offset % dp_size]
        if ("swap", slot) not in state:
            state["swap", slot] = True
            swaps[slot].wait_recv()
        span = pl.ds(pl.multiple_of(skew_of(offset) + start, 16), size)
        return grads[slot, span, :] + mate_in[slot, span, :].astype(jnp.float32)

    rings, folds = {}, {}
    ring_last = ((reach - 1, reach), (reach, reach - 1))
    ring_out, ring_in = (edge_out, middle_out), (edge_in, middle_in)

    def fold_over(index, cut):
        at = (index, cut)
        fold_out[at] = base(index, *piece_of(other_at, edge, cuts, cut)).astype(jnp.bfloat16)
        folds[at] = send(fold_out.at[at], fold_in.at[at], fold_send.at[at], fold_recv.at[at], across)

    def gathered_sum(offset, kind, cut):
        value = base(offset, *piece_of(*spans[kind], cuts, cut))
        if kind == EDGE:
            at = (offset % dp_size, cut)
            folds[at].wait_recv()
            value = value + fold_in[at].astype(jnp.float32)
        return value

    def gradient(way, kind, step, cut):
        value = gathered_sum(SIGN[way] * step, kind, cut)
        if step < ring_last[way][kind]:
            rings[way, kind, step + 1, cut].wait_recv()
            value = value + ring_in[kind][way, step, cut].astype(jnp.float32)
        at, sem = (way, step - 1, cut), (way, kind, step - 1, cut)
        ring_out[kind][at] = value.astype(jnp.bfloat16)
        rings[way, kind, step, cut] = send(
            ring_out[kind].at[at], ring_in[kind].at[at], ring_send.at[sem], ring_recv.at[sem], onward[way]
        )

    lasts, shares = {}, []
    last_of = (last_edge, last_middle)

    def share(third, start, size, cut, value):
        start, size = piece_of(start, size, cuts, cut)
        span = pl.ds(pl.multiple_of(start, 16), size)
        share_out[span, :] = value
        at = (third, cut)
        shares.append(send(share_out.at[span], share_in.at[span], share_send.at[at], share_recv.at[at], mate))

    def summed(kind, cut):
        value = gathered_sum(0, kind, cut)
        for way in (UP, DOWN):
            rings[way, kind, 1, cut].wait_recv()
            value = value + ring_in[kind][way, 0, cut].astype(jnp.float32)
        last = last_of[kind]
        last[0, cut] = value.astype(jnp.bfloat16)
        at = (kind, cut)
        lasts[at] = send(last.at[0, cut], last.at[1, cut], last_send.at[at], last_recv.at[at], across)
        if kind == EDGE:
            share(0, edge_at, edge, cut, last[0, cut].astype(jnp.float32))

    def shared(kind, cut):
        lasts[kind, cut].wait_recv()
        value = last_of[kind][1, cut].astype(jnp.float32)
        if kind == EDGE:
            share(1, other_at, edge, cut, value)
        else:
            share(2, edge, middle, cut, last_of[kind][0, cut].astype(jnp.float32) + value)

    def cotangent_views():
        halo_once(1)
        wide[...] = jnp.zeros_like(wide)
        inner = jnp.where(tm < tm_size - 1, 1.0, 0.0).astype(jnp.float32)
        for frame in range(frames_out + 1):
            if frame < frames_out:
                piece = cot_ref[frame * area : (frame + 1) * area, :].astype(jnp.float32)
            else:
                piece = next_cot[...].astype(jnp.float32) * inner
            wide[frame, 0:half_rows, 0:half_cols, :] = piece.reshape(half_rows, half_cols, channels)
        for dt in range(2):
            for dr in range(2):
                for dc in range(2):
                    piece = wide[dt : dt + frames_out, dr : dr + half_rows, dc : dc + half_cols, :]
                    views[4 * dt + 2 * dr + dc] = piece.reshape(count, channels).astype(jnp.bfloat16)

    def weights():
        for copy in mates:
            copy.wait_recv()

    def weight_rows(start, size):
        return jnp.concatenate([full_weight[half, start : start + size, :] for half in range(2)], axis=1)

    times = (((2, 0), (0, 1)), ((1, 1),))
    spaces = (((1, 0),), ((2, 0), (0, 1)))

    def hidden_part(part):
        part_t, part_r, part_c = part // 4, part // 2 % 2, part % 2
        total = jnp.zeros((count, channels), jnp.float32)
        for step_t, dt in times[part_t]:
            for step_r, dr in spaces[part_r]:
                for step_c, dc in spaces[part_c]:
                    tap = 9 * step_t + 3 * step_r + step_c
                    total += lax.dot_general(
                        views[4 * dt + 2 * dr + dc],
                        weight_rows(tap * channels, channels),
                        (((1,), (1,)), ((), ())),
                        preferred_element_type=jnp.float32,
                    )
        total = total.reshape(frames_out, half_rows, half_cols, channels)
        for frame in range(frames_out):
            for lane in range(lanes):
                spread[
                    lane, 2 * frame + part_t, :, part_r, pl.ds(part_c, half_cols, 2), :
                ] = total[frame, :, :, lane * 128 : (lane + 1) * 128]

    quarter = frames * half_rows // 4

    def back(part):
        mean, inv_std = state["norm"]

        def back_rows(index, sums):
            frame, row = index // half_rows, index % half_rows
            normed = (clip_ref[frame, row].astype(jnp.float32) - mean) * inv_std
            preact = normed * gain + bias
            sig = 1.0 / (1.0 + jnp.exp(-preact))
            slope = sig * (1.0 + preact * (1.0 - sig))
            hidden_grad = jnp.concatenate([spread[lane, frame, row] for lane in range(lanes)], axis=-1)
            value = hidden_grad * frame_mask(frame) * slope * gain
            for lane in range(lanes):
                spread[lane, frame, row] = value[:, :, lane * 128 : (lane + 1) * 128]
            return sums[0] + fold(value), sums[1] + fold(value * normed)

        sums = state.get("sums", (zero, zero))
        state["sums"] = lax.fori_loop(
            0, quarter, lambda step, sums: back_rows(part * quarter + step, sums), sums, unroll=4
        )

    def back_exchange():
        state["finish"] = exchange(state["sums"], back_in, 1)

    deep = 9 * channels

    def output_part(step):
        total = jnp.dot(
            patches[:, step * deep : (step + 1) * deep],
            weight_rows(step * deep, deep),
            preferred_element_type=jnp.float32,
        )
        done = state.get("outs", 0)
        if done > 0:
            total += out_sum[...]
        if done == 2:
            out_ref[...] = total.astype(jnp.bfloat16)
        else:
            out_sum[...] = total
        state["outs"] = done + 1

    def back_finish():
        total = state["finish"]()
        state["back"] = total[0:1] / entries, total[1:2] / entries

    def input_part(part):
        mean, inv_std = state["norm"]
        back_first, back_second = state["back"]

        def input_rows(index, _):
            frame, row = index // half_rows, index % half_rows
            normed = (clip_ref[frame, row].astype(jnp.float32) - mean) * inv_std
            value = jnp.concatenate([spread[lane, frame, row] for lane in range(lanes)], axis=-1)
            input_grad_ref[frame, row] = (
                frame_mask(frame) * inv_std * (value - back_first - normed * back_second)
            ).astype(jnp.bfloat16)
            return 0

        lax.fori_loop(0, quarter, lambda step, _: input_rows(part * quarter + step, 0), 0, unroll=4)

    def result():
        for copy in shares:
            copy.wait_recv()
        weight_grad_ref[:, half_lane] = share_out[...]
        weight_grad_ref[:, other_lane] = share_in[...]

    steps = {
        "m": moments, "s": statistics, "p": patch, "t": taps, "g": gathered, "x": crossed, "f": fold_over,
        "r": gradient, "u": summed, "h": shared, "v": cotangent_views, "w": weights, "d": hidden_part,
        "b": back, "e": back_exchange, "o": output_part, "z": back_finish, "i": input_part, "y": result,
    }
    for name, *where in order:
        steps[name](*where)
    for copy in pending:
        copy.wait_send()


def ring_shards(dp_size, tm_size, clips, frame_counts, weight, gain, bias, cotangent):
    clip_data, cot_block = clips[0], cotangent[0]
    frame_count, row_count, col_count, channels = clip_data.shape
    frames_out, rows_out, cols_out = cot_block.shape[:3]
    area = rows_out * cols_out
    count = frames_out * area
    split = (frame_count, row_count // 2, 2, col_count, channels)
    rows_w = weight.shape[0]
    rows = dp_size * rows_w
    lanes = channels // 128
    gather_edge, gather_cuts, edge, cuts, _ = PLAN
    middle = rows_w - 2 * edge
    reach = dp_size // 2
    window = (rows_w + 96 + 127) // 128 * 128
    dma = pltpu.SemaphoreType.DMA
    f32, bf16 = jnp.float32, jnp.bfloat16
    pairs = [
        (2, 2, reach, gather_cuts), (2, reach, gather_cuts), (2, 3, reach), (dp_size,), (dp_size, cuts),
        (2, 2, reach, cuts), (2, cuts), (3, cuts),
    ]
    output, input_grad, weight_grad = pl.pallas_call(
        functools.partial(ring_kernel, dp_size, tm_size, PLAN, channels // GROUPS),
        out_shape=(
            pltpu.VMEM((count, channels), bf16),
            pltpu.VMEM(split, bf16),
            pltpu.VMEM((rows_w, channels), f32),
        ),
        in_specs=[SMEM] + [VMEM] * 2 + [HBM] * 3,
        out_specs=(VMEM, VMEM, VMEM),
        scratch_shapes=[
            pltpu.VMEM(split, bf16),
            pltpu.VMEM((count, channels), bf16),
            pltpu.VMEM((count, channels), f32),
            pltpu.VMEM((2,) + split[1:], bf16),
            pltpu.VMEM((area, channels), bf16),
            pltpu.VMEM((2, rows, 128), bf16),
            pltpu.VMEM((count, rows + 128), bf16),
            pltpu.VMEM((count, channels), bf16),
            pltpu.VMEM((dp_size, window, 128), f32),
            pltpu.VMEM((dp_size, window, 128), bf16),
            pltpu.VMEM((dp_size, window, 128), bf16),
            pltpu.VMEM((dp_size, cuts, edge // cuts, 128), bf16),
            pltpu.VMEM((dp_size, cuts, edge // cuts, 128), bf16),
            pltpu.VMEM((2, reach, cuts, edge // cuts, 128), bf16),
            pltpu.VMEM((2, reach, cuts, edge // cuts, 128), bf16),
            pltpu.VMEM((2, reach, cuts, middle // cuts, 128), bf16),
            pltpu.VMEM((2, reach, cuts, middle // cuts, 128), bf16),
            pltpu.VMEM((2, cuts, edge // cuts, 128), bf16),
            pltpu.VMEM((2, cuts, middle // cuts, 128), bf16),
            pltpu.VMEM((rows_w, 128), f32),
            pltpu.VMEM((rows_w, 128), f32),
            pltpu.VMEM((lanes, rows_out + 1, 2, col_count + 8, 128), f32),
            pltpu.VMEM((frames_out + 1, rows_out + 1, 16, channels), f32),
            pltpu.VMEM((8, count, channels), bf16),
            pltpu.VMEM((lanes,) + split[:-1] + (128,), f32),
            pltpu.VMEM((tm_size, 8, channels), f32),
            pltpu.VMEM((tm_size, 8, channels), f32),
        ]
        + [dma((2,))] * 2
        + [dma((2, tm_size))] * 2
        + [dma((2,)), dma((frame_count + 1,))]
        + [dma(shape) for shape in pairs for _ in range(2)],
        compiler_params=pltpu.CompilerParams(
            collective_id=0, has_side_effects=True, vmem_limit_bytes=RING_VMEM
        ),
    )(frame_counts, gain[None], bias[None], clip_data.reshape(split), cot_block.reshape(count, channels), weight)
    output, input_grad, weight_grad = settled(output, input_grad, weight_grad)
    return (
        output.reshape(cot_block.shape)[None],
        input_grad.reshape(clip_data.shape)[None],
        weight_grad,
    )


def copy_kernel(*refs):
    count = len(refs) // 2
    sems = refs[-1]
    copies = []
    for index in range(count):
        size = refs[index].shape[0] // COPY_PARTS
        for part in range(COPY_PARTS):
            span = pl.ds(part * size, size)
            copies.append(
                pltpu.make_async_copy(refs[index].at[span], refs[count + index].at[span], sems.at[len(copies)])
            )
            copies[-1].start()
    for copy in copies:
        copy.wait()


def settled(*arrays):
    sems = pltpu.SemaphoreType.DMA((COPY_PARTS * len(arrays),))
    return pl.pallas_call(
        copy_kernel,
        out_shape=tuple(jax.ShapeDtypeStruct(array.shape, array.dtype) for array in arrays),
        in_specs=[VMEM] * len(arrays),
        out_specs=(HBM,) * len(arrays),
        scratch_shapes=[sems],
        compiler_params=pltpu.CompilerParams(vmem_limit_bytes=COPY_VMEM),
    )(*arrays)


def by_ring(dp_size, tm_size, weight_rows):
    return dp_size == 8 and tm_size == 4 and weight_rows == 864


def device_part(dp_size, tm_size, *arrays):
    chosen = ring_shards if by_ring(dp_size, tm_size, arrays[2].shape[0]) else shards
    return chosen(dp_size, tm_size, *arrays)


def solution(mesh):
    placed = (
        P("dp", "tm", None, None, None),
        P("dp"),
        P("dp", None),
        P(),
        P(),
        P("dp", "tm", None, None, None),
    )
    return jax.shard_map(
        functools.partial(device_part, mesh.shape["dp"], mesh.shape["tm"]),
        mesh=mesh,
        in_specs=placed,
        out_specs=(P("dp", "tm", None, None, None), P("dp", "tm", None, None, None), P("dp", None)),
        check_vma=False,
    )
```

```python
import functools

import jax
import jax.numpy as jnp
from jax import lax
from jax.experimental import pallas as pl
from jax.experimental.pallas import tpu as pltpu
from jax.sharding import PartitionSpec as P

GROUPS = 32
EPS = 1e-06
PARTS = 3
MESH = pl.DeviceIdType.MESH
VMEM = pl.BlockSpec(memory_space=pltpu.VMEM)
SMEM = pl.BlockSpec(memory_space=pltpu.SMEM)


def plan(dp_size, tm_size):
    dp_bits = [("dp", k) for k in range(dp_size.bit_length() - 1)]
    tm_bits = [("tm", k) for k in range(tm_size.bit_length() - 1)]
    cut = len(dp_bits) // 2
    ways = [tm_bits[1:], dp_bits[:cut], dp_bits[cut:]]
    orders = []
    for part in range(PARTS):
        turned = ways[part:] + ways[:part]
        orders.append(tm_bits[:1] + turned[0] + turned[1] + turned[2])
    return dp_bits[::-1] + tm_bits[::-1], orders


def lane_group_sum(value, width):
    channels = value.shape[-1]
    lane = lax.broadcasted_iota(jnp.int32, value.shape, value.ndim - 1)
    step = 1
    while step < width:
        above = pltpu.roll(value, channels - step, value.ndim - 1)
        below = pltpu.roll(value, step, value.ndim - 1)
        value = value + jnp.where((lane // step) % 2 == 0, above, below)
        step *= 2
    return value


def block_kernel(
    labels, orders, dp_size, tm_size, near, width_g,
    valid_ref, params_ref, clip_ref, cot_ref, weight_ref,
    out_ref, input_grad_ref, weight_grad_ref,
    earlier, next_cot, full_weight, patches, grads, held, wide, views, spread, shared, sums_in, back_in,
    *scratch,
):
    frames, half_rows, _, cols, channels = clip_ref.shape
    frames_out, half_cols, lanes = frames // 2, cols // 2, channels // 128
    area = half_rows * half_cols
    count = frames_out * area
    depth = len(labels)
    sends, receives, kept = (scratch[i * depth : (i + 1) * depth] for i in range(3))
    (send_sem, recv_sem, share_send, share_recv, ring_send, ring_recv, sum_send, sum_recv,
     far_send, far_recv, near_send, near_recv, mate_send, mate_recv, cross_send, cross_recv, own_sem) = scratch[3 * depth :]
    dp, tm = lax.axis_index("dp"), lax.axis_index("tm")
    place = {"dp": dp, "tm": tm}
    far_size = dp_size // near
    far_at, near_at = dp // near, dp % near
    core = tm % 2
    mate = {"tm": tm + 1 - 2 * core}

    def bit_of(label):
        return (place[label[0]] // 2 ** label[1]) % 2

    def partner(label):
        return {label[0]: place[label[0]] + (1 - 2 * bit_of(label)) * 2 ** label[1]}

    def send(source, target, sem_out, sem_in, device):
        copy = pltpu.make_async_remote_copy(
            src_ref=source, dst_ref=target, send_sem=sem_out, recv_sem=sem_in,
            device_id=device, device_id_type=MESH,
        )
        copy.start()
        return copy

    barrier = pltpu.get_barrier_semaphore()
    greeted = [{"tm": (tm + step) % tm_size} for step in range(1, tm_size)]
    greeted += [{"dp": dp_index} for dp_index in dp_peers(dp, dp_size, near)]
    for device in greeted:
        pl.semaphore_signal(barrier, inc=1, device_id=device, device_id_type=MESH)
    pl.semaphore_wait(barrier, len(greeted))

    ring = [
        send(clip_ref.at[frames - 2 : frames], earlier, ring_send.at[0], ring_recv.at[0], {"tm": (tm + 1) % tm_size}),
        send(cot_ref.at[0:area], next_cot, ring_send.at[1], ring_recv.at[1], {"tm": (tm + tm_size - 1) % tm_size}),
    ]

    rows_w = weight_ref.shape[0]
    half_lane = pl.ds(pl.multiple_of(core * 128, 128), 128)

    crossed = tm_size == 4 and rows_w % 48 == 0
    rows_x = rows_w // 3 if crossed else 0
    span_w = rows_w - rows_x
    across = (tm // 2) % 2 if crossed else 0
    cross_mate = {"tm": (tm + 2) % tm_size}
    span_at = across * rows_x

    def rows_of(index, start, size):
        return full_weight.at[pl.ds(pl.multiple_of(index * rows_w + start, 8), size), half_lane]

    def block_at(index):
        return rows_of(index, span_at, span_w)

    own_copy = pltpu.make_async_copy(
        weight_ref, full_weight.at[pl.ds(pl.multiple_of(dp * rows_w, 8), rows_w), :], own_sem
    )
    own_copy.start()
    own_half = weight_ref.at[pl.ds(pl.multiple_of(span_at, 8), span_w), half_lane]
    far_copies = [
        send(own_half, block_at(dp), far_send.at[step], far_recv.at[step],
             {"dp": ((far_at + step) % far_size) * near + near_at})
        for step in range(1, far_size)
    ]
    near_copies, mate_copies, cross_copies = {}, [], []

    def send_near(step, source, index):
        for hop in range(1, near):
            near_copies[step, hop] = send(
                source, block_at(index), near_send.at[step, hop], near_recv.at[step, hop],
                {"dp": far_at * near + (near_at + hop) % near},
            )

    def send_mate(step, hop, index):
        if crossed:
            cross = rows_of(index, across * (span_w), rows_x)
            copy = send(cross, cross, cross_send.at[step, hop], cross_recv.at[step, hop], cross_mate)
            cross_copies.append((copy, step, hop, index))
        mate_copies.append(
            send(block_at(index), block_at(index), mate_send.at[0, step, hop], mate_recv.at[0, step, hop], mate)
        )

    def weight_cross():
        for copy, step, hop, index in cross_copies:
            copy.wait_recv()
            rest = rows_of(index, (1 - across) * span_w, rows_x)
            mate_copies.append(
                send(rest, rest, mate_send.at[1, step, hop], mate_recv.at[1, step, hop], mate)
            )

    send_near(0, own_half, dp)

    def weight_far(step):
        far_copies[step - 1].wait_recv()
        index = ((far_at + far_size - step) % far_size) * near + near_at
        send_near(step, block_at(index), index)
        send_mate(step, 0, index)

    def weight_near(step):
        for hop in range(1, near):
            near_copies[step, hop].wait_recv()
            index = ((far_at + far_size - step) % far_size) * near + (near_at + near - hop) % near
            send_mate(step, hop, index)

    first = tm * frames
    valid = valid_ref[0]
    gain, bias = params_ref[0:1, :], params_ref[1:2, :]
    entries = jnp.full((1, channels), valid.astype(jnp.float32)) * float(2 * half_rows * cols * width_g)
    zero = jnp.zeros((8, channels), jnp.float32)

    def fold(value):
        return jnp.sum(value.reshape(-1, 8, channels), axis=0)

    def frame_mask(frame):
        slot = first + frame
        return jnp.where((slot >= 0) & (slot < valid), 1.0, 0.0).astype(jnp.float32)

    def moment_rows(index, sums):
        frame, row = index // half_rows, index % half_rows
        values = clip_ref[frame, row].astype(jnp.float32)
        masked = values * frame_mask(frame)
        return sums[0] + fold(masked), sums[1] + fold(masked * values)

    def exchange(sums, buffer, sems):
        pair = [jnp.sum(value, axis=0, keepdims=True) for value in sums]
        buffer[tm] = jnp.concatenate(pair + [jnp.zeros((6, channels), jnp.float32)], axis=0)
        copies = [
            send(buffer.at[tm], buffer.at[tm], sum_send.at[sems, step], sum_recv.at[sems, step],
                 {"tm": (tm + step) % tm_size})
            for step in range(1, tm_size)
        ]

        def finish():
            for copy in copies:
                copy.wait()
            total = buffer[0]
            for index in range(1, tm_size):
                total = total + buffer[index]
            return lane_group_sum(total, width_g)

        return finish

    finish = exchange(lax.fori_loop(0, frames * half_rows, moment_rows, (zero, zero), unroll=4), sums_in, 0)
    held[...] = jnp.zeros_like(held)
    total = finish()
    mean = total[0:1] / entries
    inv_std = lax.rsqrt(total[1:2] / entries - mean * mean + EPS)
    for copy in ring:
        copy.wait()

    ticks = [functools.partial(weight_far, step) for step in range(1, far_size)]
    for frame in range(frames + 1):
        source = earlier.at[frame] if frame < 2 else clip_ref.at[frame - 2]
        mask = frame_mask(frame - 2)

        def rows(index, _):
            values = source[index].astype(jnp.float32)
            preact = (values - mean) * inv_std * gain + bias
            hidden = preact / (1.0 + jnp.exp(-preact)) * mask
            for lane in range(lanes):
                part = hidden[:, :, lane * 128 : (lane + 1) * 128]
                held[lane, index, 1, 8 : 8 + cols, :] = part[0]
                held[lane, index + 1, 0, 8 : 8 + cols, :] = part[1]
            return 0

        lax.fori_loop(0, half_rows, rows, 0, unroll=4)
        for step_r in range(3):
            for step_c in range(3):
                pieces = [
                    held[
                        lane,
                        step_r // 2 : step_r // 2 + half_rows,
                        step_r % 2,
                        pl.ds(7 + step_c, half_cols, 2),
                        :,
                    ].reshape(area, 128)
                    for lane in range(lanes)
                ]
                piece = jnp.concatenate(pieces, axis=1).astype(jnp.bfloat16)
                for step_t in range(3):
                    if (frame - step_t) % 2 == 0 and 0 <= frame - step_t < frames:
                        at = (frame - step_t) // 2
                        tap = 9 * step_t + 3 * step_r + step_c
                        patches[at * area : (at + 1) * area, tap * channels : (tap + 1) * channels] = piece
        if frame % 3 == 2 and ticks:
            ticks.pop(0)()

    def tap_grad(tap, _):
        at = pl.multiple_of(tap * channels, channels)
        grads[pl.ds(at, channels), :] = lax.dot_general(
            patches[:, pl.ds(at, channels)],
            cot_ref[...],
            (((0,), (0,)), ((), ())),
            preferred_element_type=jnp.float32,
        )
        return 0

    for tick in ticks:
        tick()
    weight_near(0)
    lax.fori_loop(0, 27, tap_grad, 0)

    left = [list(labels) for _ in range(PARTS)]
    copies = [[None] * depth for _ in range(PARTS)]
    piece_rows = grads.shape[0] // (dp_size * tm_size * PARTS)

    def index_of(stride, number, bit):
        return (number // stride) * (2 * stride) + bit * stride + number % stride

    def read(stage, part, index):
        if stage == 0:
            at = (index * PARTS + part) * piece_rows
            if piece_rows % 8 == 0:
                return grads[pl.ds(pl.multiple_of(at, 8), piece_rows), :]
            window = (piece_rows + 14) // 8 * 8
            block = grads[pl.ds(pl.multiple_of(at // 8 * 8, 8), window), :]
            return pltpu.roll(block, (window - at % 8) % window, 0)[:piece_rows]
        return kept[stage - 1][part, index]

    def add(stage, part):
        label = orders[part][stage]
        stride = 2 ** (len(left[part]) - 1 - left[part].index(label))
        number = 2 ** (len(left[part]) - 1)
        copies[part][stage].wait_recv()

        def one(block, _):
            kept[stage][part, block] = read(
                stage, part, index_of(stride, block, bit_of(label))
            ) + receives[stage][part, block].astype(jnp.float32)
            return 0

        lax.fori_loop(0, number, one, 0)
        left[part].remove(label)

    def halve(stage):
        for part in range(PARTS):
            if stage > 0:
                add(stage - 1, part)
            label = orders[part][stage]
            stride = 2 ** (len(left[part]) - 1 - left[part].index(label))
            number = 2 ** (len(left[part]) - 1)

            def pack(block, _):
                sends[stage][part, block] = read(
                    stage, part, index_of(stride, block, 1 - bit_of(label))
                ).astype(jnp.bfloat16)
                return 0

            lax.fori_loop(0, number, pack, 0)
            copies[part][stage] = send(
                sends[stage].at[part], receives[stage].at[part],
                send_sem.at[part, stage], recv_sem.at[part, stage], partner(label),
            )

    halve(0)
    for step in range(1, far_size):
        weight_near(step)
    halve(1)
    weight_cross()
    for copy in mate_copies:
        copy.wait_recv()
    own_copy.wait()
    total = jnp.zeros((count, channels), jnp.float32)
    deep = 9 * channels
    for step in range(3):
        total += jnp.dot(
            patches[:, step * deep : (step + 1) * deep],
            full_weight[step * deep : (step + 1) * deep, :],
            preferred_element_type=jnp.float32,
        )
    out_ref[...] = total.astype(jnp.bfloat16)
    wide[...] = jnp.zeros_like(wide)
    last = jnp.where(tm < tm_size - 1, 1.0, 0.0).astype(jnp.float32)
    for frame in range(frames_out + 1):
        if frame < frames_out:
            piece = cot_ref[frame * area : (frame + 1) * area, :].astype(jnp.float32)
        else:
            piece = next_cot[...].astype(jnp.float32) * last
        wide[frame, 0:half_rows, 0:half_cols, :] = piece.reshape(half_rows, half_cols, channels)
    for dt in range(2):
        for dr in range(2):
            for dc in range(2):
                piece = wide[dt : dt + frames_out, dr : dr + half_rows, dc : dc + half_cols, :]
                views[4 * dt + 2 * dr + dc] = piece.reshape(count, channels).astype(jnp.bfloat16)
    times = (((2, 0), (0, 1)), ((1, 1),))
    spaces = (((1, 0),), ((2, 0), (0, 1)))
    stage = 2
    for part_t in range(2):
        for part_r in range(2):
            for part_c in range(2):
                total = jnp.zeros((count, channels), jnp.float32)
                for step_t, dt in times[part_t]:
                    for step_r, dr in spaces[part_r]:
                        for step_c, dc in spaces[part_c]:
                            tap = 9 * step_t + 3 * step_r + step_c
                            total += lax.dot_general(
                                views[4 * dt + 2 * dr + dc],
                                full_weight[tap * channels : (tap + 1) * channels, :],
                                (((1,), (1,)), ((), ())),
                                preferred_element_type=jnp.float32,
                            )
                total = total.reshape(frames_out, half_rows, half_cols, channels)
                for frame in range(frames_out):
                    for lane in range(lanes):
                        spread[
                            lane, 2 * frame + part_t, :, part_r, pl.ds(part_c, half_cols, 2), :
                        ] = total[frame, :, :, lane * 128 : (lane + 1) * 128]
    halve(stage)

    def back_rows(index, sums):
        frame, row = index // half_rows, index % half_rows
        normed = (clip_ref[frame, row].astype(jnp.float32) - mean) * inv_std
        preact = normed * gain + bias
        sig = 1.0 / (1.0 + jnp.exp(-preact))
        slope = sig * (1.0 + preact * (1.0 - sig))
        hidden_grad = jnp.concatenate([spread[lane, frame, row] for lane in range(lanes)], axis=-1)
        value = hidden_grad * frame_mask(frame) * slope * gain
        for lane in range(lanes):
            spread[lane, frame, row] = value[:, :, lane * 128 : (lane + 1) * 128]
        return sums[0] + fold(value), sums[1] + fold(value * normed)

    finish = exchange(lax.fori_loop(0, frames * half_rows, back_rows, (zero, zero), unroll=4), back_in, 1)
    for stage in range(3, depth):
        halve(stage)
    for part in range(PARTS):
        add(depth - 1, part)
        shared[tm, part] = kept[depth - 1][part, 0].astype(jnp.bfloat16)

    tm_bits = [label for label in labels if label[0] == "tm"]
    shares, serial = [], 0
    for label in tm_bits:
        span = 2 ** (label[1] + 1)
        stage_shares = []
        for high in range(tm_size // span):
            block = high * span + tm % span
            stage_shares.append(
                send(shared.at[block], shared.at[block],
                     share_send.at[serial], share_recv.at[serial], partner(label))
            )
            serial += 1
        if label == tm_bits[0]:
            total = finish()
            back_first, back_second = total[0:1] / entries, total[1:2] / entries

            def input_rows(index, _):
                frame, row = index // half_rows, index % half_rows
                normed = (clip_ref[frame, row].astype(jnp.float32) - mean) * inv_std
                value = jnp.concatenate([spread[lane, frame, row] for lane in range(lanes)], axis=-1)
                input_grad_ref[frame, row] = (
                    frame_mask(frame) * inv_std * (value - back_first - normed * back_second)
                ).astype(jnp.bfloat16)
                return 0

            lax.fori_loop(0, frames * half_rows, input_rows, 0, unroll=4)
        for share in stage_shares:
            share.wait_recv()
        shares += stage_shares
    for block in range(tm_size):
        weight_grad_ref[block] = shared[block].astype(jnp.float32)
    for copy in shares + far_copies + list(near_copies.values()) + mate_copies + [item[0] for item in cross_copies]:
        copy.wait_send()
    for part in range(PARTS):
        for copy in copies[part]:
            copy.wait_send()


def dp_peers(dp, dp_size, near):
    far_at, near_at, far_size = dp // near, dp % near, dp_size // near
    peers = [((far_at + step) % far_size) * near + near_at for step in range(1, far_size)]
    return peers + [far_at * near + (near_at + hop) % near for hop in range(1, near)]


def shards(dp_size, tm_size, clips, frame_counts, weight, gain, bias, cotangent):
    clip_data, cot_block = clips[0], cotangent[0]
    frame_count, row_count, col_count, channels = clip_data.shape
    frames_out, rows_out, cols_out = cot_block.shape[:3]
    area = rows_out * cols_out
    count = frames_out * area
    split = (frame_count, row_count // 2, 2, col_count, channels)
    labels, orders = plan(dp_size, tm_size)
    depth = len(labels)
    rows = dp_size * weight.shape[0]
    piece = rows // (dp_size * tm_size * PARTS)
    halves = [(PARTS, 2 ** (depth - 1 - stage), piece, channels) for stage in range(depth)]
    near = 2 ** ((dp_size.bit_length() - 1) // 2)
    far = dp_size // near
    lanes = channels // 128
    dma = pltpu.SemaphoreType.DMA
    f32, bf16 = jnp.float32, jnp.bfloat16
    output, input_grad, weight_grad = pl.pallas_call(
        functools.partial(block_kernel, labels, orders, dp_size, tm_size, near, channels // GROUPS),
        out_shape=(
            jax.ShapeDtypeStruct((count, channels), bf16),
            jax.ShapeDtypeStruct(split, bf16),
            jax.ShapeDtypeStruct((tm_size, PARTS, piece, channels), f32),
        ),
        in_specs=[SMEM] + [VMEM] * 4,
        out_specs=(VMEM, VMEM, VMEM),
        scratch_shapes=[
            pltpu.VMEM((2,) + split[1:], bf16),
            pltpu.VMEM((area, channels), bf16),
            pltpu.VMEM((rows, channels), bf16),
            pltpu.VMEM((count, rows), bf16),
            pltpu.VMEM((rows, channels), f32),
            pltpu.VMEM((lanes, rows_out + 1, 2, col_count + 8, 128), f32),
            pltpu.VMEM((frames_out + 1, rows_out + 1, 16, channels), f32),
            pltpu.VMEM((8, count, channels), bf16),
            pltpu.VMEM((lanes,) + split[:-1] + (128,), f32),
            pltpu.VMEM((tm_size, PARTS, piece, channels), bf16),
            pltpu.VMEM((tm_size, 8, channels), f32),
            pltpu.VMEM((tm_size, 8, channels), f32),
        ]
        + [pltpu.VMEM(shape, bf16) for shape in halves] * 2
        + [pltpu.VMEM(shape, f32) for shape in halves]
        + [dma((PARTS, depth))] * 2
        + [dma((tm_size,))] * 2
        + [dma((2,))] * 2
        + [dma((2, tm_size))] * 2
        + [dma((far,))] * 2
        + [dma((far, near))] * 2
        + [dma((2, far, near))] * 2
        + [dma((far, near))] * 2
        + [dma(())],
        compiler_params=pltpu.CompilerParams(
            collective_id=0, has_side_effects=True, vmem_limit_bytes=56 * 2**20
        ),
    )(frame_counts, jnp.stack([gain, bias]), clip_data.reshape(split), cot_block.reshape(count, channels), weight)
    return (
        output.reshape(cot_block.shape)[None],
        input_grad.reshape(clip_data.shape)[None],
        weight_grad.reshape(weight.shape),
    )


HBM = pl.BlockSpec(memory_space=pl.ANY)
UP, DOWN = 0, 1
EDGE, MIDDLE = 0, 1
SIGN = (1, -1)
COPY_PARTS = 2
RING_VMEM = 54 * 2**20
COPY_VMEM = 16 * 2**20
ORDER = (
    ("m",), ("s",), ("p", 0), ("p", 2), ("p", 4), ("p", 5), ("g", 1, 0, 1, 0), ("g", 0, 0, 1, 0),
    ("g", 1, 0, 1, 1), ("p", 1), ("g", 0, 1, 1, 0), ("g", 1, 1, 1, 0), ("p", 6), ("g", 0, 1, 1, 1),
    ("g", 1, 1, 1, 1), ("g", 0, 0, 1, 1), ("p", 3), ("p", 7), ("p", 8), ("t", 0), ("t", 1), ("t", 2),
    ("g", 0, 0, 2, 0), ("g", 1, 0, 2, 0), ("t", 3), ("g", 0, 1, 2, 0), ("t", 4), ("g", 1, 0, 2, 1), ("t", 5),
    ("g", 1, 1, 2, 0), ("g", 0, 1, 2, 1), ("t", 6), ("t", 7), ("v",), ("g", 1, 1, 2, 1), ("g", 0, 0, 2, 1),
    ("g", 1, 0, 3, 0), ("r", 0, 1, 4, 0), ("f", 4, 0), ("r", 1, 1, 3, 0), ("f", 3, 0), ("g", 0, 0, 3, 0),
    ("g", 0, 0, 3, 1), ("f", 5, 0), ("x", 0, 2, 0), ("x", 0, 1, 0), ("x", 1, 1, 0), ("g", 1, 0, 3, 1),
    ("g", 0, 1, 3, 0), ("g", 1, 1, 3, 0), ("x", 1, 2, 0), ("g", 0, 1, 3, 1), ("r", 1, 0, 4, 0), ("f", 2, 0),
    ("r", 0, 1, 3, 0), ("x", 0, 3, 0), ("g", 0, 0, 4, 0), ("g", 1, 1, 3, 1), ("x", 0, 1, 1), ("g", 0, 0, 4, 1),
    ("r", 0, 0, 3, 0), ("f", 6, 0), ("x", 1, 3, 0), ("g", 1, 1, 4, 0), ("r", 1, 0, 3, 0), ("x", 1, 2, 1),
    ("r", 1, 1, 2, 0), ("x", 0, 3, 1), ("r", 0, 1, 2, 0), ("f", 1, 0), ("x", 0, 2, 1), ("g", 1, 1, 4, 1),
    ("x", 0, 4, 0), ("x", 1, 3, 1), ("r", 0, 0, 2, 0), ("f", 7, 0), ("f", 0, 0), ("x", 1, 1, 1), ("x", 0, 4, 1),
    ("r", 1, 0, 2, 0), ("r", 1, 1, 1, 0), ("w",), ("r", 0, 1, 1, 0), ("d", 3), ("d", 2), ("d", 0), ("d", 4),
    ("d", 6), ("r", 0, 0, 1, 0), ("d", 7), ("r", 1, 0, 1, 0), ("d", 1), ("d", 5), ("b", 2), ("b", 1), ("b", 3),
    ("u", 1, 0), ("o", 2), ("b", 0), ("e",), ("u", 0, 0), ("o", 0), ("o", 1), ("h", 1, 0), ("z",), ("i", 1),
    ("h", 0, 0), ("i", 0), ("i", 3), ("i", 2), ("y",),
)
PLAN = (224, 2, 208, 1, ORDER)


def ring_kernel(
    dp_size, tm_size, plan, width_g,
    valid_ref, gain_ref, bias_ref, clip_hbm, cot_hbm, weight_hbm,
    out_ref, input_grad_ref, weight_grad_ref,
    clip_ref, cot_ref, out_sum, earlier, next_cot, full_weight, patches, turned, grads, mate_out, mate_in,
    fold_out, fold_in, edge_out, edge_in, middle_out, middle_in,
    last_edge, last_middle, share_out, share_in,
    held, wide, views, spread, sums_in, back_in,
    halo_send, halo_recv, sum_send, sum_recv, own_sem, load_sem,
    gather_send, gather_recv, cross_send, cross_recv, copy_send, copy_recv,
    mate_send, mate_recv, fold_send, fold_recv, ring_send, ring_recv,
    last_send, last_recv, share_send, share_recv,
):
    frames, half_rows, _, cols, channels = clip_ref.shape
    frames_out, half_cols, lanes = frames // 2, cols // 2, channels // 128
    area = half_rows * half_cols
    count = frames_out * area
    window, rows_all = grads.shape[1], full_weight.shape[1]
    rows_w = weight_hbm.shape[0]
    gather_edge, gather_cuts, edge, cuts, order = plan
    gather_middle, middle = rows_w - 2 * gather_edge, rows_w - 2 * edge
    dp, tm = lax.axis_index("dp"), lax.axis_index("tm")
    core, side = tm % 2, tm // 2
    mate = {"tm": tm + 1 - 2 * core}
    across = {"tm": (tm + 2) % tm_size}
    far_size, reach = dp_size // 2, dp_size // 2
    pos = dp // 2 + (dp % 2) * (2 * far_size - 1 - 2 * (dp // 2))

    def dp_at(place):
        place = (place + 2 * dp_size) % dp_size
        turn = place // far_size
        return 2 * (place + turn * (2 * far_size - 1 - 2 * place)) + turn

    onward = [{"dp": dp_at(pos + sign)} for sign in SIGN]
    pending = []

    def send(source, target, sem_out, sem_in, device):
        copy = pltpu.make_async_remote_copy(
            src_ref=source, dst_ref=target, send_sem=sem_out, recv_sem=sem_in,
            device_id=device, device_id_type=MESH,
        )
        copy.start()
        pending.append(copy)
        return copy

    barrier = pltpu.get_barrier_semaphore()
    greeted = [{"tm": (tm + step) % tm_size} for step in range(1, tm_size)] + onward
    for device in greeted:
        pl.semaphore_signal(barrier, inc=1, device_id=device, device_id_type=MESH)

    half_lane = pl.ds(pl.multiple_of(core * 128, 128), 128)
    other_lane = pl.ds(pl.multiple_of((1 - core) * 128, 128), 128)

    def planes(edge, middle):
        return side * (edge + middle), (1 - side) * (edge + middle)

    gather_at, gather_other = planes(gather_edge, gather_middle)
    gather_spans = ((gather_at, gather_edge), (gather_edge, gather_middle))

    def piece_of(start, size, cuts, cut):
        return start + cut * (size // cuts), size // cuts

    def rows_at(block, start, size):
        return pl.ds(pl.multiple_of(block * rows_w + start, 16), size)

    def region(block, start, size):
        return full_weight.at[core, rows_at(block, start, size)]

    gather_last = ((reach, reach - 1), (reach - 1, reach))
    gathers, crosses, mates = {}, {}, []

    def gather(way, kind, step, cut):
        start, size = piece_of(*gather_spans[kind], gather_cuts, cut)
        target = region(dp_at(pos - SIGN[way] * (step - 1)), start, size)
        at = (way, kind, step - 1, cut)
        gathers[way, kind, step, cut] = send(target, target, gather_send.at[at], gather_recv.at[at], onward[way])

    def to_mate(way, third, step, start, size):
        block = region(dp_at(pos - SIGN[way] * step), start, size)
        at = (way, third, step - 1)
        mates.append(send(block, block, copy_send.at[at], copy_recv.at[at], mate))

    def gathered(way, kind, step, cut):
        gathers[way, kind, step, cut].wait_recv()
        if step < gather_last[way][kind]:
            gather(way, kind, step + 1, cut)
        if kind == EDGE:
            start, size = piece_of(*gather_spans[kind], gather_cuts, cut)
            block = region(dp_at(pos - SIGN[way] * step), start, size)
            at = (way, step - 1, cut)
            crosses[way, step, cut] = send(block, block, cross_send.at[at], cross_recv.at[at], across)
        if cut == gather_cuts - 1:
            to_mate(way, kind, step, *gather_spans[kind])

    def crossed(way, step, cut):
        crosses[way, step, cut].wait_recv()
        if cut == gather_cuts - 1:
            to_mate(way, 2, step, gather_other, gather_edge)

    first = tm * frames
    valid = valid_ref[0]
    gain, bias = gain_ref[...], bias_ref[...]
    entries = jnp.full((1, channels), valid.astype(jnp.float32)) * float(2 * half_rows * cols * width_g)
    zero = jnp.zeros((8, channels), jnp.float32)

    def fold(value):
        return jnp.sum(value.reshape(-1, 8, channels), axis=0)

    def frame_mask(frame):
        slot = first + frame
        return jnp.where((slot >= 0) & (slot < valid), 1.0, 0.0).astype(jnp.float32)

    def moment_rows(index, sums):
        frame, row = index // half_rows, index % half_rows
        values = clip_ref[frame, row].astype(jnp.float32)
        masked = values * frame_mask(frame)
        return sums[0] + fold(masked), sums[1] + fold(masked * values)

    def exchange(sums, buffer, sems):
        pair = [jnp.sum(value, axis=0, keepdims=True) for value in sums]
        buffer[tm] = jnp.concatenate(pair + [jnp.zeros((6, channels), jnp.float32)], axis=0)
        copies = [
            send(buffer.at[tm], buffer.at[tm], sum_send.at[sems, step], sum_recv.at[sems, step],
                 {"tm": (tm + step) % tm_size})
            for step in range(1, tm_size)
        ]

        def finish():
            for copy in copies:
                copy.wait_recv()
            total = buffer[0]
            for index in range(1, tm_size):
                total = total + buffer[index]
            return lane_group_sum(total, width_g)

        return finish

    state = {}
    own_loads = [
        pltpu.make_async_copy(
            weight_hbm.at[:, half * 128 : (half + 1) * 128], full_weight.at[half, rows_at(dp, 0, rows_w)],
            own_sem.at[half],
        )
        for half in range(2)
    ]
    clip_loads = [
        pltpu.make_async_copy(clip_hbm.at[frame], clip_ref.at[frame], load_sem.at[frame]) for frame in range(frames)
    ]
    cot_load = pltpu.make_async_copy(cot_hbm, cot_ref, load_sem.at[frames])
    for copy in clip_loads + own_loads + [cot_load]:
        copy.start()

    def begin():
        for kind in (EDGE, MIDDLE):
            for cut in range(gather_cuts):
                for way in (UP, DOWN):
                    gather(way, kind, 1, cut)

    def moments():
        sums = (zero, zero)
        for frame in range(frames):
            clip_loads[frame].wait()
            sums = lax.fori_loop(
                0, half_rows, lambda step, sums: moment_rows(frame * half_rows + step, sums), sums, unroll=4
            )
        pl.semaphore_wait(barrier, len(greeted))
        state["finish"] = exchange(sums, sums_in, 0)
        for copy in own_loads:
            copy.wait()
        begin()
        cot_load.wait()
        state["halos"] = [
            send(clip_ref.at[frames - 2 : frames], earlier, halo_send.at[0], halo_recv.at[0],
                 {"tm": (tm + 1) % tm_size}),
            send(cot_ref.at[0:area], next_cot, halo_send.at[1], halo_recv.at[1],
                 {"tm": (tm + tm_size - 1) % tm_size}),
        ]
        held[...] = jnp.zeros_like(held)
        turned[:, 0:128] = cot_ref[:, half_lane]
        turned[:, 128:256] = cot_ref[:, other_lane]
        patches[:, rows_all:] = jnp.zeros((count, patches.shape[1] - rows_all), jnp.bfloat16)

    def statistics():
        total = state["finish"]()
        mean = total[0:1] / entries
        inv_std = lax.rsqrt(total[1:2] / entries - mean * mean + EPS)
        state["norm"] = mean, inv_std

    def halo_once(index):
        if index not in state:
            state[index] = True
            state["halos"][index].wait_recv()

    def patch(turn):
        frame = (turn + 2) % (frames + 1)
        if frame < 2:
            halo_once(0)
        mean, inv_std = state["norm"]
        source = earlier.at[frame] if frame < 2 else clip_ref.at[frame - 2]
        mask = frame_mask(frame - 2)

        def rows(index, _):
            values = source[index].astype(jnp.float32)
            preact = (values - mean) * inv_std * gain + bias
            hidden = preact / (1.0 + jnp.exp(-preact)) * mask
            for lane in range(lanes):
                part = hidden[:, :, lane * 128 : (lane + 1) * 128]
                held[lane, index, 1, 8 : 8 + cols, :] = part[0]
                held[lane, index + 1, 0, 8 : 8 + cols, :] = part[1]
            return 0

        lax.fori_loop(0, half_rows, rows, 0, unroll=4)
        for step_r in range(3):
            for step_c in range(3):
                pieces = [
                    held[
                        lane,
                        step_r // 2 : step_r // 2 + half_rows,
                        step_r % 2,
                        pl.ds(7 + step_c, half_cols, 2),
                        :,
                    ].reshape(area, 128)
                    for lane in range(lanes)
                ]
                piece = jnp.concatenate(pieces, axis=1).astype(jnp.bfloat16)
                for step_t in range(3):
                    if (frame - step_t) % 2 == 0 and 0 <= frame - step_t < frames:
                        at = (frame - step_t) // 2
                        tap = 9 * step_t + 3 * step_r + step_c
                        patches[at * area : (at + 1) * area, tap * channels : (tap + 1) * channels] = piece

    offsets = [reach]
    for step in range(reach - 1, 0, -1):
        offsets += [-step, step]
    offsets.append(0)
    slot_of = {offset % dp_size: slot for slot, offset in enumerate(offsets)}
    swaps = {}

    def skew_of(offset):
        return dp_at(pos + offset) * rows_w % 128

    def taps(slot):
        skew = skew_of(offsets[slot])
        start = pl.multiple_of(dp_at(pos + offsets[slot]) * rows_w - skew, 128)
        value = lax.dot_general(
            patches[:, pl.ds(start, window)],
            turned[...],
            (((0,), (0,)), ((), ())),
            preferred_element_type=jnp.float32,
        )
        grads[slot] = value[:, 0:128]
        mate_out[slot] = value[:, 128:256].astype(jnp.bfloat16)
        span = pl.ds(pl.multiple_of(skew, 32), rows_w)
        swaps[slot] = send(
            mate_out.at[slot, span], mate_in.at[slot, span], mate_send.at[slot], mate_recv.at[slot], mate
        )

    edge_at, other_at = planes(edge, middle)
    spans = ((edge_at, edge), (edge, middle))

    def base(offset, start, size):
        slot = slot_of[offset % dp_size]
        if ("swap", slot) not in state:
            state["swap", slot] = True
            swaps[slot].wait_recv()
        span = pl.ds(pl.multiple_of(skew_of(offset) + start, 16), size)
        return grads[slot, span, :] + mate_in[slot, span, :].astype(jnp.float32)

    rings, folds = {}, {}
    ring_last = ((reach - 1, reach), (reach, reach - 1))
    ring_out, ring_in = (edge_out, middle_out), (edge_in, middle_in)

    def fold_over(index, cut):
        at = (index, cut)
        fold_out[at] = base(index, *piece_of(other_at, edge, cuts, cut)).astype(jnp.bfloat16)
        folds[at] = send(fold_out.at[at], fold_in.at[at], fold_send.at[at], fold_recv.at[at], across)

    def gathered_sum(offset, kind, cut):
        value = base(offset, *piece_of(*spans[kind], cuts, cut))
        if kind == EDGE:
            at = (offset % dp_size, cut)
            folds[at].wait_recv()
            value = value + fold_in[at].astype(jnp.float32)
        return value

    def gradient(way, kind, step, cut):
        value = gathered_sum(SIGN[way] * step, kind, cut)
        if step < ring_last[way][kind]:
            rings[way, kind, step + 1, cut].wait_recv()
            value = value + ring_in[kind][way, step, cut].astype(jnp.float32)
        at, sem = (way, step - 1, cut), (way, kind, step - 1, cut)
        ring_out[kind][at] = value.astype(jnp.bfloat16)
        rings[way, kind, step, cut] = send(
            ring_out[kind].at[at], ring_in[kind].at[at], ring_send.at[sem], ring_recv.at[sem], onward[way]
        )

    lasts, shares = {}, []
    last_of = (last_edge, last_middle)

    def share(third, start, size, cut, value):
        start, size = piece_of(start, size, cuts, cut)
        span = pl.ds(pl.multiple_of(start, 16), size)
        share_out[span, :] = value
        at = (third, cut)
        shares.append(send(share_out.at[span], share_in.at[span], share_send.at[at], share_recv.at[at], mate))

    def summed(kind, cut):
        value = gathered_sum(0, kind, cut)
        for way in (UP, DOWN):
            rings[way, kind, 1, cut].wait_recv()
            value = value + ring_in[kind][way, 0, cut].astype(jnp.float32)
        last = last_of[kind]
        last[0, cut] = value.astype(jnp.bfloat16)
        at = (kind, cut)
        lasts[at] = send(last.at[0, cut], last.at[1, cut], last_send.at[at], last_recv.at[at], across)
        if kind == EDGE:
            share(0, edge_at, edge, cut, last[0, cut].astype(jnp.float32))

    def shared(kind, cut):
        lasts[kind, cut].wait_recv()
        value = last_of[kind][1, cut].astype(jnp.float32)
        if kind == EDGE:
            share(1, other_at, edge, cut, value)
        else:
            share(2, edge, middle, cut, last_of[kind][0, cut].astype(jnp.float32) + value)

    def cotangent_views():
        halo_once(1)
        wide[...] = jnp.zeros_like(wide)
        inner = jnp.where(tm < tm_size - 1, 1.0, 0.0).astype(jnp.float32)
        for frame in range(frames_out + 1):
            if frame < frames_out:
                piece = cot_ref[frame * area : (frame + 1) * area, :].astype(jnp.float32)
            else:
                piece = next_cot[...].astype(jnp.float32) * inner
            wide[frame, 0:half_rows, 0:half_cols, :] = piece.reshape(half_rows, half_cols, channels)
        for dt in range(2):
            for dr in range(2):
                for dc in range(2):
                    piece = wide[dt : dt + frames_out, dr : dr + half_rows, dc : dc + half_cols, :]
                    views[4 * dt + 2 * dr + dc] = piece.reshape(count, channels).astype(jnp.bfloat16)

    def weights():
        for copy in mates:
            copy.wait_recv()

    def weight_rows(start, size):
        return jnp.concatenate([full_weight[half, start : start + size, :] for half in range(2)], axis=1)

    times = (((2, 0), (0, 1)), ((1, 1),))
    spaces = (((1, 0),), ((2, 0), (0, 1)))

    def hidden_part(part):
        part_t, part_r, part_c = part // 4, part // 2 % 2, part % 2
        total = jnp.zeros((count, channels), jnp.float32)
        for step_t, dt in times[part_t]:
            for step_r, dr in spaces[part_r]:
                for step_c, dc in spaces[part_c]:
                    tap = 9 * step_t + 3 * step_r + step_c
                    total += lax.dot_general(
                        views[4 * dt + 2 * dr + dc],
                        weight_rows(tap * channels, channels),
                        (((1,), (1,)), ((), ())),
                        preferred_element_type=jnp.float32,
                    )
        total = total.reshape(frames_out, half_rows, half_cols, channels)
        for frame in range(frames_out):
            for lane in range(lanes):
                spread[
                    lane, 2 * frame + part_t, :, part_r, pl.ds(part_c, half_cols, 2), :
                ] = total[frame, :, :, lane * 128 : (lane + 1) * 128]

    quarter = frames * half_rows // 4

    def back(part):
        mean, inv_std = state["norm"]

        def back_rows(index, sums):
            frame, row = index // half_rows, index % half_rows
            normed = (clip_ref[frame, row].astype(jnp.float32) - mean) * inv_std
            preact = normed * gain + bias
            sig = 1.0 / (1.0 + jnp.exp(-preact))
            slope = sig * (1.0 + preact * (1.0 - sig))
            hidden_grad = jnp.concatenate([spread[lane, frame, row] for lane in range(lanes)], axis=-1)
            value = hidden_grad * frame_mask(frame) * slope * gain
            for lane in range(lanes):
                spread[lane, frame, row] = value[:, :, lane * 128 : (lane + 1) * 128]
            return sums[0] + fold(value), sums[1] + fold(value * normed)

        sums = state.get("sums", (zero, zero))
        state["sums"] = lax.fori_loop(
            0, quarter, lambda step, sums: back_rows(part * quarter + step, sums), sums, unroll=4
        )

    def back_exchange():
        state["finish"] = exchange(state["sums"], back_in, 1)

    deep = 9 * channels

    def output_part(step):
        total = jnp.dot(
            patches[:, step * deep : (step + 1) * deep],
            weight_rows(step * deep, deep),
            preferred_element_type=jnp.float32,
        )
        done = state.get("outs", 0)
        if done > 0:
            total += out_sum[...]
        if done == 2:
            out_ref[...] = total.astype(jnp.bfloat16)
        else:
            out_sum[...] = total
        state["outs"] = done + 1

    def back_finish():
        total = state["finish"]()
        state["back"] = total[0:1] / entries, total[1:2] / entries

    def input_part(part):
        mean, inv_std = state["norm"]
        back_first, back_second = state["back"]

        def input_rows(index, _):
            frame, row = index // half_rows, index % half_rows
            normed = (clip_ref[frame, row].astype(jnp.float32) - mean) * inv_std
            value = jnp.concatenate([spread[lane, frame, row] for lane in range(lanes)], axis=-1)
            input_grad_ref[frame, row] = (
                frame_mask(frame) * inv_std * (value - back_first - normed * back_second)
            ).astype(jnp.bfloat16)
            return 0

        lax.fori_loop(0, quarter, lambda step, _: input_rows(part * quarter + step, 0), 0, unroll=4)

    def result():
        for copy in shares:
            copy.wait_recv()
        weight_grad_ref[:, half_lane] = share_out[...]
        weight_grad_ref[:, other_lane] = share_in[...]

    steps = {
        "m": moments, "s": statistics, "p": patch, "t": taps, "g": gathered, "x": crossed, "f": fold_over,
        "r": gradient, "u": summed, "h": shared, "v": cotangent_views, "w": weights, "d": hidden_part,
        "b": back, "e": back_exchange, "o": output_part, "z": back_finish, "i": input_part, "y": result,
    }
    for name, *where in order:
        steps[name](*where)
    for copy in pending:
        copy.wait_send()


def ring_shards(dp_size, tm_size, clips, frame_counts, weight, gain, bias, cotangent):
    clip_data, cot_block = clips[0], cotangent[0]
    frame_count, row_count, col_count, channels = clip_data.shape
    frames_out, rows_out, cols_out = cot_block.shape[:3]
    area = rows_out * cols_out
    count = frames_out * area
    split = (frame_count, row_count // 2, 2, col_count, channels)
    rows_w = weight.shape[0]
    rows = dp_size * rows_w
    lanes = channels // 128
    gather_edge, gather_cuts, edge, cuts, _ = PLAN
    middle = rows_w - 2 * edge
    reach = dp_size // 2
    window = (rows_w + 96 + 127) // 128 * 128
    dma = pltpu.SemaphoreType.DMA
    f32, bf16 = jnp.float32, jnp.bfloat16
    pairs = [
        (2, 2, reach, gather_cuts), (2, reach, gather_cuts), (2, 3, reach), (dp_size,), (dp_size, cuts),
        (2, 2, reach, cuts), (2, cuts), (3, cuts),
    ]
    output, input_grad, weight_grad = pl.pallas_call(
        functools.partial(ring_kernel, dp_size, tm_size, PLAN, channels // GROUPS),
        out_shape=(
            pltpu.VMEM((count, channels), bf16),
            pltpu.VMEM(split, bf16),
            pltpu.VMEM((rows_w, channels), f32),
        ),
        in_specs=[SMEM] + [VMEM] * 2 + [HBM] * 3,
        out_specs=(VMEM, VMEM, VMEM),
        scratch_shapes=[
            pltpu.VMEM(split, bf16),
            pltpu.VMEM((count, channels), bf16),
            pltpu.VMEM((count, channels), f32),
            pltpu.VMEM((2,) + split[1:], bf16),
            pltpu.VMEM((area, channels), bf16),
            pltpu.VMEM((2, rows, 128), bf16),
            pltpu.VMEM((count, rows + 128), bf16),
            pltpu.VMEM((count, channels), bf16),
            pltpu.VMEM((dp_size, window, 128), f32),
            pltpu.VMEM((dp_size, window, 128), bf16),
            pltpu.VMEM((dp_size, window, 128), bf16),
            pltpu.VMEM((dp_size, cuts, edge // cuts, 128), bf16),
            pltpu.VMEM((dp_size, cuts, edge // cuts, 128), bf16),
            pltpu.VMEM((2, reach, cuts, edge // cuts, 128), bf16),
            pltpu.VMEM((2, reach, cuts, edge // cuts, 128), bf16),
            pltpu.VMEM((2, reach, cuts, middle // cuts, 128), bf16),
            pltpu.VMEM((2, reach, cuts, middle // cuts, 128), bf16),
            pltpu.VMEM((2, cuts, edge // cuts, 128), bf16),
            pltpu.VMEM((2, cuts, middle // cuts, 128), bf16),
            pltpu.VMEM((rows_w, 128), f32),
            pltpu.VMEM((rows_w, 128), f32),
            pltpu.VMEM((lanes, rows_out + 1, 2, col_count + 8, 128), f32),
            pltpu.VMEM((frames_out + 1, rows_out + 1, 16, channels), f32),
            pltpu.VMEM((8, count, channels), bf16),
            pltpu.VMEM((lanes,) + split[:-1] + (128,), f32),
            pltpu.VMEM((tm_size, 8, channels), f32),
            pltpu.VMEM((tm_size, 8, channels), f32),
        ]
        + [dma((2,))] * 2
        + [dma((2, tm_size))] * 2
        + [dma((2,)), dma((frame_count + 1,))]
        + [dma(shape) for shape in pairs for _ in range(2)],
        compiler_params=pltpu.CompilerParams(
            collective_id=0, has_side_effects=True, vmem_limit_bytes=RING_VMEM
        ),
    )(frame_counts, gain[None], bias[None], clip_data.reshape(split), cot_block.reshape(count, channels), weight)
    output, input_grad, weight_grad = settled(output, input_grad, weight_grad)
    return (
        output.reshape(cot_block.shape)[None],
        input_grad.reshape(clip_data.shape)[None],
        weight_grad,
    )


def copy_kernel(*refs):
    count = len(refs) // 2
    sems = refs[-1]
    copies = []
    for index in range(count):
        size = refs[index].shape[0] // COPY_PARTS
        for part in range(COPY_PARTS):
            span = pl.ds(part * size, size)
            copies.append(
                pltpu.make_async_copy(refs[index].at[span], refs[count + index].at[span], sems.at[len(copies)])
            )
            copies[-1].start()
    for copy in copies:
        copy.wait()


def settled(*arrays):
    sems = pltpu.SemaphoreType.DMA((COPY_PARTS * len(arrays),))
    return pl.pallas_call(
        copy_kernel,
        out_shape=tuple(jax.ShapeDtypeStruct(array.shape, array.dtype) for array in arrays),
        in_specs=[VMEM] * len(arrays),
        out_specs=(HBM,) * len(arrays),
        scratch_shapes=[sems],
        compiler_params=pltpu.CompilerParams(vmem_limit_bytes=COPY_VMEM),
    )(*arrays)


def by_ring(dp_size, tm_size, weight_rows):
    return dp_size == 8 and tm_size == 4 and weight_rows == 864


def device_part(dp_size, tm_size, *arrays):
    chosen = ring_shards if by_ring(dp_size, tm_size, arrays[2].shape[0]) else shards
    return chosen(dp_size, tm_size, *arrays)


def solution(mesh):
    placed = (
        P("dp", "tm", None, None, None),
        P("dp"),
        P("dp", None),
        P(),
        P(),
        P("dp", "tm", None, None, None),
    )
    return jax.shard_map(
        functools.partial(device_part, mesh.shape["dp"], mesh.shape["tm"]),
        mesh=mesh,
        in_specs=placed,
        out_specs=(P("dp", "tm", None, None, None), P("dp", "tm", None, None, None), P("dp", None)),
        check_vma=False,
    )
```
